128 devices in a mesh: row: 16 (over y, z), col: 8 (over x, core).
Axes of the slice: x: 4, y: 4, z: 4, core: 2. Of those that a mesh axis runs over, the one named last changes fastest.
Arguments:
- pair_list: int32 [512, 2], P(('row', 'col')), may hold values from 0 to 127, as said below
- jacobian: float32 [512, 1024, 256], P(('row', 'col'))
- damping: float32 [16384], P('row'), may hold values from 0.5 to 2
Outputs:
- factor: float32 [16384, 1024], P('row')
- trailing: float32 [16384, 16384], P('row', 'col')
The draws below stay inside these ranges and needn't reach their ends.
Inputs may be any that keep to these rules, and one draw needn't show every extreme that they name: `pair_list`: for pair p with entries (a, b): 0 <= b < a, and a lies in block row p // 32 of 8 subapertures, that is a * 16 // 128 equals it. A pair may appear more than once.
All inputs are finite; a program needn't handle non-finite values.
Results may differ from the reference program's by a relative error of at most 0.0001.
Values sent between devices are 32-bit elements; how exact they have to be, the bound alone decides.
No kernel may reach another device: no remote copies, remote signals or barrier semaphores. Data moves between devices by JAX's collectives and lax.ppermute only.
A program may use at most 128 MiB of HBM per device.

```python
import math
import jax
import jax.numpy as jnp
from jax import lax

SUBS = 128
TERMS = 128
PANEL = 512
PANELS = 2
JROWS = 1024
PAIR_DEV = 4
PAIRS = 512
SEP = 16384
N_ROW = 16
N_COL = 8


def draw_pair_list(key, part):
    key_first, key_second = jax.random.split(jax.random.fold_in(key, 11))
    pair_ids = jnp.arange(PAIRS)
    per_row = PAIR_DEV * N_COL
    block_row = pair_ids // per_row
    sub_rows = SUBS // N_ROW
    panel_subs = PANELS * PANEL // TERMS
    chosen = block_row * sub_rows + jax.random.randint(key_first, (PAIRS,), 0, sub_rows)
    chosen = jnp.maximum(chosen, 1)
    leading = pair_ids % PAIR_DEV == 0
    first_ids = jnp.where(leading, (block_row + 1) * sub_rows - 1, chosen)
    raw_draw = jax.random.randint(key_second, (PAIRS,), 0, 1 << 20)
    lead_second = pair_ids // PAIR_DEV % jnp.minimum(first_ids, panel_subs)
    second_ids = jnp.where(leading, lead_second, raw_draw % first_ids)
    return jnp.stack([first_ids, second_ids], axis=1).astype(jnp.int32)


def draw_jacobian(key, part):
    key_left, key_right = jax.random.split(jax.random.fold_in(key, 23), 2)
    half_shape = (PAIRS, JROWS, TERMS)
    left_draw = jax.random.normal(key_left, half_shape, jnp.float32)
    right_draw = jax.random.normal(key_right, half_shape, jnp.float32)
    row_scale = jnp.ones((PAIRS, JROWS, 1), jnp.float32)
    scale_rows = row_scale / math.sqrt(JROWS)
    own_part = left_draw * scale_rows
    partner_part = (-0.8 * left_draw + 0.6 * right_draw) * scale_rows
    return jnp.concatenate([own_part, partner_part], axis=2)


def block_levels(stream_key, extent, pieces, low, largest):
    def one(position, blocks):
        draws = jax.random.uniform(jax.random.fold_in(jax.random.fold_in(stream_key, 6), position), (blocks,), jnp.float32, low / len(pieces), largest / len(pieces))
        return jnp.repeat(jnp.exp(draws), extent[position] // blocks).reshape((-1,) + (1,) * (len(extent) - position - 1))

    factor_of = one(*pieces[0])
    for cut in pieces[1:]:
        factor_of = factor_of * one(*cut)
    return factor_of


def setup_inputs(seed: int = 0) -> dict:
    keys = jax.random.split(jax.random.key(seed), 4)
    pair_list = draw_pair_list(jax.random.fold_in(keys[3], 71), 0)
    jacobian = draw_jacobian(jax.random.fold_in(keys[3], 71), 0)
    damping = jnp.clip(jnp.exp(math.log(2.0) - 1.3862944 * jax.random.uniform(keys[2], (SEP,), jnp.float32) ** block_levels(keys[2], (SEP,), ((0, 16),), -0.2, 0.2)), 0.5, 2.0)
    return {"pair_list": pair_list, "jacobian": jacobian, "damping": damping}


def reference(pair_list, jacobian, damping):
    first_ids = pair_list[:, 0]
    second_ids = pair_list[:, 1]
    gram_blocks = jnp.einsum('pra,prb->pab', jacobian, jacobian, precision=lax.Precision.HIGHEST)
    dense_tiles = jnp.zeros((SUBS, TERMS, SUBS, TERMS), jnp.float32)
    dense_tiles = dense_tiles.at[first_ids, :, first_ids, :].add(gram_blocks[:, :TERMS, :TERMS])
    dense_tiles = dense_tiles.at[first_ids, :, second_ids, :].add(gram_blocks[:, :TERMS, TERMS:])
    dense_tiles = dense_tiles.at[second_ids, :, second_ids, :].add(gram_blocks[:, TERMS:, TERMS:])
    order = SUBS * TERMS
    matrix = dense_tiles.reshape(order, order)
    diagonal_ids = jnp.arange(order).astype(jnp.int32)
    matrix = matrix.at[diagonal_ids, diagonal_ids].add(damping)
    positions = jnp.arange(order)
    local_tiles = jnp.arange(PANEL) // TERMS
    factors = []
    for panel_index in range(PANELS):
        begin_col = panel_index * PANEL
        end_col = begin_col + PANEL
        pivot_tile = matrix[begin_col:end_col, begin_col:end_col]
        symmetric = jnp.where(local_tiles[:, None] >= local_tiles[None, :], pivot_tile, pivot_tile.T)
        lower_factor = jnp.linalg.cholesky(symmetric)
        column = matrix[:, begin_col:end_col]
        solved = jax.scipy.linalg.solve_triangular(lower_factor, column.T, lower=True).T
        placed = jnp.zeros_like(column).at[begin_col:end_col].set(lower_factor)
        panel_local = jnp.where((positions >= end_col)[:, None], solved, placed)
        matrix = matrix - jnp.dot(panel_local, panel_local.T, precision=lax.Precision.HIGHEST)
        factors.append(panel_local)
    factor = jnp.concatenate(factors, axis=1)
    tile_ids = positions // TERMS
    limit = PANELS * PANEL
    keep_mask = (tile_ids[:, None] >= tile_ids[None, :]) & (positions >= limit)[:, None] & (positions >= limit)[None, :]
    trailing = jnp.where(keep_mask, matrix, 0.0)
    return (factor, trailing)
```

```python
import jax
import jax.numpy as jnp
from jax import lax
from jax.experimental import pallas as pl
from jax.experimental.pallas import tpu as pltpu
from jax.sharding import PartitionSpec as P

F32 = jnp.float32
BF16 = jnp.bfloat16
HI = lax.Precision.HIGHEST
BOTH = ("row", "col")
NROW, NCOL = 16, 8
NDEV = NROW * NCOL
TILE = 128
LEAD = 8
SLOTS1 = 16
SLOTS2 = 48
DAMP_SLOT = 36
DIAG_SLOT = 40
VMEM = pltpu.VMEM
SMEM = pltpu.SMEM


def nt(a, b, precision=None):
    return lax.dot_general(
        a, b, (((1,), (1,)), ((), ())), precision=precision, preferred_element_type=F32
    )


def tn(a, b, precision=None):
    return lax.dot_general(
        a, b, (((0,), (0,)), ((), ())), precision=precision, preferred_element_type=F32
    )


def split(x):
    high = x.astype(BF16)
    return high, (x - high.astype(F32)).astype(BF16)


def nt3(ah, al, bh, bl):
    return nt(ah, bh) + (nt(ah, bl) + nt(al, bh))


def first_tile(b):
    return b * LEAD - (b * (b - 1)) // 2


def gram_kernel(jac_ref, idx_ref, damp_ref, pay_ref, cross_ref):
    q = pl.program_id(0)
    high, low = split(jac_ref[0])
    mixed = tn(high, low)
    gram = tn(high, high) + (mixed + mixed.T)
    pay_ref[pl.ds(q, TILE, stride=SLOTS1), :] = gram[:TILE, :TILE]
    pay_ref[pl.ds(q + 4, TILE, stride=SLOTS1), :] = gram[TILE:, TILE:]
    pay_ref[pl.ds(q + 8, TILE, stride=SLOTS1), :] = gram[:TILE, TILE:]
    cross_ref[0] = gram[:TILE, TILE:]

    @pl.when(q == 0)
    def _():
        pay_ref[pl.ds(12, TILE, stride=SLOTS1), :] = jnp.broadcast_to(idx_ref[...], (TILE, TILE))
        wide = jnp.concatenate([damp_ref[...], jnp.zeros((TILE - 8, TILE), F32)], axis=0)
        pay_ref[pl.ds(13, TILE, stride=SLOTS1), :] = wide.T
        zero = jnp.zeros((TILE, TILE), F32)
        pay_ref[pl.ds(14, TILE, stride=SLOTS1), :] = zero
        pay_ref[pl.ds(15, TILE, stride=SLOTS1), :] = zero


def grams(jacobian, idx, damp):
    return pl.pallas_call(
        gram_kernel,
        grid=(4,),
        in_specs=[
            pl.BlockSpec((1, 1024, 256), lambda q: (q, 0, 0)),
            pl.BlockSpec((1, TILE), lambda q: (0, 0)),
            pl.BlockSpec((8, TILE), lambda q: (0, 0)),
        ],
        out_specs=[
            pl.BlockSpec((TILE * SLOTS1, TILE), lambda q: (0, 0)),
            pl.BlockSpec((1, TILE, TILE), lambda q: (q, 0, 0)),
        ],
        out_shape=[
            jax.ShapeDtypeStruct((TILE * SLOTS1, TILE), F32),
            jax.ShapeDtypeStruct((4, TILE, TILE), F32),
        ],
        name="grams",
    )(jacobian, idx, damp)


def gather_kernel(recv_ref, pay_ref, idx_ref):
    lane = lax.broadcasted_iota(jnp.int32, (TILE, TILE), 1)
    sub = lax.broadcasted_iota(jnp.int32, (TILE, TILE), 0)
    index = recv_ref[pl.ds(12, NDEV, stride=SLOTS1), :].astype(jnp.int32)
    idx_ref[...] = index
    across = recv_ref[pl.ds(12, NDEV, stride=SLOTS1), :].T.astype(jnp.int32)
    diag = jnp.zeros((TILE, TILE), F32)
    lead = jnp.zeros((40, TILE), F32)
    sub40 = lax.broadcasted_iota(jnp.int32, (40, TILE), 0)
    lane40 = lax.broadcasted_iota(jnp.int32, (40, TILE), 1)
    for q in range(4):
        a = across[2 * q : 2 * q + 1, :]
        b = across[2 * q + 1 : 2 * q + 2, :]
        first = recv_ref[pl.ds(q, NDEV, stride=SLOTS1), :]
        second = recv_ref[pl.ds(q + 4, NDEV, stride=SLOTS1), :]
        cross = recv_ref[pl.ds(q + 8, NDEV, stride=SLOTS1), :]
        diag = diag + jnp.dot((sub == a).astype(F32), first, precision=HI)
        diag = diag + jnp.dot((sub == b).astype(F32), second, precision=HI)
        place = first_tile(b) + (a - b)
        hit = (sub40 == place) & (lane40 < NCOL)
        lead = lead + jnp.dot(hit.astype(F32), cross, precision=HI)
    hit = (sub40 == first_tile(lane40)) & (lane40 < LEAD)
    lead = lead + jnp.dot(hit.astype(F32), diag, precision=HI)
    damp = jnp.broadcast_to(recv_ref[13:14, :], (40, TILE))
    lead = jnp.where(sub40 == DAMP_SLOT, damp, lead)
    for r in range(NROW):
        for c in range(NCOL):
            base = (r * NCOL + c) * SLOTS2
            pay_ref[base : base + 40, :] = lead
            pay_ref[base + 40 : base + 48, :] = diag[8 * r : 8 * r + 8, :]


def gather_rows(recv):
    return pl.pallas_call(
        gather_kernel,
        out_shape=[
            jax.ShapeDtypeStruct((NDEV * SLOTS2, TILE), F32),
            jax.ShapeDtypeStruct((NDEV, TILE), jnp.int32),
        ],
        name="gather_rows",
    )(recv)


def factor128(rows):
    lane = lax.broadcasted_iota(jnp.int32, (8, TILE), 1)
    sub = lax.broadcasted_iota(jnp.int32, (8, TILE), 0)
    block = list(rows)
    inv = [jnp.where(lane == sub + 8 * v, 1.0, 0.0) for v in range(16)]
    upper, inverse = [], []

    def row(x, i):
        return jnp.broadcast_to(x[i : i + 1, :], (8, TILE))

    def col(x, i):
        return jnp.broadcast_to(x[:, i : i + 1], (8, TILE))

    for t in range(16):
        cols = [col(block[t], 8 * t + k) for k in range(8)]
        left, right = block[t], inv[t]
        up = jnp.zeros((8, TILE), F32)
        low, recip = up, up
        for j in range(8):
            pivot = row(cols[j], j)
            root = lax.rsqrt(pivot)
            over = 1.0 / pivot
            hit = sub == j
            scale = jnp.where(hit, 0.0, cols[j] * over)
            left_row, right_row = row(left, j), row(right, j)
            up = jnp.where(hit, left_row * root, up)
            low = jnp.where(hit, right_row * root, low)
            recip = jnp.where(hit, over, recip)
            for k in range(j + 1, 8):
                cols[k] = cols[k] - scale * row(cols[k], j)
            left = left - scale * left_row
            right = right - scale * right_row
        upper.append(jnp.where(lane >= sub + 8 * t, up, 0.0))
        inverse.append(low)
        if t < 15:
            left, right = left * recip, right * recip
            lefts = [row(left, j) for j in range(8)]
            rights = [row(right, j) for j in range(8)]
            for v in range(t + 1, 16):
                parts = [col(block[v], 8 * t + k) for k in range(8)]
                one = [parts[k] * lefts[k] for k in range(8)]
                two = [parts[k] * rights[k] for k in range(8)]
                while len(one) > 1:
                    one = [one[i] + one[i + 1] for i in range(0, len(one), 2)]
                    two = [two[i] + two[i + 1] for i in range(0, len(two), 2)]
                block[v] = block[v] - one[0]
                inv[v] = inv[v] - two[0]
    return upper, inverse


def at(i, n=TILE):
    return pl.ds(pl.multiple_of(i * n, n), n)


def factor_kernel(scal_ref, recv_ref, cross_ref, x_ref, l_ref, inv_ref, body):
    place = 0
    for k in range(LEAD):
        for i in range(k):
            body[TILE * i : TILE * (i + 1), TILE * k : TILE * (k + 1)] = jnp.zeros((TILE, TILE), F32)
        for i in range(k, LEAD):
            tile = recv_ref[pl.ds(place, TILE, stride=SLOTS2), :]
            if i == k:
                damp = recv_ref[pl.ds(DAMP_SLOT, TILE, stride=SLOTS2), :]
                lane = lax.broadcasted_iota(jnp.int32, (TILE, TILE), 1)
                sub = lax.broadcasted_iota(jnp.int32, (TILE, TILE), 0)
                tile = tile + jnp.where(lane == sub, damp[:, k : k + 1], 0.0)
            body[TILE * i : TILE * (i + 1), TILE * k : TILE * (k + 1)] = tile
            place += 1

    def clear(i, _):
        body[pl.ds(pl.multiple_of(1024 + 32 * i, 32), 32), :] = jnp.zeros((32, 1024), F32)
        return 0

    lax.fori_loop(0, 32, clear, 0)
    row = scal_ref[192]

    def fill(p, _):
        a = scal_ref[2 * p] - LEAD * row
        b = scal_ref[2 * p + 1]

        @pl.when(b < LEAD)
        def _():
            body[at(LEAD + a), at(b)] += cross_ref[at(p), :]

        return 0

    lax.fori_loop(0, 32, fill, 0)

    def step(k, _):
        rows = [
            body[pl.ds(pl.multiple_of(k * TILE + 8 * v, 8), 8), at(k)] for v in range(16)
        ]
        upper, inverse = factor128(rows)
        inv = jnp.concatenate(inverse, axis=0)
        inv_ref[at(k), :] = inv
        lower = jnp.concatenate(upper, axis=0).T

        def panel(i, _):
            x = nt(body[at(i, 256), at(k)], inv, HI)
            index = i * 256 + lax.broadcasted_iota(jnp.int32, (256, TILE), 0)
            body[at(i, 256), at(k)] = jnp.where(index >= (k + 1) * TILE, x, 0.0)
            return 0

        lax.fori_loop(0, 8, panel, 0)

        def update(j, _):
            right = body[at(j), at(k)]

            def rows_of(i, _):
                body[at(i, 512), at(j)] -= nt(body[at(i, 512), at(k)], right, HI)
                return 0

            lax.fori_loop(0, 4, rows_of, 0)
            return 0

        lax.fori_loop(k + 1, LEAD, update, 0)
        body[at(k), at(k)] = lower
        return 0

    lax.fori_loop(0, LEAD, step, 0)

    def out(i, _):
        part = pl.ds(pl.multiple_of(32 * i, 32), 32)
        below = pl.ds(pl.multiple_of(1024 + 32 * i, 32), 32)
        l_ref[part, :] = body[part, :]
        x_ref[part, :] = jnp.where(row == 0, body[part, :], body[below, :])
        return 0

    lax.fori_loop(0, 32, out, 0)


def factorise(scal, recv, cross):
    return pl.pallas_call(
        factor_kernel,
        in_specs=[
            pl.BlockSpec(memory_space=SMEM),
            pl.BlockSpec(memory_space=VMEM),
            pl.BlockSpec(memory_space=VMEM),
        ],
        out_specs=[pl.BlockSpec(memory_space=VMEM)] * 3,
        out_shape=[
            jax.ShapeDtypeStruct((1024, 1024), F32),
            jax.ShapeDtypeStruct((1024, 1024), F32),
            jax.ShapeDtypeStruct((1024, TILE), F32),
        ],
        scratch_shapes=[VMEM((2048, 1024), F32)],
        compiler_params=pltpu.CompilerParams(vmem_limit_bytes=48 * 1024 * 1024),
        cost_estimate=pl.CostEstimate(
            flops=60_000_000_000, bytes_accessed=20_000_000, transcendentals=0
        ),
        name="factorise",
    )(scal, recv, cross)


def schur_kernel(
    scal_ref, x_ref, l_ref, inv_ref, col_ref, cross_ref, diag_ref, damp_ref, out_ref,
    colx, lh, ll, xh, xl, ch, cl,
):
    step = pl.program_id(0)
    row = scal_ref[192]
    column = scal_ref[193]

    @pl.when(step == 0)
    def _():
        def clear(i, _):
            colx[at(i, 32), :] = jnp.zeros((32, 1024), F32)
            return 0

        lax.fori_loop(0, 64, clear, 0)

        def fill(p, _):
            a = scal_ref[64 + 2 * p] - 16 * column
            b = scal_ref[64 + 2 * p + 1]

            @pl.when(b < LEAD)
            def _():
                colx[at(a), at(b)] += col_ref[at(p), :]

            return 0

        lax.fori_loop(0, 64, fill, 0)

        def parts(i, _):
            lh[at(i), :], ll[at(i), :] = split(l_ref[at(i), :])
            xh[at(i), :], xl[at(i), :] = split(x_ref[at(i), :])
            return 0

        lax.fori_loop(0, 8, parts, 0)
        for k in range(LEAD):
            here = slice(TILE * k, TILE * (k + 1))
            wh, wl = split(inv_ref[here, :])

            def solve(i, _):
                rest = colx[at(i, 512), here]
                if k:
                    rest = rest - nt3(
                        ch[at(i, 512), : TILE * k],
                        cl[at(i, 512), : TILE * k],
                        lh[here, : TILE * k],
                        ll[here, : TILE * k],
                    )
                rh, rl = split(rest)
                ch[at(i, 512), here], cl[at(i, 512), here] = split(nt3(rh, rl, wh, wl))
                return 0

            lax.fori_loop(0, 4, solve, 0)

    first = 16 * column + 2 * step
    live = (row >= 1) & (first + 1 >= LEAD) & (first <= LEAD * row + 7)

    @pl.when(jnp.logical_not(live))
    def _():
        out_ref[...] = jnp.zeros_like(out_ref)

    @pl.when(live)
    def _():
        def part(i, _):
            prod = nt3(
                xh[at(i, 256), :], xl[at(i, 256), :], ch[at(step, 256), :], cl[at(step, 256), :]
            )
            tile_row = LEAD * row + 2 * i + lax.broadcasted_iota(jnp.int32, (256, 256), 0) // TILE
            tile_col = first + lax.broadcasted_iota(jnp.int32, (256, 256), 1) // TILE
            keep = (tile_row >= tile_col) & (tile_col >= LEAD)
            out_ref[at(i, 256), :] = jnp.where(keep, -prod, 0.0)
            return 0

        lax.fori_loop(0, 4, part, 0)

        def fill(p, _):
            a = scal_ref[2 * p] - LEAD * row
            b = scal_ref[2 * p + 1]

            @pl.when((b >= LEAD) & (b >= first) & (b < first + 2))
            def _():
                out_ref[at(a), at(b - first)] += cross_ref[at(p), :]

            return 0

        lax.fori_loop(0, 32, fill, 0)
        for s in range(LEAD):
            b = LEAD * row + s

            @pl.when((b >= first) & (b < first + 2))
            def _(s=s, b=b):
                lane = lax.broadcasted_iota(jnp.int32, (TILE, TILE), 1)
                sub = lax.broadcasted_iota(jnp.int32, (TILE, TILE), 0)
                damp = jnp.broadcast_to(damp_ref[s : s + 1, :], (TILE, TILE))
                tile = diag_ref[pl.ds(DIAG_SLOT + s, TILE, stride=SLOTS2), :]
                out_ref[TILE * s : TILE * (s + 1), at(b - first)] += tile + jnp.where(
                    lane == sub, damp, 0.0
                )


def schur(scal, x, lower, inv, col_cross, cross, recv, damp):
    whole = pl.BlockSpec(memory_space=VMEM)
    return pl.pallas_call(
        schur_kernel,
        grid=(8,),
        in_specs=[pl.BlockSpec(memory_space=SMEM)] + [whole] * 7,
        out_specs=pl.BlockSpec((1024, 256), lambda s: (0, s)),
        out_shape=jax.ShapeDtypeStruct((1024, 2048), F32),
        scratch_shapes=[
            VMEM((2048, 1024), F32),
            VMEM((1024, 1024), BF16),
            VMEM((1024, 1024), BF16),
            VMEM((1024, 1024), BF16),
            VMEM((1024, 1024), BF16),
            VMEM((2048, 1024), BF16),
            VMEM((2048, 1024), BF16),
        ],
        compiler_params=pltpu.CompilerParams(vmem_limit_bytes=60 * 1024 * 1024),
        cost_estimate=pl.CostEstimate(
            flops=20_000_000_000, bytes_accessed=30_000_000, transcendentals=0
        ),
        name="schur",
    )(scal, x, lower, inv, col_cross, cross, recv, damp)


def spread(x, axis, size):
    wide = jnp.broadcast_to(x[None], (size,) + x.shape)
    return lax.all_to_all(wide, axis, 0, 0, tiled=True)


def local(pair_list, jacobian, damping):
    row = lax.axis_index("row")
    column = lax.axis_index("col")
    idx = jnp.zeros((1, TILE), F32).at[0, :8].set(pair_list.reshape(8).astype(F32))
    damp = damping.reshape(8, TILE)
    payload, cross = grams(jacobian, idx, damp)
    recv = lax.all_to_all(payload.reshape(NDEV, SLOTS1, TILE), BOTH, 0, 0, tiled=True)
    payload, index = gather_rows(recv.reshape(NDEV * SLOTS1, TILE))
    recv = lax.all_to_all(payload.reshape(NDEV, SLOTS2, TILE), BOTH, 0, 0, tiled=True)
    recv = recv.reshape(NDEV * SLOTS2, TILE)

    row_cross = spread(cross.reshape(512, TILE), "col", NCOL).reshape(32 * TILE, TILE)
    moves = [
        (r * NCOL + c, (NCOL * (r % 2) + c) * NCOL + r // 2) for r in range(NROW) for c in range(NCOL)
    ]
    moved = lax.ppermute(cross.reshape(512, TILE), BOTH, moves)
    col_cross = spread(moved, "row", NROW).reshape(64 * TILE, TILE)

    index = index[:, :8].reshape(NDEV * 8)
    scal = jnp.concatenate(
        [
            lax.dynamic_slice(index, (row * 64,), (64,)),
            lax.dynamic_slice(index, (column * 128,), (128,)),
            jnp.stack([row, column]).astype(jnp.int32),
        ]
    )
    factor, lower, inv = factorise(scal, recv, row_cross)
    trailing = schur(scal, factor, lower, inv, col_cross, row_cross, recv, damp)
    return factor, trailing


def solution(mesh):
    placed = (P(("row", "col"), None), P(("row", "col"), None, None), P("row"))
    return jax.shard_map(
        local,
        mesh=mesh,
        in_specs=placed,
        out_specs=(P("row", None), P("row", "col")),
        check_vma=False,
    )
```

```python
import jax
import jax.numpy as jnp
from jax import lax
from jax.experimental import pallas as pl
from jax.experimental.pallas import tpu as pltpu
from jax.sharding import PartitionSpec as P

F32 = jnp.float32
BF16 = jnp.bfloat16
HI = lax.Precision.HIGHEST
BOTH = ("row", "col")
NROW, NCOL = 16, 8
NDEV = NROW * NCOL
TILE = 128
LEAD = 8
SLOTS1 = 16
SLOTS2 = 48
DAMP_SLOT = 36
DIAG_SLOT = 40
VMEM = pltpu.VMEM
SMEM = pltpu.SMEM


def nt(a, b, precision=None):
    return lax.dot_general(
        a, b, (((1,), (1,)), ((), ())), precision=precision, preferred_element_type=F32
    )


def tn(a, b, precision=None):
    return lax.dot_general(
        a, b, (((0,), (0,)), ((), ())), precision=precision, preferred_element_type=F32
    )


def split(x):
    high = x.astype(BF16)
    return high, (x - high.astype(F32)).astype(BF16)


def nt3(ah, al, bh, bl):
    return nt(ah, bh) + (nt(ah, bl) + nt(al, bh))


def first_tile(b):
    return b * LEAD - (b * (b - 1)) // 2


def gram_kernel(jac_ref, idx_ref, damp_ref, pay_ref, cross_ref):
    q = pl.program_id(0)
    high, low = split(jac_ref[0])
    mixed = tn(high, low)
    gram = tn(high, high) + (mixed + mixed.T)
    pay_ref[pl.ds(q, TILE, stride=SLOTS1), :] = gram[:TILE, :TILE]
    pay_ref[pl.ds(q + 4, TILE, stride=SLOTS1), :] = gram[TILE:, TILE:]
    pay_ref[pl.ds(q + 8, TILE, stride=SLOTS1), :] = gram[:TILE, TILE:]
    cross_ref[0] = gram[:TILE, TILE:]

    @pl.when(q == 0)
    def _():
        lane = lax.broadcasted_iota(jnp.int32, (TILE, TILE), 1)
        index = jnp.zeros((TILE, TILE), F32)
        for e in range(8):
            index = jnp.where(lane == e, idx_ref[e].astype(F32), index)
        pay_ref[pl.ds(12, TILE, stride=SLOTS1), :] = index
        wide = jnp.concatenate([damp_ref[...], jnp.zeros((TILE - 8, TILE), F32)], axis=0)
        pay_ref[pl.ds(13, TILE, stride=SLOTS1), :] = wide.T
        zero = jnp.zeros((TILE, TILE), F32)
        pay_ref[pl.ds(14, TILE, stride=SLOTS1), :] = zero
        pay_ref[pl.ds(15, TILE, stride=SLOTS1), :] = zero


def grams(jacobian, idx, damp):
    return pl.pallas_call(
        gram_kernel,
        grid=(4,),
        in_specs=[
            pl.BlockSpec((1, 1024, 256), lambda q: (q, 0, 0)),
            pl.BlockSpec(memory_space=SMEM),
            pl.BlockSpec((8, TILE), lambda q: (0, 0)),
        ],
        out_specs=[
            pl.BlockSpec((TILE * SLOTS1, TILE), lambda q: (0, 0)),
            pl.BlockSpec((1, TILE, TILE), lambda q: (q, 0, 0)),
        ],
        out_shape=[
            jax.ShapeDtypeStruct((TILE * SLOTS1, TILE), F32),
            jax.ShapeDtypeStruct((4, TILE, TILE), F32),
        ],
        name="grams",
    )(jacobian, idx, damp)


def gather_kernel(recv_ref, pay_ref, idx_ref):
    lane = lax.broadcasted_iota(jnp.int32, (TILE, TILE), 1)
    sub = lax.broadcasted_iota(jnp.int32, (TILE, TILE), 0)
    index = recv_ref[pl.ds(12, NDEV, stride=SLOTS1), :].astype(jnp.int32)
    idx_ref[...] = index
    across = recv_ref[pl.ds(12, NDEV, stride=SLOTS1), :].T.astype(jnp.int32)
    diag = jnp.zeros((TILE, TILE), F32)
    lead = jnp.zeros((40, TILE), F32)
    sub40 = lax.broadcasted_iota(jnp.int32, (40, TILE), 0)
    lane40 = lax.broadcasted_iota(jnp.int32, (40, TILE), 1)
    for q in range(4):
        a = across[2 * q : 2 * q + 1, :]
        b = across[2 * q + 1 : 2 * q + 2, :]
        first = recv_ref[pl.ds(q, NDEV, stride=SLOTS1), :]
        second = recv_ref[pl.ds(q + 4, NDEV, stride=SLOTS1), :]
        cross = recv_ref[pl.ds(q + 8, NDEV, stride=SLOTS1), :]
        diag = diag + jnp.dot((sub == a).astype(F32), first, precision=HI)
        diag = diag + jnp.dot((sub == b).astype(F32), second, precision=HI)
        place = first_tile(b) + (a - b)
        hit = (sub40 == place) & (lane40 < NCOL)
        lead = lead + jnp.dot(hit.astype(F32), cross, precision=HI)
    hit = (sub40 == first_tile(lane40)) & (lane40 < LEAD)
    lead = lead + jnp.dot(hit.astype(F32), diag, precision=HI)
    damp = jnp.broadcast_to(recv_ref[13:14, :], (40, TILE))
    lead = jnp.where(sub40 == DAMP_SLOT, damp, lead)
    for r in range(NROW):
        for c in range(NCOL):
            base = (r * NCOL + c) * SLOTS2
            pay_ref[base : base + 40, :] = lead
            pay_ref[base + 40 : base + 48, :] = diag[8 * r : 8 * r + 8, :]


def gather_rows(recv):
    return pl.pallas_call(
        gather_kernel,
        out_shape=[
            jax.ShapeDtypeStruct((NDEV * SLOTS2, TILE), F32),
            jax.ShapeDtypeStruct((NDEV, TILE), jnp.int32),
        ],
        name="gather_rows",
    )(recv)


def factor128(rows):
    lane = lax.broadcasted_iota(jnp.int32, (8, TILE), 1)
    sub = lax.broadcasted_iota(jnp.int32, (8, TILE), 0)
    block = list(rows)
    inv = [jnp.where(lane == sub + 8 * v, 1.0, 0.0) for v in range(16)]
    upper, inverse = [], []

    def row(x, i):
        return jnp.broadcast_to(x[i : i + 1, :], (8, TILE))

    def col(x, i):
        return jnp.broadcast_to(x[:, i : i + 1], (8, TILE))

    for t in range(16):
        cols = [col(block[t], 8 * t + k) for k in range(8)]
        left, right = block[t], inv[t]
        up = jnp.zeros((8, TILE), F32)
        low, recip = up, up
        for j in range(8):
            pivot = row(cols[j], j)
            root = lax.rsqrt(pivot)
            over = 1.0 / pivot
            hit = sub == j
            scale = jnp.where(hit, 0.0, cols[j] * over)
            left_row, right_row = row(left, j), row(right, j)
            up = jnp.where(hit, left_row * root, up)
            low = jnp.where(hit, right_row * root, low)
            recip = jnp.where(hit, over, recip)
            for k in range(j + 1, 8):
                cols[k] = cols[k] - scale * row(cols[k], j)
            left = left - scale * left_row
            right = right - scale * right_row
        upper.append(jnp.where(lane >= sub + 8 * t, up, 0.0))
        inverse.append(low)
        if t < 15:
            left, right = left * recip, right * recip
            lefts = [row(left, j) for j in range(8)]
            rights = [row(right, j) for j in range(8)]
            for v in range(t + 1, 16):
                parts = [col(block[v], 8 * t + k) for k in range(8)]
                one = [parts[k] * lefts[k] for k in range(8)]
                two = [parts[k] * rights[k] for k in range(8)]
                while len(one) > 1:
                    one = [one[i] + one[i + 1] for i in range(0, len(one), 2)]
                    two = [two[i] + two[i + 1] for i in range(0, len(two), 2)]
                block[v] = block[v] - one[0]
                inv[v] = inv[v] - two[0]
    return upper, inverse


def at(i, n=TILE):
    return pl.ds(pl.multiple_of(i * n, n), n)


def three(x):
    high = x.astype(BF16)
    rest = x - high.astype(F32)
    mid = rest.astype(BF16)
    return high, mid, (rest - mid.astype(F32)).astype(BF16)


def stacks(x):
    h, m, low = three(x)
    return (
        jnp.concatenate([h, h], axis=1),
        jnp.concatenate([m, h], axis=1),
        jnp.concatenate([low, m], axis=1),
    )


def right_stacks(x):
    h, m, low = three(x)
    return jnp.concatenate([h, m], axis=1), jnp.concatenate([h, low], axis=1)


def six(pa, pb, pc, ra, rb):
    return nt(pa, ra) + (nt(pb, rb) + nt(pc, ra))


def factor_kernel(recv_ref, lh_ref, ll_ref, inv_ref, diag_ref, body, pa, pb, pc, ra, rb):
    place = 0
    lane = lax.broadcasted_iota(jnp.int32, (TILE, TILE), 1)
    sub = lax.broadcasted_iota(jnp.int32, (TILE, TILE), 0)
    damp = recv_ref[pl.ds(DAMP_SLOT, TILE, stride=SLOTS2), :]
    for k in range(LEAD):
        for i in range(k, LEAD):
            tile = recv_ref[pl.ds(place, TILE, stride=SLOTS2), :]
            if i == k:
                tile = tile + jnp.where(lane == sub, damp[:, k : k + 1], 0.0)
            body[TILE * i : TILE * (i + 1), TILE * k : TILE * (k + 1)] = tile
            place += 1
        diag_ref[TILE * k : TILE * (k + 1), :] = recv_ref[
            pl.ds(DIAG_SLOT + k, TILE, stride=SLOTS2), :
        ]

    def step(k, _):
        rows = [
            body[pl.ds(pl.multiple_of(k * TILE + 8 * v, 8), 8), at(k)] for v in range(16)
        ]
        upper, inverse = factor128(rows)
        inv = jnp.concatenate(inverse, axis=0)
        inv_ref[at(k), :] = inv
        wa, wb = right_stacks(inv)

        def panel(i, _):
            x = six(*stacks(body[at(i, 512), at(k)]), wa, wb)
            index = i * 512 + lax.broadcasted_iota(jnp.int32, (512, TILE), 0)
            x = jnp.where(index >= (k + 1) * TILE, x, 0.0)
            h, m, low = three(x)
            pa[at(i, 512), :] = jnp.concatenate([h, h], axis=1)
            pb[at(i, 512), :] = jnp.concatenate([m, h], axis=1)
            pc[at(i, 512), :] = jnp.concatenate([low, m], axis=1)
            ra[at(i, 512), :] = jnp.concatenate([h, m], axis=1)
            rb[at(i, 512), :] = jnp.concatenate([h, low], axis=1)
            lh_ref[at(i, 512), at(k)] = h
            ll_ref[at(i, 512), at(k)] = m
            return 0

        begin = (k >= 3).astype(jnp.int32)
        @pl.when(k >= 3)
        def _():
            zero = jnp.zeros((512, TILE), BF16)
            lh_ref[:512, at(k)] = zero
            ll_ref[:512, at(k)] = zero

        lax.fori_loop(begin, 2, panel, 0)

        def update(j, _):
            wa, wb = ra[at(j), :], rb[at(j), :]

            def rows_of(i, _):
                part = at(i, 512)
                body[part, at(j)] -= six(pa[part, :], pb[part, :], pc[part, :], wa, wb)
                return 0

            lax.fori_loop((j >= 4).astype(jnp.int32), 2, rows_of, 0)
            return 0

        lax.fori_loop(k + 1, LEAD, update, 0)
        lh_ref[at(k), at(k)], ll_ref[at(k), at(k)] = split(jnp.concatenate(upper, axis=0).T)
        return 0

    lax.fori_loop(0, LEAD, step, 0)


def factorise(recv):
    return pl.pallas_call(
        factor_kernel,
        in_specs=[pl.BlockSpec(memory_space=VMEM)],
        out_specs=[pl.BlockSpec(memory_space=VMEM)] * 4,
        out_shape=[
            jax.ShapeDtypeStruct((1024, 1024), BF16),
            jax.ShapeDtypeStruct((1024, 1024), BF16),
            jax.ShapeDtypeStruct((1024, TILE), F32),
            jax.ShapeDtypeStruct((1024, TILE), F32),
        ],
        scratch_shapes=[VMEM((1024, 1024), F32)] + [VMEM((1024, 256), BF16)] * 5,
        compiler_params=pltpu.CompilerParams(vmem_limit_bytes=32 * 1024 * 1024),
        cost_estimate=pl.CostEstimate(
            flops=40_000_000_000, bytes_accessed=8_000_000, transcendentals=0
        ),
        name="factorise",
    )(recv)


def schur_kernel(
    scal_ref, lh_ref, ll_ref, inv_ref, col_ref, cross_ref, diag_ref, damp_ref,
    factor_ref, out_ref, rows, ch, cl, where_ref, tiles_ref,
):
    row = scal_ref[192]
    column = scal_ref[193]
    for u in range(24):
        where_ref[u] = 0

    def mark_row(p, _):
        a = scal_ref[2 * p] - LEAD * row
        where_ref[a] = jnp.where(scal_ref[2 * p + 1] < LEAD, 1, where_ref[a])
        return 0

    def mark_col(p, _):
        tile = scal_ref[64 + 2 * p]
        a = tile - 16 * column + LEAD
        used = (scal_ref[65 + 2 * p] < LEAD) & (tile >= LEAD) & (tile <= LEAD * row + 7)
        where_ref[a] = jnp.where(used, 1, where_ref[a])
        return 0

    @pl.when(row >= 1)
    def _():
        lax.fori_loop(0, 32, mark_row, 0)
        lax.fori_loop(0, 64, mark_col, 0)

    def place(u, count):
        used = where_ref[u] == 1
        where_ref[u] = jnp.where(used, count, -1)
        tiles_ref[count] = u
        return count + used.astype(jnp.int32)

    n_row = lax.fori_loop(0, LEAD, place, jnp.int32(0))
    total = lax.fori_loop(LEAD, 24, place, n_row)

    def clear(i, _):
        rows[at(i), :] = jnp.zeros((TILE, 1024), F32)
        return 0

    lax.fori_loop(0, total, clear, 0)

    def fill_row(p, _):
        a = scal_ref[2 * p] - LEAD * row
        b = scal_ref[2 * p + 1]

        @pl.when((b < LEAD) & (where_ref[a] >= 0))
        def _():
            rows[at(where_ref[a]), at(b)] += cross_ref[at(p), :]

        return 0

    def fill_col(p, _):
        a = scal_ref[64 + 2 * p] - 16 * column + LEAD
        b = scal_ref[65 + 2 * p]

        @pl.when((b < LEAD) & (where_ref[a] >= 0))
        def _():
            rows[at(where_ref[a]), at(b)] += col_ref[at(p), :]

        return 0

    lax.fori_loop(0, 32, fill_row, 0)
    lax.fori_loop(0, 64, fill_col, 0)

    def blank(i, _):
        out_ref[at(i, 32), :] = jnp.zeros((32, 2048), F32)
        return 0

    lax.fori_loop(0, 32, blank, 0)

    def fill_out(p, _):
        a = scal_ref[2 * p] - LEAD * row
        b = scal_ref[2 * p + 1]
        here = b - 16 * column

        @pl.when((b >= LEAD) & (here >= 0) & (here < 16))
        def _():
            out_ref[at(a), at(here)] += cross_ref[at(p), :]

        return 0

    lax.fori_loop(0, 32, fill_out, 0)

    @pl.when((row >= 1) & (row // 2 == column))
    def _():
        lane = lax.broadcasted_iota(jnp.int32, (TILE, TILE), 1)
        sub = lax.broadcasted_iota(jnp.int32, (TILE, TILE), 0)
        for s in range(LEAD):
            damp = jnp.broadcast_to(damp_ref[s : s + 1, :], (TILE, TILE))
            tile = diag_ref[TILE * s : TILE * (s + 1), :] + jnp.where(lane == sub, damp, 0.0)
            out_ref[TILE * s : TILE * (s + 1), at(LEAD * (row % 2) + s)] += tile

    for k in range(LEAD):
        here = slice(TILE * k, TILE * (k + 1))
        wh, wl = split(inv_ref[here, :])

        def solve(i, _, k=k, here=here, wh=wh, wl=wl):
            rest = rows[at(i, 512), here]
            if k:
                rest = rest - nt3(
                    ch[at(i, 512), : TILE * k],
                    cl[at(i, 512), : TILE * k],
                    lh_ref[here, : TILE * k],
                    ll_ref[here, : TILE * k],
                )
            x = nt3(*split(rest), wh, wl)
            rows[at(i, 512), here] = x
            ch[at(i, 512), here], cl[at(i, 512), here] = split(x)
            return 0

        lax.fori_loop(0, (total + 3) // 4, solve, 0)

    for s in range(LEAD):
        part = slice(TILE * s, TILE * (s + 1))

        @pl.when(where_ref[s] >= 0)
        def _(s=s, part=part):
            factor_ref[part, :] = rows[at(where_ref[s]), :]

        @pl.when((where_ref[s] < 0) & (row >= 1))
        def _(part=part):
            factor_ref[part, :] = jnp.zeros((TILE, 1024), F32)

        @pl.when(row == 0)
        def _(part=part):
            factor_ref[part, :] = lh_ref[part, :].astype(F32) + ll_ref[part, :].astype(F32)

    n_col = total - n_row

    def columns(j, _):
        jt = n_row + 2 * j
        right = pl.ds(pl.multiple_of(jt * TILE, TILE), 256)

        def blocks(i, _):
            left = at(i, 256)
            prod = nt3(ch[left, :], cl[left, :], ch[right, :], cl[right, :])
            for p in range(2):
                for q in range(2):
                    it = 2 * i + p
                    a = tiles_ref[jnp.minimum(it, 23)]
                    b = tiles_ref[jnp.minimum(jt + q, 23)] - LEAD
                    keep = (it < n_row) & (jt + q < total) & (LEAD * row + a >= 16 * column + b)

                    @pl.when(keep)
                    def _(a=a, b=b, p=p, q=q):
                        out_ref[at(a), at(b)] -= prod[
                            TILE * p : TILE * (p + 1), TILE * q : TILE * (q + 1)
                        ]

            return 0

        lax.fori_loop(0, (n_row + 1) // 2, blocks, 0)
        return 0

    lax.fori_loop(0, (n_col + 1) // 2, columns, 0)


def schur(scal, lh, ll, inv, col_cross, cross, diag, damp):
    whole = pl.BlockSpec(memory_space=VMEM)
    return pl.pallas_call(
        schur_kernel,
        in_specs=[pl.BlockSpec(memory_space=SMEM)] + [whole] * 7,
        out_specs=[whole] * 2,
        out_shape=[
            jax.ShapeDtypeStruct((1024, 1024), F32),
            jax.ShapeDtypeStruct((1024, 2048), F32),
        ],
        scratch_shapes=[
            VMEM((3072, 1024), F32),
            VMEM((3328, 1024), BF16),
            VMEM((3328, 1024), BF16),
            SMEM((24,), jnp.int32),
            SMEM((25,), jnp.int32),
        ],
        compiler_params=pltpu.CompilerParams(vmem_limit_bytes=60 * 1024 * 1024),
        cost_estimate=pl.CostEstimate(
            flops=20_000_000_000, bytes_accessed=30_000_000, transcendentals=0
        ),
        name="schur",
    )(scal, lh, ll, inv, col_cross, cross, diag, damp)


def local(pair_list, jacobian, damping):
    row = lax.axis_index("row")
    column = lax.axis_index("col")
    damp = damping.reshape(8, TILE)
    payload, cross = grams(jacobian, pair_list.reshape(8), damp)
    recv = lax.all_to_all(payload.reshape(NDEV, SLOTS1, TILE), BOTH, 0, 0, tiled=True)
    payload, index = gather_rows(recv.reshape(NDEV * SLOTS1, TILE))
    recv = lax.all_to_all(payload.reshape(NDEV, SLOTS2, TILE), BOTH, 0, 0, tiled=True)
    lower_high, lower_low, inv, diag = factorise(recv.reshape(NDEV * SLOTS2, TILE))

    cross = cross.reshape(4 * TILE, TILE)
    moves = [
        (r * NCOL + c, (NCOL * (r % 2) + c) * NCOL + r // 2) for r in range(NROW) for c in range(NCOL)
    ]
    moved = lax.ppermute(cross, BOTH, moves)
    row_cross = lax.all_gather(cross, "col", axis=0, tiled=True)
    col_cross = lax.all_gather(moved, "row", axis=0, tiled=True)

    index = index[:, :8].reshape(NDEV * 8)
    scal = jnp.concatenate(
        [
            lax.dynamic_slice(index, (row * 64,), (64,)),
            lax.dynamic_slice(index, (column * 128,), (128,)),
            jnp.stack([row, column]).astype(jnp.int32),
        ]
    )
    return tuple(schur(scal, lower_high, lower_low, inv, col_cross, row_cross, diag, damp))


def solution(mesh):
    placed = (P(("row", "col"), None), P(("row", "col"), None, None), P("row"))
    return jax.shard_map(
        local,
        mesh=mesh,
        in_specs=placed,
        out_specs=(P("row", None), P("row", "col")),
        check_vma=False,
    )
```

```python
import jax
import jax.numpy as jnp
from jax import lax
from jax.experimental import pallas as pl
from jax.experimental.pallas import tpu as pltpu
from jax.sharding import PartitionSpec as P

F32 = jnp.float32
BF16 = jnp.bfloat16
HI = lax.Precision.HIGHEST
BOTH = ("row", "col")
NROW, NCOL = 16, 8
NDEV = NROW * NCOL
TILE = 128
LEAD = 8
SLOTS1 = 16
SLOTS2 = 40
DAMP_SLOT = 36
VMEM = pltpu.VMEM
SMEM = pltpu.SMEM


def nt(a, b, precision=None):
    return lax.dot_general(
        a, b, (((1,), (1,)), ((), ())), precision=precision, preferred_element_type=F32
    )


def tn(a, b, precision=None):
    return lax.dot_general(
        a, b, (((0,), (0,)), ((), ())), precision=precision, preferred_element_type=F32
    )


def split(x):
    high = x.astype(BF16)
    return high, (x - high.astype(F32)).astype(BF16)


def nt3(ah, al, bh, bl):
    return nt(ah, bh) + (nt(ah, bl) + nt(al, bh))


def first_tile(b):
    return b * LEAD - (b * (b - 1)) // 2


def gram_kernel(jac_ref, idx_ref, damp_ref, pay_ref, cross_ref):
    q = pl.program_id(0)
    high, low = split(jac_ref[0])
    mixed = tn(high, low)
    gram = tn(high, high) + (mixed + mixed.T)
    pay_ref[pl.ds(q, TILE, stride=SLOTS1), :] = gram[:TILE, :TILE]
    pay_ref[pl.ds(q + 4, TILE, stride=SLOTS1), :] = gram[TILE:, TILE:]
    pay_ref[pl.ds(q + 8, TILE, stride=SLOTS1), :] = gram[:TILE, TILE:]
    cross_ref[0] = gram[:TILE, TILE:]

    @pl.when(q == 0)
    def _():
        lane = lax.broadcasted_iota(jnp.int32, (TILE, TILE), 1)
        index = jnp.zeros((TILE, TILE), F32)
        for e in range(8):
            index = jnp.where(lane == e, idx_ref[e // 2, e % 2].astype(F32), index)
        pay_ref[pl.ds(12, TILE, stride=SLOTS1), :] = index
        rows = [damp_ref[TILE * b : TILE * (b + 1)].reshape(1, TILE) for b in range(LEAD)]
        wide = jnp.concatenate(rows + [jnp.zeros((TILE - 8, TILE), F32)], axis=0)
        pay_ref[pl.ds(13, TILE, stride=SLOTS1), :] = wide.T
        zero = jnp.zeros((TILE, TILE), F32)
        pay_ref[pl.ds(14, TILE, stride=SLOTS1), :] = zero
        pay_ref[pl.ds(15, TILE, stride=SLOTS1), :] = zero


def grams(jacobian, idx, damp):
    return pl.pallas_call(
        gram_kernel,
        grid=(4,),
        in_specs=[
            pl.BlockSpec((1, 1024, 256), lambda q: (q, 0, 0)),
            pl.BlockSpec(memory_space=SMEM),
            pl.BlockSpec((1024,), lambda q: (0,)),
        ],
        out_specs=[
            pl.BlockSpec((TILE * SLOTS1, TILE), lambda q: (0, 0)),
            pl.BlockSpec((1, TILE, TILE), lambda q: (q, 0, 0)),
        ],
        out_shape=[
            jax.ShapeDtypeStruct((TILE * SLOTS1, TILE), F32),
            jax.ShapeDtypeStruct((4, TILE, TILE), F32),
        ],
        name="grams",
    )(jacobian, idx, damp)


def gather_kernel(recv_ref, pay_ref, diag_ref, idx_ref):
    lane = lax.broadcasted_iota(jnp.int32, (TILE, TILE), 1)
    sub = lax.broadcasted_iota(jnp.int32, (TILE, TILE), 0)
    index = recv_ref[pl.ds(12, NDEV, stride=SLOTS1), :].astype(jnp.int32)
    idx_ref[...] = index
    across = recv_ref[pl.ds(12, NDEV, stride=SLOTS1), :].T.astype(jnp.int32)
    diag = jnp.zeros((TILE, TILE), F32)
    lead = jnp.zeros((40, TILE), F32)
    sub40 = lax.broadcasted_iota(jnp.int32, (40, TILE), 0)
    lane40 = lax.broadcasted_iota(jnp.int32, (40, TILE), 1)
    for q in range(4):
        a = across[2 * q : 2 * q + 1, :]
        b = across[2 * q + 1 : 2 * q + 2, :]
        first = recv_ref[pl.ds(q, NDEV, stride=SLOTS1), :]
        second = recv_ref[pl.ds(q + 4, NDEV, stride=SLOTS1), :]
        cross = recv_ref[pl.ds(q + 8, NDEV, stride=SLOTS1), :]
        diag = diag + jnp.dot((sub == a).astype(F32), first, precision=HI)
        diag = diag + jnp.dot((sub == b).astype(F32), second, precision=HI)
        place = first_tile(b) + (a - b)
        hit = (sub40 == place) & (lane40 < NCOL)
        lead = lead + jnp.dot(hit.astype(F32), cross, precision=HI)
    hit = (sub40 == first_tile(lane40)) & (lane40 < LEAD)
    lead = lead + jnp.dot(hit.astype(F32), diag, precision=HI)
    damp = jnp.broadcast_to(recv_ref[13:14, :], (40, TILE))
    lead = jnp.where(sub40 == DAMP_SLOT, damp, lead)
    for r in range(NROW):
        for c in range(NCOL):
            device = r * NCOL + c
            pay_ref[device * SLOTS2 : (device + 1) * SLOTS2, :] = lead
            diag_ref[device * LEAD : (device + 1) * LEAD, :] = diag[8 * r : 8 * r + 8, :]


def gather_rows(recv):
    return pl.pallas_call(
        gather_kernel,
        out_shape=[
            jax.ShapeDtypeStruct((NDEV * SLOTS2, TILE), F32),
            jax.ShapeDtypeStruct((NDEV * LEAD, TILE), F32),
            jax.ShapeDtypeStruct((NDEV, TILE), jnp.int32),
        ],
        name="gather_rows",
    )(recv)


def factor128(rows):
    lane = lax.broadcasted_iota(jnp.int32, (8, TILE), 1)
    sub = lax.broadcasted_iota(jnp.int32, (8, TILE), 0)
    block = list(rows)
    inv = [jnp.where(lane == sub + 8 * v, 1.0, 0.0) for v in range(16)]
    upper, inverse = [], []

    def row(x, i):
        return jnp.broadcast_to(x[i : i + 1, :], (8, TILE))

    def col(x, i):
        return jnp.broadcast_to(x[:, i : i + 1], (8, TILE))

    for t in range(16):
        cols = [col(block[t], 8 * t + k) for k in range(8)]
        left, right = block[t], inv[t]
        up = jnp.zeros((8, TILE), F32)
        low, recip = up, up
        for j in range(8):
            pivot = row(cols[j], j)
            root = lax.rsqrt(pivot)
            over = 1.0 / pivot
            hit = sub == j
            scale = jnp.where(hit, 0.0, cols[j] * over)
            left_row, right_row = row(left, j), row(right, j)
            up = jnp.where(hit, left_row * root, up)
            low = jnp.where(hit, right_row * root, low)
            recip = jnp.where(hit, over, recip)
            for k in range(j + 1, 8):
                cols[k] = cols[k] - scale * row(cols[k], j)
            left = left - scale * left_row
            right = right - scale * right_row
        upper.append(jnp.where(lane >= sub + 8 * t, up, 0.0))
        inverse.append(low)
        if t < 15:
            left, right = left * recip, right * recip
            lefts = [row(left, j) for j in range(8)]
            rights = [row(right, j) for j in range(8)]
            for v in range(t + 1, 16):
                parts = [col(block[v], 8 * t + k) for k in range(8)]
                one = [parts[k] * lefts[k] for k in range(8)]
                two = [parts[k] * rights[k] for k in range(8)]
                while len(one) > 1:
                    one = [one[i] + one[i + 1] for i in range(0, len(one), 2)]
                    two = [two[i] + two[i + 1] for i in range(0, len(two), 2)]
                block[v] = block[v] - one[0]
                inv[v] = inv[v] - two[0]
    return upper, inverse


def at(i, n=TILE):
    return pl.ds(pl.multiple_of(i * n, n), n)


def three(x):
    high = x.astype(BF16)
    rest = x - high.astype(F32)
    mid = rest.astype(BF16)
    return high, mid, (rest - mid.astype(F32)).astype(BF16)


def stacks(x):
    h, m, low = three(x)
    return (
        jnp.concatenate([h, h], axis=1),
        jnp.concatenate([m, h], axis=1),
        jnp.concatenate([low, m], axis=1),
    )


def right_stacks(x):
    h, m, low = three(x)
    return jnp.concatenate([h, m], axis=1), jnp.concatenate([h, low], axis=1)


def six(pa, pb, pc, ra, rb):
    return nt(pa, ra) + (nt(pb, rb) + nt(pc, ra))


def nn(a, b):
    return jnp.dot(a, b, precision=HI, preferred_element_type=F32)


def factor_kernel(
    recv_ref, lh_hbm, ll_hbm, wh_hbm, wl_hbm,
    lh_ref, ll_ref, wh_ref, wl_ref, body, inv_ref, pa, pb, pc, ra, rb, sem,
):
    place = 0
    lane = lax.broadcasted_iota(jnp.int32, (TILE, TILE), 1)
    sub = lax.broadcasted_iota(jnp.int32, (TILE, TILE), 0)
    damp = recv_ref[pl.ds(DAMP_SLOT, TILE, stride=SLOTS2), :]
    for k in range(LEAD):
        for i in range(k, LEAD):
            tile = recv_ref[pl.ds(place, TILE, stride=SLOTS2), :]
            if i == k:
                tile = tile + jnp.where(lane == sub, damp[:, k : k + 1], 0.0)
            body[TILE * i : TILE * (i + 1), TILE * k : TILE * (k + 1)] = tile
            place += 1

    def step(k, _):
        rows = [
            body[pl.ds(pl.multiple_of(k * TILE + 8 * v, 8), 8), at(k)] for v in range(16)
        ]
        upper, inverse = factor128(rows)
        inv = jnp.concatenate(inverse, axis=0)
        inv_ref[at(k), :] = inv
        wa, wb = right_stacks(inv)

        def panel(i, _):
            x = six(*stacks(body[at(i, 512), at(k)]), wa, wb)
            index = i * 512 + lax.broadcasted_iota(jnp.int32, (512, TILE), 0)
            x = jnp.where(index >= (k + 1) * TILE, x, 0.0)
            h, m, low = three(x)
            pa[at(i, 512), :] = jnp.concatenate([h, h], axis=1)
            pb[at(i, 512), :] = jnp.concatenate([m, h], axis=1)
            pc[at(i, 512), :] = jnp.concatenate([low, m], axis=1)
            ra[at(i, 512), :] = jnp.concatenate([h, m], axis=1)
            rb[at(i, 512), :] = jnp.concatenate([h, low], axis=1)
            lh_ref[at(i, 512), at(k)] = h
            ll_ref[at(i, 512), at(k)] = m
            return 0

        begin = (k >= 3).astype(jnp.int32)

        @pl.when(k >= 3)
        def _():
            zero = jnp.zeros((512, TILE), BF16)
            lh_ref[:512, at(k)] = zero
            ll_ref[:512, at(k)] = zero

        lax.fori_loop(begin, 2, panel, 0)

        def update(j, _):
            wa, wb = ra[at(j, 256), :], rb[at(j, 256), :]

            def rows_of(i, _):
                part = at(i, 512)
                body[part, at(j, 256)] -= six(pa[part, :], pb[part, :], pc[part, :], wa, wb)
                return 0

            lax.fori_loop((j >= 2).astype(jnp.int32), 2, rows_of, 0)
            return 0

        lax.fori_loop((k + 1) // 2, 4, update, 0)
        tile = jnp.concatenate(upper, axis=0).T
        body[at(k), at(k)] = tile
        lh_ref[at(k), at(k)], ll_ref[at(k), at(k)] = split(tile)
        pltpu.make_async_copy(lh_ref.at[:, at(k)], lh_hbm.at[:, at(k)], sem.at[0]).start()
        pltpu.make_async_copy(ll_ref.at[:, at(k)], ll_hbm.at[:, at(k)], sem.at[1]).start()
        return 0

    lax.fori_loop(0, LEAD, step, 0)
    for g in range(4):
        one = slice(256 * g, 256 * g + TILE)
        two = slice(256 * g + TILE, 256 * g + 256)
        cross = lh_ref[two, one].astype(F32) + ll_ref[two, one].astype(F32)
        corner = -nn(inv_ref[two, :], nn(cross, inv_ref[one, :]))
        wh_ref[one, :TILE], wl_ref[one, :TILE] = split(inv_ref[one, :])
        zero = jnp.zeros((TILE, TILE), BF16)
        wh_ref[one, TILE:], wl_ref[one, TILE:] = zero, zero
        wh_ref[two, :TILE], wl_ref[two, :TILE] = split(corner)
        wh_ref[two, TILE:], wl_ref[two, TILE:] = split(inv_ref[two, :])
    last = [
        pltpu.make_async_copy(wh_ref, wh_hbm, sem.at[2]),
        pltpu.make_async_copy(wl_ref, wl_hbm, sem.at[3]),
    ]
    for copy in last:
        copy.start()
    pltpu.make_async_copy(lh_ref, lh_hbm, sem.at[0]).wait()
    pltpu.make_async_copy(ll_ref, ll_hbm, sem.at[1]).wait()
    for copy in last:
        copy.wait()


def factorise(recv):
    return pl.pallas_call(
        factor_kernel,
        in_specs=[pl.BlockSpec(memory_space=VMEM)],
        out_specs=[pl.BlockSpec(memory_space=pltpu.HBM)] * 4,
        out_shape=[
            jax.ShapeDtypeStruct((1024, 1024), BF16),
            jax.ShapeDtypeStruct((1024, 1024), BF16),
            jax.ShapeDtypeStruct((1024, 256), BF16),
            jax.ShapeDtypeStruct((1024, 256), BF16),
        ],
        scratch_shapes=[VMEM((1024, 1024), BF16)] * 2
        + [VMEM((1024, 256), BF16)] * 2
        + [VMEM((1024, 1024), F32), VMEM((1024, TILE), F32)]
        + [VMEM((1024, 256), BF16)] * 5
        + [pltpu.SemaphoreType.DMA((4,))],
        compiler_params=pltpu.CompilerParams(vmem_limit_bytes=58 * 1024 * 1024),
        cost_estimate=pl.CostEstimate(
            flops=40_000_000_000, bytes_accessed=8_000_000, transcendentals=0
        ),
        name="factorise",
    )(recv)


def schur_kernel(
    scal_ref, damp_ref, lh_hbm, ll_hbm, wh_hbm, wl_hbm, col_hbm, cross_hbm, diag_hbm,
    factor_hbm, out_hbm,
    lh_ref, ll_ref, wh_ref, wl_ref, col_ref, cross_ref, diag_ref, out_ref, rows, ch, cl,
    none_ref, where_ref, tiles_ref, load_sem, factor_sem, out_sem,
):
    row = scal_ref[192]
    column = scal_ref[193]
    loads = [
        pltpu.make_async_copy(source, target, load_sem.at[i])
        for i, (source, target) in enumerate(
            [
                (cross_hbm, cross_ref),
                (col_hbm, col_ref),
                (diag_hbm, diag_ref),
                (lh_hbm, lh_ref),
                (ll_hbm, ll_ref),
                (wh_hbm, wh_ref),
                (wl_hbm, wl_ref),
            ]
        )
    ]
    for copy in loads:
        copy.start()
    none_ref[...] = jnp.zeros_like(none_ref)
    for u in range(24):
        where_ref[u] = 0

    def mark_row(p, _):
        a = scal_ref[2 * p] - LEAD * row
        where_ref[a] = jnp.where(scal_ref[2 * p + 1] < LEAD, 1, where_ref[a])
        return 0

    def mark_col(p, _):
        tile = scal_ref[64 + 2 * p]
        a = tile - 16 * column + LEAD
        used = (scal_ref[65 + 2 * p] < LEAD) & (tile >= LEAD) & (tile <= LEAD * row + 7)
        where_ref[a] = jnp.where(used, 1, where_ref[a])
        return 0

    @pl.when(row >= 1)
    def _():
        lax.fori_loop(0, 32, mark_row, 0)
        lax.fori_loop(0, 64, mark_col, 0)

    def place(u, count):
        used = where_ref[u] == 1
        where_ref[u] = jnp.where(used, count, -1)
        tiles_ref[count] = u
        return count + used.astype(jnp.int32)

    n_row = lax.fori_loop(0, LEAD, place, jnp.int32(0))
    total = lax.fori_loop(LEAD, 24, place, n_row)

    def blank(i, _):
        out_ref[at(i, 32), :] = jnp.zeros((32, 2048), F32)
        return 0

    lax.fori_loop(0, 32, blank, 0)

    def clear(i, _):
        rows[at(i), :] = jnp.zeros((TILE, 1024), F32)
        return 0

    lax.fori_loop(0, total, clear, 0)
    loads[0].wait()

    def fill_row(p, _):
        a = scal_ref[2 * p] - LEAD * row
        b = scal_ref[2 * p + 1]
        here = b - 16 * column

        @pl.when((b < LEAD) & (where_ref[a] >= 0))
        def _():
            rows[at(where_ref[a]), at(b)] += cross_ref[at(p), :]

        @pl.when((b >= LEAD) & (here >= 0) & (here < 16))
        def _():
            out_ref[at(a), at(here)] += cross_ref[at(p), :]

        return 0

    def fill_col(p, _):
        a = scal_ref[64 + 2 * p] - 16 * column + LEAD
        b = scal_ref[65 + 2 * p]

        @pl.when((b < LEAD) & (where_ref[a] >= 0))
        def _():
            rows[at(where_ref[a]), at(b)] += col_ref[at(p), :]

        return 0

    lax.fori_loop(0, 32, fill_row, 0)
    loads[1].wait()
    lax.fori_loop(0, 64, fill_col, 0)
    loads[2].wait()

    @pl.when((row >= 1) & (row // 2 == column))
    def _():
        lane = lax.broadcasted_iota(jnp.int32, (TILE, TILE), 1)
        sub = lax.broadcasted_iota(jnp.int32, (TILE, TILE), 0)
        for s in range(LEAD):
            damp = damp_ref[TILE * s : TILE * (s + 1)].reshape(1, TILE)
            damp = jnp.broadcast_to(damp, (TILE, TILE))
            tile = diag_ref[pl.ds(s, TILE, stride=LEAD), :] + jnp.where(lane == sub, damp, 0.0)
            out_ref[TILE * s : TILE * (s + 1), at(LEAD * (row % 2) + s)] += tile

    for copy in loads[3:]:
        copy.wait()

    for g in range(4):
        here = slice(256 * g, 256 * (g + 1))

        def solve(i, _, g=g, here=here):
            rest = rows[at(i, 512), here]
            if g:
                rest = rest - nt3(
                    ch[at(i, 512), : 256 * g],
                    cl[at(i, 512), : 256 * g],
                    lh_ref[here, : 256 * g],
                    ll_ref[here, : 256 * g],
                )
            x = nt3(*split(rest), wh_ref[here, :], wl_ref[here, :])
            rows[at(i, 512), here] = x
            ch[at(i, 512), here], cl[at(i, 512), here] = split(x)
            return 0

        lax.fori_loop(0, (total + 3) // 4, solve, 0)

    for s in range(LEAD):
        part = slice(TILE * s, TILE * (s + 1))

        @pl.when(row == 0)
        def _(part=part):
            rows[part, :] = lh_ref[part, :].astype(F32) + ll_ref[part, :].astype(F32)
            pltpu.make_async_copy(rows.at[part], factor_hbm.at[part], factor_sem.at[0]).start()

        @pl.when((row >= 1) & (where_ref[s] >= 0))
        def _(s=s, part=part):
            pltpu.make_async_copy(
                rows.at[at(where_ref[s])], factor_hbm.at[part], factor_sem.at[0]
            ).start()

        @pl.when((row >= 1) & (where_ref[s] < 0))
        def _(part=part):
            pltpu.make_async_copy(none_ref, factor_hbm.at[part], factor_sem.at[0]).start()

    n_col = total - n_row

    def send(c):
        part = at(c)
        pltpu.make_async_copy(out_ref.at[:, part], out_hbm.at[:, part], out_sem.at[0]).start()

    def columns(j, sent):
        jt = n_row + 2 * j
        right = pl.ds(pl.multiple_of(jt * TILE, TILE), 256)

        def blocks(i, _):
            left = at(i, 256)
            prod = nt3(ch[left, :], cl[left, :], ch[right, :], cl[right, :])
            for p in range(2):
                for q in range(2):
                    it = 2 * i + p
                    a = tiles_ref[jnp.minimum(it, 23)]
                    b = tiles_ref[jnp.minimum(jt + q, 23)] - LEAD
                    keep = (it < n_row) & (jt + q < total) & (LEAD * row + a >= 16 * column + b)

                    @pl.when(keep)
                    def _(a=a, b=b, p=p, q=q):
                        out_ref[at(a), at(b)] -= prod[
                            TILE * p : TILE * (p + 1), TILE * q : TILE * (q + 1)
                        ]

            return 0

        lax.fori_loop(0, (n_row + 1) // 2, blocks, 0)
        done = tiles_ref[jnp.minimum(jt + 1, total - 1)] - LEAD + 1

        def one(c, _):
            send(c)
            return 0

        lax.fori_loop(sent, done, one, 0)
        return done

    sent = lax.fori_loop(0, (n_col + 1) // 2, columns, jnp.int32(0))

    def last(c, _):
        send(c)
        return 0

    lax.fori_loop(sent, 16, last, 0)
    pltpu.make_async_copy(rows.at[:1024], factor_hbm, factor_sem.at[0]).wait()
    pltpu.make_async_copy(out_ref, out_hbm, out_sem.at[0]).wait()


def schur(scal, lh, ll, wh, wl, col_cross, cross, diag, damp):
    return pl.pallas_call(
        schur_kernel,
        in_specs=[pl.BlockSpec(memory_space=SMEM), pl.BlockSpec(memory_space=VMEM)]
        + [pl.BlockSpec(memory_space=pltpu.HBM)] * 7,
        out_specs=[pl.BlockSpec(memory_space=pl.ANY)] * 2,
        out_shape=[
            jax.ShapeDtypeStruct((1024, 1024), F32),
            jax.ShapeDtypeStruct((1024, 2048), F32),
        ],
        scratch_shapes=[
            VMEM((1024, 1024), BF16),
            VMEM((1024, 1024), BF16),
            VMEM((1024, 256), BF16),
            VMEM((1024, 256), BF16),
            VMEM((64 * TILE, TILE), F32),
            VMEM((32 * TILE, TILE), F32),
            VMEM((NDEV * LEAD, TILE), F32),
            VMEM((1024, 2048), F32),
            VMEM((3072, 1024), F32),
            VMEM((3328, 1024), BF16),
            VMEM((3328, 1024), BF16),
            VMEM((TILE, 1024), F32),
            SMEM((24,), jnp.int32),
            SMEM((25,), jnp.int32),
            pltpu.SemaphoreType.DMA((7,)),
            pltpu.SemaphoreType.DMA((1,)),
            pltpu.SemaphoreType.DMA((1,)),
        ],
        compiler_params=pltpu.CompilerParams(vmem_limit_bytes=60 * 1024 * 1024),
        cost_estimate=pl.CostEstimate(
            flops=20_000_000_000, bytes_accessed=30_000_000, transcendentals=0
        ),
        name="schur",
    )(scal, damp, lh, ll, wh, wl, col_cross, cross, diag)


def local(pair_list, jacobian, damping):
    row = lax.axis_index("row")
    column = lax.axis_index("col")
    payload, cross = grams(jacobian, pair_list, damping)
    recv = lax.all_to_all(payload.reshape(NDEV, SLOTS1, TILE), BOTH, 0, 0, tiled=True)
    payload, diag, index = gather_rows(recv.reshape(NDEV * SLOTS1, TILE))
    cross = cross.reshape(4 * TILE, TILE)
    moves = [
        (r * NCOL + c, (NCOL * (r % 2) + c) * NCOL + r // 2) for r in range(NROW) for c in range(NCOL)
    ]
    moved = lax.ppermute(cross, BOTH, moves)
    payload, cross, moved = lax.optimization_barrier((payload, cross, moved))
    recv = lax.all_to_all(payload.reshape(NDEV, SLOTS2, TILE), BOTH, 0, 0, tiled=True)
    recv, diag = lax.optimization_barrier((recv, diag))
    diag = lax.all_to_all(diag.reshape(NDEV, LEAD, TILE), BOTH, 0, 0, tiled=True)
    diag = diag.reshape(NDEV * LEAD, TILE)
    lh, ll, wh, wl = factorise(recv.reshape(NDEV * SLOTS2, TILE))

    row_cross = lax.all_gather(cross, "col", axis=0, tiled=True)
    col_cross = lax.all_gather(moved, "row", axis=0, tiled=True)

    index = index[:, :8].reshape(NDEV * 8)
    scal = jnp.concatenate(
        [
            lax.dynamic_slice(index, (row * 64,), (64,)),
            lax.dynamic_slice(index, (column * 128,), (128,)),
            jnp.stack([row, column]).astype(jnp.int32),
        ]
    )
    return tuple(schur(scal, lh, ll, wh, wl, col_cross, row_cross, diag, damping))


def solution(mesh):
    placed = (P(("row", "col"), None), P(("row", "col"), None, None), P("row"))
    return jax.shard_map(
        local,
        mesh=mesh,
        in_specs=placed,
        out_specs=(P("row", None), P("row", "col")),
        check_vma=False,
    )
```

```python
import jax
import jax.numpy as jnp
from jax import lax
from jax.experimental import pallas as pl
from jax.experimental.pallas import tpu as pltpu
from jax.sharding import PartitionSpec as P

F32 = jnp.float32
BF16 = jnp.bfloat16
HI = lax.Precision.HIGHEST
BOTH = ("row", "col")
NROW, NCOL = 16, 8
NDEV = NROW * NCOL
TILE = 128
LEAD = 8
SLOTS1 = 16
SLOTS2 = 40
DAMP_SLOT = 36
VMEM = pltpu.VMEM
SMEM = pltpu.SMEM


def nt(a, b, precision=None):
    return lax.dot_general(
        a, b, (((1,), (1,)), ((), ())), precision=precision, preferred_element_type=F32
    )


def tn(a, b, precision=None):
    return lax.dot_general(
        a, b, (((0,), (0,)), ((), ())), precision=precision, preferred_element_type=F32
    )


def split(x):
    high = x.astype(BF16)
    return high, (x - high.astype(F32)).astype(BF16)


def nt3(ah, al, bh, bl):
    return nt(ah, bh) + (nt(ah, bl) + nt(al, bh))


def nn3(ah, al, bh, bl):
    def nn(a, b):
        return jnp.dot(a, b, preferred_element_type=F32)

    return nn(ah, bh) + (nn(ah, bl) + nn(al, bh))


def first_tile(b):
    return b * LEAD - (b * (b - 1)) // 2


def gram_kernel(jac_ref, idx_ref, damp_ref, pay_ref, cross_ref):
    q = pl.program_id(0)
    high, low = split(jac_ref[0])
    mixed = tn(high, low)
    gram = tn(high, high) + (mixed + mixed.T)
    pay_ref[pl.ds(q, TILE, stride=SLOTS1), :] = gram[:TILE, :TILE]
    pay_ref[pl.ds(q + 4, TILE, stride=SLOTS1), :] = gram[TILE:, TILE:]
    pay_ref[pl.ds(q + 8, TILE, stride=SLOTS1), :] = gram[:TILE, TILE:]
    cross_ref[0] = gram[:TILE, TILE:]

    @pl.when(q == 0)
    def _():
        lane = lax.broadcasted_iota(jnp.int32, (TILE, TILE), 1)
        index = jnp.zeros((TILE, TILE), F32)
        for e in range(8):
            index = jnp.where(lane == e, idx_ref[e // 2, e % 2].astype(F32), index)
        pay_ref[pl.ds(12, TILE, stride=SLOTS1), :] = index
        rows = [damp_ref[TILE * b : TILE * (b + 1)].reshape(1, TILE) for b in range(LEAD)]
        wide = jnp.concatenate(rows + [jnp.zeros((TILE - 8, TILE), F32)], axis=0)
        pay_ref[pl.ds(13, TILE, stride=SLOTS1), :] = wide.T
        zero = jnp.zeros((TILE, TILE), F32)
        pay_ref[pl.ds(14, TILE, stride=SLOTS1), :] = zero
        pay_ref[pl.ds(15, TILE, stride=SLOTS1), :] = zero


def grams(jacobian, idx, damp):
    return pl.pallas_call(
        gram_kernel,
        grid=(4,),
        in_specs=[
            pl.BlockSpec((1, 1024, 256), lambda q: (q, 0, 0)),
            pl.BlockSpec(memory_space=SMEM),
            pl.BlockSpec((1024,), lambda q: (0,)),
        ],
        out_specs=[
            pl.BlockSpec((TILE * SLOTS1, TILE), lambda q: (0, 0)),
            pl.BlockSpec((1, TILE, TILE), lambda q: (q, 0, 0)),
        ],
        out_shape=[
            jax.ShapeDtypeStruct((TILE * SLOTS1, TILE), F32),
            jax.ShapeDtypeStruct((4, TILE, TILE), F32),
        ],
        name="grams",
    )(jacobian, idx, damp)


def gather_kernel(recv_ref, pay_ref, diag_ref, idx_ref):
    lane = lax.broadcasted_iota(jnp.int32, (TILE, TILE), 1)
    sub = lax.broadcasted_iota(jnp.int32, (TILE, TILE), 0)
    index = recv_ref[pl.ds(12, NDEV, stride=SLOTS1), :].astype(jnp.int32)
    idx_ref[...] = index
    across = recv_ref[pl.ds(12, NDEV, stride=SLOTS1), :].T.astype(jnp.int32)
    diag = jnp.zeros((TILE, TILE), F32)
    lead = jnp.zeros((40, TILE), F32)
    sub40 = lax.broadcasted_iota(jnp.int32, (40, TILE), 0)
    lane40 = lax.broadcasted_iota(jnp.int32, (40, TILE), 1)
    for q in range(4):
        a = across[2 * q : 2 * q + 1, :]
        b = across[2 * q + 1 : 2 * q + 2, :]
        first = recv_ref[pl.ds(q, NDEV, stride=SLOTS1), :]
        second = recv_ref[pl.ds(q + 4, NDEV, stride=SLOTS1), :]
        cross = recv_ref[pl.ds(q + 8, NDEV, stride=SLOTS1), :]
        diag = diag + jnp.dot((sub == a).astype(F32), first, precision=HI)
        diag = diag + jnp.dot((sub == b).astype(F32), second, precision=HI)
        place = first_tile(b) + (a - b)
        hit = (sub40 == place) & (lane40 < NCOL)
        lead = lead + jnp.dot(hit.astype(F32), cross, precision=HI)
    hit = (sub40 == first_tile(lane40)) & (lane40 < LEAD)
    lead = lead + jnp.dot(hit.astype(F32), diag, precision=HI)
    damp = jnp.broadcast_to(recv_ref[13:14, :], (40, TILE))
    lead = jnp.where(sub40 == DAMP_SLOT, damp, lead)
    for r in range(NROW):
        for c in range(NCOL):
            device = r * NCOL + c
            pay_ref[device * SLOTS2 : (device + 1) * SLOTS2, :] = lead
            diag_ref[device * LEAD : (device + 1) * LEAD, :] = diag[8 * r : 8 * r + 8, :]


def gather_rows(recv):
    return pl.pallas_call(
        gather_kernel,
        out_shape=[
            jax.ShapeDtypeStruct((NDEV * SLOTS2, TILE), F32),
            jax.ShapeDtypeStruct((NDEV * LEAD, TILE), F32),
            jax.ShapeDtypeStruct((NDEV, TILE), jnp.int32),
        ],
        name="gather_rows",
    )(recv)


def pieces(x):
    high = x.astype(BF16).astype(F32)
    rest = x - high
    mid = rest.astype(BF16).astype(F32)
    return high, mid, rest - mid


def factor128(rows):
    lane = lax.broadcasted_iota(jnp.int32, (8, TILE), 1)
    sub = lax.broadcasted_iota(jnp.int32, (8, TILE), 0)
    block = list(rows)
    inv = [jnp.where(lane == sub + 8 * v, 1.0, 0.0) for v in range(16)]
    upper, inverse = [], []

    def row(x, i):
        return jnp.broadcast_to(x[i : i + 1, :], (8, TILE))

    def col(x, i):
        return jnp.broadcast_to(x[:, i : i + 1], (8, TILE))

    for t in range(16):
        cols = [col(block[t], 8 * t + k) for k in range(8)]
        left, right = block[t], inv[t]
        up = jnp.zeros((8, TILE), F32)
        low = up
        for j in range(0, 8, 2):
            one, two = sub == j, sub == j + 1
            both = one | two
            x, y = cols[j], cols[j + 1]
            p, b, q = row(x, j), row(x, j + 1), row(y, j + 1)
            det = p * q - b * b
            over = 1.0 / det
            n1 = jnp.where(one, -q, jnp.where(two, b, x * q - y * b))
            n2 = jnp.where(one, b, jnp.where(two, -p, y * p - x * b))
            for k in range(j + 2, 8):
                change = (n1 * row(cols[k], j) + n2 * row(cols[k], j + 1)) * over
                cols[k] = jnp.where(both, 0.0, cols[k]) - change
            m1, m2 = n1 * over, n2 * over
            inv_p = 1.0 / p
            root_1, root_2, ratio = lax.rsqrt(p), lax.rsqrt(det * inv_p), b * inv_p
            l1, l2, r1, r2 = row(left, j), row(left, j + 1), row(right, j), row(right, j + 1)
            up = jnp.where(one, l1 * root_1, jnp.where(two, (l2 - ratio * l1) * root_2, up))
            low = jnp.where(one, r1 * root_1, jnp.where(two, (r2 - ratio * r1) * root_2, low))
            left = jnp.where(both, 0.0, left) - (m1 * l1 + m2 * l2)
            right = jnp.where(both, 0.0, right) - (m1 * r1 + m2 * r2)
        upper.append(jnp.where(lane >= sub + 8 * t, up, 0.0))
        inverse.append(low)
        if t < 15:
            parts = [col(block[t + 1], 8 * t + k) for k in range(8)]
            one = [parts[k] * row(left, k) for k in range(8)]
            two = [parts[k] * row(right, k) for k in range(8)]
            while len(one) > 1:
                one = [one[i] + one[i + 1] for i in range(0, len(one), 2)]
                two = [two[i] + two[i + 1] for i in range(0, len(two), 2)]
            block[t + 1] = block[t + 1] - one[0]
            inv[t + 1] = inv[t + 1] - two[0]
        if t < 14:
            h, m, low_part = pieces(block[t])
            mult = jnp.concatenate([h, h, m, h, low_part, m], axis=0).T.astype(BF16)
            h, m, low_part = pieces(jnp.concatenate([left, right], axis=1))
            base = jnp.concatenate([h, m, h, low_part, h, m], axis=0).astype(BF16)
            late = jnp.dot(mult, base, preferred_element_type=F32)
            for v in range(t + 2, 16):
                block[v] = block[v] - late[8 * v : 8 * v + 8, :TILE]
                inv[v] = inv[v] - late[8 * v : 8 * v + 8, TILE:]
    return upper, inverse


def at(i, n=TILE):
    return pl.ds(pl.multiple_of(i * n, n), n)


def three(x):
    high = x.astype(BF16)
    rest = x - high.astype(F32)
    mid = rest.astype(BF16)
    return high, mid, (rest - mid.astype(F32)).astype(BF16)


def stacks(x):
    h, m, low = three(x)
    return (
        jnp.concatenate([h, h], axis=1),
        jnp.concatenate([m, h], axis=1),
        jnp.concatenate([low, m], axis=1),
    )


def right_stacks(x):
    h, m, low = three(x)
    return jnp.concatenate([h, m], axis=1), jnp.concatenate([h, low], axis=1)


def six(pa, pb, pc, ra, rb):
    return nt(pa, ra) + (nt(pb, rb) + nt(pc, ra))


def nn(a, b):
    return jnp.dot(a, b, precision=HI, preferred_element_type=F32)


def factor_kernel(
    recv_ref, lh_hbm, ll_hbm, wh_hbm, wl_hbm,
    lh_ref, ll_ref, wh_ref, wl_ref, body, inv_ref, pa, pb, pc, ra, rb, sem,
):
    place = 0
    lane = lax.broadcasted_iota(jnp.int32, (TILE, TILE), 1)
    sub = lax.broadcasted_iota(jnp.int32, (TILE, TILE), 0)
    damp = recv_ref[pl.ds(DAMP_SLOT, TILE, stride=SLOTS2), :]
    for k in range(LEAD):
        for i in range(k, LEAD):
            tile = recv_ref[pl.ds(place, TILE, stride=SLOTS2), :]
            if i == k:
                tile = tile + jnp.where(lane == sub, damp[:, k : k + 1], 0.0)
            body[TILE * i : TILE * (i + 1), TILE * k : TILE * (k + 1)] = tile
            place += 1

    def step(k, _):
        rows = [
            body[pl.ds(pl.multiple_of(k * TILE + 8 * v, 8), 8), at(k)] for v in range(16)
        ]
        upper, inverse = factor128(rows)
        inv = jnp.concatenate(inverse, axis=0)
        inv_ref[at(k), :] = inv
        wa, wb = right_stacks(inv)

        def panel(i, _):
            x = six(*stacks(body[at(i, 512), at(k)]), wa, wb)
            index = i * 512 + lax.broadcasted_iota(jnp.int32, (512, TILE), 0)
            x = jnp.where(index >= (k + 1) * TILE, x, 0.0)
            h, m, low = three(x)
            pa[at(i, 512), :] = jnp.concatenate([h, h], axis=1)
            pb[at(i, 512), :] = jnp.concatenate([m, h], axis=1)
            pc[at(i, 512), :] = jnp.concatenate([low, m], axis=1)
            ra[at(i, 512), :] = jnp.concatenate([h, m], axis=1)
            rb[at(i, 512), :] = jnp.concatenate([h, low], axis=1)
            lh_ref[at(i, 512), at(k)] = h
            ll_ref[at(i, 512), at(k)] = m
            return 0

        begin = (k >= 3).astype(jnp.int32)

        @pl.when(k >= 3)
        def _():
            zero = jnp.zeros((512, TILE), BF16)
            lh_ref[:512, at(k)] = zero
            ll_ref[:512, at(k)] = zero

        lax.fori_loop(begin, 2, panel, 0)

        def update(j, _):
            wa, wb = ra[at(j, 256), :], rb[at(j, 256), :]

            def rows_of(i, _):
                part = at(i, 512)
                body[part, at(j, 256)] -= six(pa[part, :], pb[part, :], pc[part, :], wa, wb)
                return 0

            lax.fori_loop((j >= 2).astype(jnp.int32), 2, rows_of, 0)
            return 0

        lax.fori_loop((k + 1) // 2, 4, update, 0)
        tile = jnp.concatenate(upper, axis=0).T
        body[at(k), at(k)] = tile
        lh_ref[at(k), at(k)], ll_ref[at(k), at(k)] = split(tile)
        pltpu.make_async_copy(lh_ref.at[:, at(k)], lh_hbm.at[:, at(k)], sem.at[0]).start()
        pltpu.make_async_copy(ll_ref.at[:, at(k)], ll_hbm.at[:, at(k)], sem.at[1]).start()
        return 0

    lax.fori_loop(0, LEAD, step, 0)
    for g in range(4):
        one = slice(256 * g, 256 * g + TILE)
        two = slice(256 * g + TILE, 256 * g + 256)
        cross = lh_ref[two, one].astype(F32) + ll_ref[two, one].astype(F32)
        corner = -nn(inv_ref[two, :], nn(cross, inv_ref[one, :]))
        wh_ref[one, :TILE], wl_ref[one, :TILE] = split(inv_ref[one, :])
        zero = jnp.zeros((TILE, TILE), BF16)
        wh_ref[one, TILE:], wl_ref[one, TILE:] = zero, zero
        wh_ref[two, :TILE], wl_ref[two, :TILE] = split(corner)
        wh_ref[two, TILE:], wl_ref[two, TILE:] = split(inv_ref[two, :])
    last = [
        pltpu.make_async_copy(wh_ref, wh_hbm, sem.at[2]),
        pltpu.make_async_copy(wl_ref, wl_hbm, sem.at[3]),
    ]
    for copy in last:
        copy.start()
    pltpu.make_async_copy(lh_ref, lh_hbm, sem.at[0]).wait()
    pltpu.make_async_copy(ll_ref, ll_hbm, sem.at[1]).wait()
    for copy in last:
        copy.wait()


def factorise(recv):
    return pl.pallas_call(
        factor_kernel,
        in_specs=[pl.BlockSpec(memory_space=VMEM)],
        out_specs=[pl.BlockSpec(memory_space=pltpu.HBM)] * 4,
        out_shape=[
            jax.ShapeDtypeStruct((1024, 1024), BF16),
            jax.ShapeDtypeStruct((1024, 1024), BF16),
            jax.ShapeDtypeStruct((1024, 256), BF16),
            jax.ShapeDtypeStruct((1024, 256), BF16),
        ],
        scratch_shapes=[VMEM((1024, 1024), BF16)] * 2
        + [VMEM((1024, 256), BF16)] * 2
        + [VMEM((1024, 1024), F32), VMEM((1024, TILE), F32)]
        + [VMEM((1024, 256), BF16)] * 5
        + [pltpu.SemaphoreType.DMA((4,))],
        compiler_params=pltpu.CompilerParams(vmem_limit_bytes=58 * 1024 * 1024),
        cost_estimate=pl.CostEstimate(
            flops=40_000_000_000, bytes_accessed=8_000_000, transcendentals=0
        ),
        name="factorise",
    )(recv)


def schur_kernel(
    scal_ref, damp_ref, lh_hbm, ll_hbm, wh_hbm, wl_hbm, col_hbm, cross_hbm, diag_hbm,
    factor_hbm, out_hbm,
    lh_ref, ll_ref, wh_ref, wl_ref, col_ref, cross_ref, diag_ref, out_ref, rows, cols,
    xh, xl, yh, yl, bh, bl, none_ref, where_ref, row_tiles, col_tiles, used_ref,
    load_sem, factor_sem, out_sem,
):
    row = scal_ref[192]
    column = scal_ref[193]
    loads = [
        pltpu.make_async_copy(source, target, load_sem.at[i])
        for i, (source, target) in enumerate(
            [
                (cross_hbm, cross_ref),
                (col_hbm, col_ref),
                (diag_hbm, diag_ref),
                (lh_hbm, lh_ref),
                (ll_hbm, ll_ref),
                (wh_hbm, wh_ref),
                (wl_hbm, wl_ref),
            ]
        )
    ]
    for copy in loads:
        copy.start()
    none_ref[...] = jnp.zeros_like(none_ref)
    for u in range(24):
        where_ref[u] = 0
    for u in range(64):
        used_ref[u] = 0

    def mark_row(p, _):
        a = scal_ref[2 * p] - LEAD * row
        where_ref[a] = jnp.where(scal_ref[2 * p + 1] < LEAD, 1, where_ref[a])
        return 0

    def mark_col(p, _):
        tile = scal_ref[64 + 2 * p]
        a = tile - 16 * column + LEAD
        b = scal_ref[65 + 2 * p]

        @pl.when((b < LEAD) & (tile >= LEAD) & (tile <= LEAD * row + 7))
        def _():
            where_ref[a] = 1
            used_ref[4 * (a - LEAD) + b // 2] = 1

        return 0

    @pl.when(row >= 1)
    def _():
        lax.fori_loop(0, 32, mark_row, 0)
        lax.fori_loop(0, 64, mark_col, 0)

    def place_row(u, count):
        used = where_ref[u] == 1
        where_ref[u] = jnp.where(used, count, -1)
        row_tiles[count] = u
        return count + used.astype(jnp.int32)

    def place_col(u, count):
        used = where_ref[u + LEAD] == 1
        where_ref[u + LEAD] = jnp.where(used, count, -1)
        col_tiles[count] = u
        return count + used.astype(jnp.int32)

    n_row = lax.fori_loop(0, LEAD, place_row, jnp.int32(0))
    n_col = lax.fori_loop(0, 16, place_col, jnp.int32(0))

    def blank(i, _):
        out_ref[at(i, 32), :] = jnp.zeros((32, 2048), F32)
        return 0

    lax.fori_loop(0, 32, blank, 0)

    def clear(i, _):
        rows[at(i), :] = jnp.zeros((TILE, 1024), F32)
        return 0

    lax.fori_loop(0, n_row, clear, 0)

    def clear_cols(i, _):
        cols[at(i), :] = jnp.zeros((TILE, 1024), F32)
        return 0

    lax.fori_loop(0, n_col, clear_cols, 0)
    loads[0].wait()

    def fill_row(p, _):
        a = scal_ref[2 * p] - LEAD * row
        b = scal_ref[2 * p + 1]
        here = b - 16 * column

        @pl.when((b < LEAD) & (where_ref[a] >= 0))
        def _():
            rows[at(where_ref[a]), at(b)] += cross_ref[at(p), :]

        @pl.when((b >= LEAD) & (here >= 0) & (here < 16))
        def _():
            out_ref[at(a), at(here)] += cross_ref[at(p), :]

        return 0

    def fill_col(p, _):
        a = scal_ref[64 + 2 * p] - 16 * column + LEAD
        b = scal_ref[65 + 2 * p]

        @pl.when((b < LEAD) & (where_ref[a] >= 0))
        def _():
            cols[at(where_ref[a]), at(b)] += col_ref[at(p), :]

        return 0

    lax.fori_loop(0, 32, fill_row, 0)
    loads[1].wait()
    lax.fori_loop(0, 64, fill_col, 0)
    loads[2].wait()

    @pl.when((row >= 1) & (row // 2 == column))
    def _():
        lane = lax.broadcasted_iota(jnp.int32, (TILE, TILE), 1)
        sub = lax.broadcasted_iota(jnp.int32, (TILE, TILE), 0)
        for s in range(LEAD):
            damp = damp_ref[TILE * s : TILE * (s + 1)].reshape(1, TILE)
            damp = jnp.broadcast_to(damp, (TILE, TILE))
            tile = diag_ref[pl.ds(s, TILE, stride=LEAD), :] + jnp.where(lane == sub, damp, 0.0)
            out_ref[TILE * s : TILE * (s + 1), at(LEAD * (row % 2) + s)] += tile

    for copy in loads[3:]:
        copy.wait()

    chunks = (n_row + 1) // 2
    for g in range(4):
        here = slice(256 * g, 256 * (g + 1))

        def forward(i, _, g=g, here=here):
            part = at(i, 256)
            rest = rows[part, here]
            if g:
                rest = rest - nt3(
                    xh[part, : 256 * g],
                    xl[part, : 256 * g],
                    lh_ref[here, : 256 * g],
                    ll_ref[here, : 256 * g],
                )
            x = nt3(*split(rest), wh_ref[here, :], wl_ref[here, :])
            rows[part, here] = x
            xh[part, here], xl[part, here] = split(x)
            return 0

        lax.fori_loop(0, chunks, forward, 0)

    for s in range(LEAD):
        part = slice(TILE * s, TILE * (s + 1))

        @pl.when(row == 0)
        def _(part=part):
            rows[part, :] = lh_ref[part, :].astype(F32) + ll_ref[part, :].astype(F32)
            pltpu.make_async_copy(rows.at[part], factor_hbm.at[part], factor_sem.at[0]).start()

        @pl.when((row >= 1) & (where_ref[s] >= 0))
        def _(s=s, part=part):
            pltpu.make_async_copy(
                rows.at[at(where_ref[s])], factor_hbm.at[part], factor_sem.at[0]
            ).start()

        @pl.when((row >= 1) & (where_ref[s] < 0))
        def _(part=part):
            pltpu.make_async_copy(none_ref, factor_hbm.at[part], factor_sem.at[0]).start()

    for g in reversed(range(4)):
        here = slice(256 * g, 256 * (g + 1))

        def backward(i, _, g=g, here=here):
            part = at(i, 256)
            rest = rows[part, here]
            if g < 3:
                past = slice(256 * (g + 1), 1024)
                rest = rest - nn3(
                    yh[part, past], yl[part, past], lh_ref[past, here], ll_ref[past, here]
                )
            yh[part, here], yl[part, here] = split(
                nn3(*split(rest), wh_ref[here, :], wl_ref[here, :])
            )
            return 0

        lax.fori_loop(0, chunks, backward, 0)

    def send(c):
        part = at(c)
        pltpu.make_async_copy(out_ref.at[:, part], out_hbm.at[:, part], out_sem.at[0]).start()

    def columns(j, sent):
        one_tile = col_tiles[2 * j]
        two_tile = col_tiles[jnp.minimum(2 * j + 1, n_col - 1)]

        def chunk(c, _):
            @pl.when((used_ref[4 * one_tile + c] | used_ref[4 * two_tile + c]) == 1)
            def _():
                bh[...], bl[...] = split(cols[at(j, 256), at(c, 256)])

                def blocks(i, _):
                    left = (at(i, 256), at(c, 256))
                    prod = nt3(yh[left], yl[left], bh[...], bl[...])
                    for p in range(2):
                        for q in range(2):
                            it = 2 * i + p
                            a = row_tiles[it]
                            b = two_tile if q else one_tile
                            keep = (it < n_row) & (LEAD * row + a >= 16 * column + b)
                            if q:
                                keep = keep & (2 * j + 1 < n_col)

                            @pl.when(keep)
                            def _(a=a, b=b, p=p, q=q):
                                out_ref[at(a), at(b)] -= prod[
                                    TILE * p : TILE * (p + 1), TILE * q : TILE * (q + 1)
                                ]

                    return 0

                lax.fori_loop(0, chunks, blocks, 0)

            return 0

        lax.fori_loop(0, 4, chunk, 0)
        done = two_tile + 1

        def one(c, _):
            send(c)
            return 0

        lax.fori_loop(sent, done, one, 0)
        return done

    sent = lax.fori_loop(0, (n_col + 1) // 2, columns, jnp.int32(0))

    def last(c, _):
        send(c)
        return 0

    lax.fori_loop(sent, 16, last, 0)
    pltpu.make_async_copy(rows, factor_hbm, factor_sem.at[0]).wait()
    pltpu.make_async_copy(out_ref, out_hbm, out_sem.at[0]).wait()


def schur(scal, lh, ll, wh, wl, col_cross, cross, diag, damp):
    return pl.pallas_call(
        schur_kernel,
        in_specs=[pl.BlockSpec(memory_space=SMEM), pl.BlockSpec(memory_space=VMEM)]
        + [pl.BlockSpec(memory_space=pltpu.HBM)] * 7,
        out_specs=[pl.BlockSpec(memory_space=pl.ANY)] * 2,
        out_shape=[
            jax.ShapeDtypeStruct((1024, 1024), F32),
            jax.ShapeDtypeStruct((1024, 2048), F32),
        ],
        scratch_shapes=[
            VMEM((1024, 1024), BF16),
            VMEM((1024, 1024), BF16),
            VMEM((1024, 256), BF16),
            VMEM((1024, 256), BF16),
            VMEM((64 * TILE, TILE), F32),
            VMEM((32 * TILE, TILE), F32),
            VMEM((NDEV * LEAD, TILE), F32),
            VMEM((1024, 2048), F32),
            VMEM((1024, 1024), F32),
            VMEM((2048, 1024), F32),
            VMEM((1024, 1024), BF16),
            VMEM((1024, 1024), BF16),
            VMEM((1024, 1024), BF16),
            VMEM((1024, 1024), BF16),
            VMEM((256, 256), BF16),
            VMEM((256, 256), BF16),
            VMEM((TILE, 1024), F32),
            SMEM((24,), jnp.int32),
            SMEM((9,), jnp.int32),
            SMEM((17,), jnp.int32),
            SMEM((64,), jnp.int32),
            pltpu.SemaphoreType.DMA((7,)),
            pltpu.SemaphoreType.DMA((1,)),
            pltpu.SemaphoreType.DMA((1,)),
        ],
        compiler_params=pltpu.CompilerParams(vmem_limit_bytes=60 * 1024 * 1024),
        cost_estimate=pl.CostEstimate(
            flops=20_000_000_000, bytes_accessed=30_000_000, transcendentals=0
        ),
        name="schur",
    )(scal, damp, lh, ll, wh, wl, col_cross, cross, diag)


def local(pair_list, jacobian, damping):
    row = lax.axis_index("row")
    column = lax.axis_index("col")
    payload, cross = grams(jacobian, pair_list, damping)
    recv = lax.all_to_all(payload.reshape(NDEV, SLOTS1, TILE), BOTH, 0, 0, tiled=True)
    cross = cross.reshape(4 * TILE, TILE)
    moves = [
        (r * NCOL + c, (NCOL * (r % 2) + c) * NCOL + r // 2) for r in range(NROW) for c in range(NCOL)
    ]
    moved = lax.ppermute(cross, BOTH, moves)
    row_cross = lax.all_gather(cross, "col", axis=0, tiled=True)
    payload, diag, index = gather_rows(recv.reshape(NDEV * SLOTS1, TILE))
    recv = lax.all_to_all(payload.reshape(NDEV, SLOTS2, TILE), BOTH, 0, 0, tiled=True)
    recv, diag, moved = lax.optimization_barrier((recv, diag, moved))
    col_cross = lax.all_gather(moved, "row", axis=0, tiled=True)
    diag = lax.all_to_all(diag.reshape(NDEV, LEAD, TILE), BOTH, 0, 0, tiled=True)
    diag = diag.reshape(NDEV * LEAD, TILE)
    lh, ll, wh, wl = factorise(recv.reshape(NDEV * SLOTS2, TILE))

    index = index[:, :8].reshape(NDEV * 8)
    scal = jnp.concatenate(
        [
            lax.dynamic_slice(index, (row * 64,), (64,)),
            lax.dynamic_slice(index, (column * 128,), (128,)),
            jnp.stack([row, column]).astype(jnp.int32),
        ]
    )
    return tuple(schur(scal, lh, ll, wh, wl, col_cross, row_cross, diag, damping))


def solution(mesh):
    placed = (P(("row", "col"), None), P(("row", "col"), None, None), P("row"))
    return jax.shard_map(
        local,
        mesh=mesh,
        in_specs=placed,
        out_specs=(P("row", None), P("row", "col")),
        check_vma=False,
    )
```

```python
import jax
import jax.numpy as jnp
from jax import lax
from jax.experimental import pallas as pl
from jax.experimental.pallas import tpu as pltpu
from jax.sharding import PartitionSpec as P

F32 = jnp.float32
BF16 = jnp.bfloat16
HI = lax.Precision.HIGHEST
BOTH = ("row", "col")
NROW, NCOL = 16, 8
NDEV = NROW * NCOL
TILE = 128
LEAD = 8
SLOTS1 = 16
SLOTS2 = 40
PAIR_SLOT = 28
DAMP_SLOT = 32
DIAG_SLOT = 33
OWN_SLOT = 36
VMEM = pltpu.VMEM
SMEM = pltpu.SMEM


def nt(a, b, precision=None):
    return lax.dot_general(
        a, b, (((1,), (1,)), ((), ())), precision=precision, preferred_element_type=F32
    )


def tn(a, b, precision=None):
    return lax.dot_general(
        a, b, (((0,), (0,)), ((), ())), precision=precision, preferred_element_type=F32
    )


def split(x):
    high = x.astype(BF16)
    return high, (x - high.astype(F32)).astype(BF16)


def nt3(ah, al, bh, bl):
    return nt(ah, bh) + (nt(ah, bl) + nt(al, bh))


def nn3(ah, al, bh, bl):
    def nn(a, b):
        return jnp.dot(a, b, preferred_element_type=F32)

    return nn(ah, bh) + (nn(ah, bl) + nn(al, bh))


def below_tile(a, b):
    return b * (LEAD - 1) - (b * (b - 1)) // 2 + (a - b - 1)


def gram_kernel(jac_ref, idx_ref, damp_ref, pay_ref, cross_ref):
    q = pl.program_id(0)
    high, low = split(jac_ref[0])
    mixed = tn(high, low)
    gram = tn(high, high) + (mixed + mixed.T)
    pay_ref[pl.ds(q, TILE, stride=SLOTS1), :] = gram[:TILE, :TILE]
    pay_ref[pl.ds(q + 4, TILE, stride=SLOTS1), :] = gram[TILE:, TILE:]
    pay_ref[pl.ds(q + 8, TILE, stride=SLOTS1), :] = gram[:TILE, TILE:]
    cross_ref[0] = gram[:TILE, TILE:]

    @pl.when(q == 0)
    def _():
        lane = lax.broadcasted_iota(jnp.int32, (TILE, TILE), 1)
        index = jnp.zeros((TILE, TILE), F32)
        for e in range(8):
            index = jnp.where(lane == e, idx_ref[e % 2, e // 2].astype(F32), index)
        pay_ref[pl.ds(12, TILE, stride=SLOTS1), :] = index
        rows = [damp_ref[TILE * b : TILE * (b + 1)].reshape(1, TILE) for b in range(LEAD)]
        wide = jnp.concatenate(rows + [jnp.zeros((TILE - 8, TILE), F32)], axis=0)
        pay_ref[pl.ds(13, TILE, stride=SLOTS1), :] = wide.T
        zero = jnp.zeros((TILE, TILE), F32)
        pay_ref[pl.ds(14, TILE, stride=SLOTS1), :] = zero
        pay_ref[pl.ds(15, TILE, stride=SLOTS1), :] = zero


def grams(jacobian, idx, damp):
    return pl.pallas_call(
        gram_kernel,
        grid=(4,),
        in_specs=[
            pl.BlockSpec((1, 1024, 256), lambda q: (q, 0, 0)),
            pl.BlockSpec(memory_space=SMEM),
            pl.BlockSpec((1024,), lambda q: (0,)),
        ],
        out_specs=[
            pl.BlockSpec((TILE * SLOTS1, TILE), lambda q: (0, 0)),
            pl.BlockSpec((1, TILE, TILE), lambda q: (q, 0, 0)),
        ],
        out_shape=[
            jax.ShapeDtypeStruct((TILE * SLOTS1, TILE), F32),
            jax.ShapeDtypeStruct((4, TILE, TILE), F32),
        ],
        name="grams",
    )(jacobian, idx, damp)


def gather_kernel(me_ref, recv_ref, pay_ref, idx_ref, flip_ref):
    me = me_ref[0]
    lane = lax.broadcasted_iota(jnp.int32, (TILE, TILE), 1)
    sub = lax.broadcasted_iota(jnp.int32, (TILE, TILE), 0)
    index = recv_ref[pl.ds(12, NDEV, stride=SLOTS1), :]
    idx_ref[...] = index.astype(jnp.int32)
    across = index.T.astype(jnp.int32)
    diag = jnp.zeros((TILE, TILE), F32)
    lead = jnp.zeros((32, TILE), F32)
    sub32 = lax.broadcasted_iota(jnp.int32, (32, TILE), 0)
    lane32 = lax.broadcasted_iota(jnp.int32, (32, TILE), 1)
    for q in range(4):
        a = across[2 * q : 2 * q + 1, :]
        b = across[2 * q + 1 : 2 * q + 2, :]
        first = recv_ref[pl.ds(q, NDEV, stride=SLOTS1), :]
        second = recv_ref[pl.ds(q + 4, NDEV, stride=SLOTS1), :]
        cross = recv_ref[pl.ds(q + 8, NDEV, stride=SLOTS1), :]
        diag = diag + jnp.dot((sub == a).astype(F32), first, precision=HI)
        diag = diag + jnp.dot((sub == b).astype(F32), second, precision=HI)
        hit = (sub32 == below_tile(a, b)) & (lane32 < NCOL)
        lead = lead + jnp.dot(hit.astype(F32), cross, precision=HI)
    packed = jnp.where(lane <= me, pltpu.roll(diag, 4, 0), diag)
    flip_ref[...] = diag.T
    entries = jnp.broadcast_to(flip_ref[pl.ds(me, 1), :], (8, TILE))
    damp = jnp.broadcast_to(recv_ref[13:14, :], (8, TILE))
    sub8 = lax.broadcasted_iota(jnp.int32, (8, TILE), 0)
    head = jnp.where(sub8 == 0, damp, jnp.where(sub8 == 1, entries, 0.0))
    last = jnp.where(sub8 >= 4, packed[:8, :], lead[24:, :])
    for r in range(NROW):
        tail = jnp.where(sub8 >= 4, packed[8 * r : 8 * r + 8, :], head)
        for c in range(NCOL):
            base = (r * NCOL + c) * SLOTS2
            pay_ref[base : base + 24, :] = lead[:24, :]
            pay_ref[base + 24 : base + 32, :] = last
            pay_ref[base + 32 : base + 40, :] = tail


def gather_rows(me, recv):
    return pl.pallas_call(
        gather_kernel,
        in_specs=[pl.BlockSpec(memory_space=SMEM), pl.BlockSpec(memory_space=VMEM)],
        out_shape=[
            jax.ShapeDtypeStruct((NDEV * SLOTS2, TILE), F32),
            jax.ShapeDtypeStruct((NDEV, TILE), jnp.int32),
        ],
        scratch_shapes=[VMEM((TILE, TILE), F32)],
        compiler_params=pltpu.CompilerParams(vmem_limit_bytes=16 * 1024 * 1024),
        name="gather_rows",
    )(me, recv)


def pieces(x):
    high = x.astype(BF16).astype(F32)
    rest = x - high
    mid = rest.astype(BF16).astype(F32)
    return high, mid, rest - mid


def factor128(rows):
    lane = lax.broadcasted_iota(jnp.int32, (8, TILE), 1)
    sub = lax.broadcasted_iota(jnp.int32, (8, TILE), 0)
    block = list(rows)
    inv = [jnp.where(lane == sub + 8 * v, 1.0, 0.0) for v in range(16)]
    upper, inverse = [], []

    def row(x, i):
        return jnp.broadcast_to(x[i : i + 1, :], (8, TILE))

    def col(x, i):
        return jnp.broadcast_to(x[:, i : i + 1], (8, TILE))

    for t in range(16):
        cols = [col(block[t], 8 * t + k) for k in range(8)]
        left, right = block[t], inv[t]
        up = jnp.zeros((8, TILE), F32)
        low = up
        for j in range(0, 8, 2):
            one, two = sub == j, sub == j + 1
            both = one | two
            x, y = cols[j], cols[j + 1]
            p, b, q = row(x, j), row(x, j + 1), row(y, j + 1)
            det = p * q - b * b
            over = 1.0 / det
            n1 = jnp.where(one, -q, jnp.where(two, b, x * q - y * b))
            n2 = jnp.where(one, b, jnp.where(two, -p, y * p - x * b))
            for k in range(j + 2, 8):
                change = (n1 * row(cols[k], j) + n2 * row(cols[k], j + 1)) * over
                cols[k] = jnp.where(both, 0.0, cols[k]) - change
            m1, m2 = n1 * over, n2 * over
            inv_p = 1.0 / p
            root_1, root_2, ratio = lax.rsqrt(p), lax.rsqrt(det * inv_p), b * inv_p
            l1, l2, r1, r2 = row(left, j), row(left, j + 1), row(right, j), row(right, j + 1)
            up = jnp.where(one, l1 * root_1, jnp.where(two, (l2 - ratio * l1) * root_2, up))
            low = jnp.where(one, r1 * root_1, jnp.where(two, (r2 - ratio * r1) * root_2, low))
            left = jnp.where(both, 0.0, left) - (m1 * l1 + m2 * l2)
            right = jnp.where(both, 0.0, right) - (m1 * r1 + m2 * r2)
        upper.append(jnp.where(lane >= sub + 8 * t, up, 0.0))
        inverse.append(low)
        if t < 15:
            parts = [col(block[t + 1], 8 * t + k) for k in range(8)]
            one = [parts[k] * row(left, k) for k in range(8)]
            two = [parts[k] * row(right, k) for k in range(8)]
            while len(one) > 1:
                one = [one[i] + one[i + 1] for i in range(0, len(one), 2)]
                two = [two[i] + two[i + 1] for i in range(0, len(two), 2)]
            block[t + 1] = block[t + 1] - one[0]
            inv[t + 1] = inv[t + 1] - two[0]
        if t < 14:
            h, m, low_part = pieces(block[t])
            mult = jnp.concatenate([h, h, m, h, low_part, m], axis=0).T.astype(BF16)
            h, m, low_part = pieces(jnp.concatenate([left, right], axis=1))
            base = jnp.concatenate([h, m, h, low_part, h, m], axis=0).astype(BF16)
            late = jnp.dot(mult, base, preferred_element_type=F32)
            for v in range(t + 2, 16):
                block[v] = block[v] - late[8 * v : 8 * v + 8, :TILE]
                inv[v] = inv[v] - late[8 * v : 8 * v + 8, TILE:]
    return upper, inverse


def at(i, n=TILE):
    return pl.ds(pl.multiple_of(i * n, n), n)


def three(x):
    high = x.astype(BF16)
    rest = x - high.astype(F32)
    mid = rest.astype(BF16)
    return high, mid, (rest - mid.astype(F32)).astype(BF16)


def stacks(x):
    h, m, low = three(x)
    return (
        jnp.concatenate([h, h], axis=1),
        jnp.concatenate([m, h], axis=1),
        jnp.concatenate([low, m], axis=1),
    )


def right_stacks(x):
    h, m, low = three(x)
    return jnp.concatenate([h, m], axis=1), jnp.concatenate([h, low], axis=1)


def six(pa, pb, pc, ra, rb):
    return nt(pa, ra) + (nt(pb, rb) + nt(pc, ra))


def unpack(pair, entries):
    lane = lax.broadcasted_iota(jnp.int32, (TILE, TILE), 1)
    sub = lax.broadcasted_iota(jnp.int32, (TILE, TILE), 0)
    low = jnp.where(lane < sub, pair, 0.0)
    high = jnp.where(lane > sub, pair, 0.0)
    one = low + low.T + jnp.where(lane == sub, pair, 0.0)
    return one, high + high.T + jnp.where(lane == sub, entries, 0.0)


def nn(a, b):
    return jnp.dot(a, b, precision=HI, preferred_element_type=F32)


def factor_kernel(
    recv_ref, lh_hbm, ll_hbm, wh_hbm, wl_hbm,
    lh_ref, ll_ref, wh_ref, wl_ref, body, inv_ref, pa, pb, pc, ra, rb, sem,
):
    lane = lax.broadcasted_iota(jnp.int32, (TILE, TILE), 1)
    sub = lax.broadcasted_iota(jnp.int32, (TILE, TILE), 0)

    def slot(i):
        return recv_ref[pl.ds(i, TILE, stride=SLOTS2), :]

    place = 0
    for k in range(LEAD):
        for i in range(k + 1, LEAD):
            body[TILE * i : TILE * (i + 1), TILE * k : TILE * (k + 1)] = slot(place)
            place += 1
    damp, entries = slot(DAMP_SLOT), slot(DIAG_SLOT)
    for u in range(4):
        one, two = unpack(slot(PAIR_SLOT + u), entries[:, 4 + u : 5 + u])
        for k, tile in ((u, one), (u + 4, two)):
            here = slice(TILE * k, TILE * (k + 1))
            body[here, here] = tile + jnp.where(lane == sub, damp[:, k : k + 1], 0.0)

    def step(k, _):
        rows = [
            body[pl.ds(pl.multiple_of(k * TILE + 8 * v, 8), 8), at(k)] for v in range(16)
        ]
        upper, inverse = factor128(rows)
        inv = jnp.concatenate(inverse, axis=0)
        inv_ref[at(k), :] = inv
        wa, wb = right_stacks(inv)

        def panel(i, _):
            x = six(*stacks(body[at(i, 512), at(k)]), wa, wb)
            index = i * 512 + lax.broadcasted_iota(jnp.int32, (512, TILE), 0)
            x = jnp.where(index >= (k + 1) * TILE, x, 0.0)
            h, m, low = three(x)
            pa[at(i, 512), :] = jnp.concatenate([h, h], axis=1)
            pb[at(i, 512), :] = jnp.concatenate([m, h], axis=1)
            pc[at(i, 512), :] = jnp.concatenate([low, m], axis=1)
            ra[at(i, 512), :] = jnp.concatenate([h, m], axis=1)
            rb[at(i, 512), :] = jnp.concatenate([h, low], axis=1)
            lh_ref[at(i, 512), at(k)] = h
            ll_ref[at(i, 512), at(k)] = m
            return 0

        begin = (k >= 3).astype(jnp.int32)

        @pl.when(k >= 3)
        def _():
            zero = jnp.zeros((512, TILE), BF16)
            lh_ref[:512, at(k)] = zero
            ll_ref[:512, at(k)] = zero

        lax.fori_loop(begin, 2, panel, 0)

        def update(j, _):
            wa, wb = ra[at(j, 256), :], rb[at(j, 256), :]

            def rows_of(i, _):
                part = at(i, 512)
                body[part, at(j, 256)] -= six(pa[part, :], pb[part, :], pc[part, :], wa, wb)
                return 0

            lax.fori_loop((j >= 2).astype(jnp.int32), 2, rows_of, 0)
            return 0

        lax.fori_loop((k + 1) // 2, 4, update, 0)
        tile = jnp.concatenate(upper, axis=0).T
        body[at(k), at(k)] = tile
        lh_ref[at(k), at(k)], ll_ref[at(k), at(k)] = split(tile)
        pltpu.make_async_copy(lh_ref.at[:, at(k)], lh_hbm.at[:, at(k)], sem.at[0]).start()
        pltpu.make_async_copy(ll_ref.at[:, at(k)], ll_hbm.at[:, at(k)], sem.at[1]).start()
        return 0

    lax.fori_loop(0, LEAD, step, 0)
    for g in range(4):
        one = slice(256 * g, 256 * g + TILE)
        two = slice(256 * g + TILE, 256 * g + 256)
        cross = lh_ref[two, one].astype(F32) + ll_ref[two, one].astype(F32)
        corner = -nn(inv_ref[two, :], nn(cross, inv_ref[one, :]))
        wh_ref[one, :TILE], wl_ref[one, :TILE] = split(inv_ref[one, :])
        zero = jnp.zeros((TILE, TILE), BF16)
        wh_ref[one, TILE:], wl_ref[one, TILE:] = zero, zero
        wh_ref[two, :TILE], wl_ref[two, :TILE] = split(corner)
        wh_ref[two, TILE:], wl_ref[two, TILE:] = split(inv_ref[two, :])
    last = [
        pltpu.make_async_copy(wh_ref, wh_hbm, sem.at[2]),
        pltpu.make_async_copy(wl_ref, wl_hbm, sem.at[3]),
    ]
    for copy in last:
        copy.start()
    pltpu.make_async_copy(lh_ref, lh_hbm, sem.at[0]).wait()
    pltpu.make_async_copy(ll_ref, ll_hbm, sem.at[1]).wait()
    for copy in last:
        copy.wait()


def factorise(recv):
    return pl.pallas_call(
        factor_kernel,
        in_specs=[pl.BlockSpec(memory_space=VMEM)],
        out_specs=[pl.BlockSpec(memory_space=pltpu.HBM)] * 4,
        out_shape=[
            jax.ShapeDtypeStruct((1024, 1024), BF16),
            jax.ShapeDtypeStruct((1024, 1024), BF16),
            jax.ShapeDtypeStruct((1024, 256), BF16),
            jax.ShapeDtypeStruct((1024, 256), BF16),
        ],
        scratch_shapes=[VMEM((1024, 1024), BF16)] * 2
        + [VMEM((1024, 256), BF16)] * 2
        + [VMEM((1024, 1024), F32), VMEM((1024, TILE), F32)]
        + [VMEM((1024, 256), BF16)] * 5
        + [pltpu.SemaphoreType.DMA((4,))],
        compiler_params=pltpu.CompilerParams(vmem_limit_bytes=58 * 1024 * 1024),
        cost_estimate=pl.CostEstimate(
            flops=40_000_000_000, bytes_accessed=8_000_000, transcendentals=0
        ),
        name="factorise",
    )(recv)


def schur_kernel(
    scal_ref, damp_ref, lh_hbm, ll_hbm, wh_hbm, wl_hbm, col_hbm, cross_hbm, recv_hbm,
    factor_hbm, out_hbm,
    lh_ref, ll_ref, wh_ref, wl_ref, col_ref, cross_ref, diag_ref, out_ref, rows, cols,
    xh, xl, yh, yl, bh, bl, none_ref, where_ref, row_tiles, col_tiles, used_ref,
    load_sem, factor_sem, out_sem,
):
    row = scal_ref[192]
    column = scal_ref[193]
    loads = [
        pltpu.make_async_copy(source, target, load_sem.at[i])
        for i, (source, target) in enumerate(
            [
                (cross_hbm, cross_ref),
                (col_hbm, col_ref),
                (recv_hbm.at[:, DAMP_SLOT:SLOTS2], diag_ref),
                (lh_hbm, lh_ref),
                (ll_hbm, ll_ref),
                (wh_hbm, wh_ref),
                (wl_hbm, wl_ref),
            ]
        )
    ]
    for copy in loads:
        copy.start()
    none_ref[...] = jnp.zeros_like(none_ref)
    for u in range(24):
        where_ref[u] = 0
    for u in range(64):
        used_ref[u] = 0

    def mark_row(p, _):
        a = scal_ref[2 * p] - LEAD * row
        where_ref[a] = jnp.where(scal_ref[2 * p + 1] < LEAD, 1, where_ref[a])
        return 0

    def mark_col(p, _):
        tile = scal_ref[64 + 2 * p]
        a = tile - 16 * column + LEAD
        b = scal_ref[65 + 2 * p]

        @pl.when((b < LEAD) & (tile >= LEAD) & (tile <= LEAD * row + 7))
        def _():
            where_ref[a] = 1
            used_ref[4 * (a - LEAD) + b // 2] = 1

        return 0

    @pl.when(row >= 1)
    def _():
        lax.fori_loop(0, 32, mark_row, 0)
        lax.fori_loop(0, 64, mark_col, 0)

    def place_row(u, count):
        used = where_ref[u] == 1
        where_ref[u] = jnp.where(used, count, -1)
        row_tiles[count] = u
        return count + used.astype(jnp.int32)

    def place_col(u, count):
        used = where_ref[u + LEAD] == 1
        where_ref[u + LEAD] = jnp.where(used, count, -1)
        col_tiles[count] = u
        return count + used.astype(jnp.int32)

    n_row = lax.fori_loop(0, LEAD, place_row, jnp.int32(0))
    n_col = lax.fori_loop(0, 16, place_col, jnp.int32(0))

    def blank(i, _):
        out_ref[at(i, 32), :] = jnp.zeros((32, 2048), F32)
        return 0

    lax.fori_loop(0, 32, blank, 0)

    def clear(i, _):
        rows[at(i), :] = jnp.zeros((TILE, 1024), F32)
        return 0

    lax.fori_loop(0, n_row, clear, 0)

    def clear_cols(i, _):
        cols[at(i), :] = jnp.zeros((TILE, 1024), F32)
        return 0

    lax.fori_loop(0, n_col, clear_cols, 0)
    loads[0].wait()

    def fill_row(p, _):
        a = scal_ref[2 * p] - LEAD * row
        b = scal_ref[2 * p + 1]
        here = b - 16 * column

        @pl.when((b < LEAD) & (where_ref[a] >= 0))
        def _():
            rows[at(where_ref[a]), at(b)] += cross_ref[at(p), :]

        @pl.when((b >= LEAD) & (here >= 0) & (here < 16))
        def _():
            out_ref[at(a), at(here)] += cross_ref[at(p), :]

        return 0

    def fill_col(p, _):
        a = scal_ref[64 + 2 * p] - 16 * column + LEAD
        b = scal_ref[65 + 2 * p]

        @pl.when((b < LEAD) & (where_ref[a] >= 0))
        def _():
            cols[at(where_ref[a]), at(b)] += col_ref[at(p), :]

        return 0

    lax.fori_loop(0, 32, fill_row, 0)
    loads[1].wait()
    lax.fori_loop(0, 64, fill_col, 0)
    loads[2].wait()

    @pl.when((row >= 1) & (row // 2 == column))
    def _():
        lane = lax.broadcasted_iota(jnp.int32, (TILE, TILE), 1)
        sub = lax.broadcasted_iota(jnp.int32, (TILE, TILE), 0)
        entries = diag_ref[:, DIAG_SLOT - DAMP_SLOT, :]
        for u in range(4):
            mine = jnp.where(lane == LEAD * row + 4 + u, entries, 0.0)
            pair = diag_ref[:, OWN_SLOT - DAMP_SLOT + u, :]
            one, two = unpack(pair, jnp.sum(mine, axis=1, keepdims=True))
            for s, tile in ((u, one), (u + 4, two)):
                damp = damp_ref[TILE * s : TILE * (s + 1)].reshape(1, TILE)
                damp = jnp.where(lane == sub, jnp.broadcast_to(damp, (TILE, TILE)), 0.0)
                out_ref[TILE * s : TILE * (s + 1), at(LEAD * (row % 2) + s)] += tile + damp

    for copy in loads[3:]:
        copy.wait()

    chunks = (n_row + 1) // 2
    for g in range(4):
        here = slice(256 * g, 256 * (g + 1))

        def forward(i, _, g=g, here=here):
            part = at(i, 256)
            rest = rows[part, here]
            if g:
                rest = rest - nt3(
                    xh[part, : 256 * g],
                    xl[part, : 256 * g],
                    lh_ref[here, : 256 * g],
                    ll_ref[here, : 256 * g],
                )
            x = nt3(*split(rest), wh_ref[here, :], wl_ref[here, :])
            rows[part, here] = x
            xh[part, here], xl[part, here] = split(x)
            return 0

        lax.fori_loop(0, chunks, forward, 0)

    for s in range(LEAD):
        part = slice(TILE * s, TILE * (s + 1))

        @pl.when(row == 0)
        def _(part=part):
            rows[part, :] = lh_ref[part, :].astype(F32) + ll_ref[part, :].astype(F32)
            pltpu.make_async_copy(rows.at[part], factor_hbm.at[part], factor_sem.at[0]).start()

        @pl.when((row >= 1) & (where_ref[s] >= 0))
        def _(s=s, part=part):
            pltpu.make_async_copy(
                rows.at[at(where_ref[s])], factor_hbm.at[part], factor_sem.at[0]
            ).start()

        @pl.when((row >= 1) & (where_ref[s] < 0))
        def _(part=part):
            pltpu.make_async_copy(none_ref, factor_hbm.at[part], factor_sem.at[0]).start()

    for g in reversed(range(4)):
        here = slice(256 * g, 256 * (g + 1))

        def backward(i, _, g=g, here=here):
            part = at(i, 256)
            rest = rows[part, here]
            if g < 3:
                past = slice(256 * (g + 1), 1024)
                rest = rest - nn3(
                    yh[part, past], yl[part, past], lh_ref[past, here], ll_ref[past, here]
                )
            yh[part, here], yl[part, here] = split(
                nn3(*split(rest), wh_ref[here, :], wl_ref[here, :])
            )
            return 0

        lax.fori_loop(0, chunks, backward, 0)

    def send(c):
        part = at(c)
        pltpu.make_async_copy(out_ref.at[:, part], out_hbm.at[:, part], out_sem.at[0]).start()

    def columns(j, sent):
        one_tile = col_tiles[2 * j]
        two_tile = col_tiles[jnp.minimum(2 * j + 1, n_col - 1)]

        def apply(i, prod):
            for p in range(2):
                for q in range(2):
                    it = 2 * i + p
                    a = row_tiles[it]
                    b = two_tile if q else one_tile
                    keep = (it < n_row) & (LEAD * row + a >= 16 * column + b)
                    if q:
                        keep = keep & (2 * j + 1 < n_col)

                    @pl.when(keep)
                    def _(a=a, b=b, p=p, q=q):
                        out_ref[at(a), at(b)] -= prod[
                            TILE * p : TILE * (p + 1), TILE * q : TILE * (q + 1)
                        ]

        def used(c):
            return used_ref[4 * one_tile + c] | used_ref[4 * two_tile + c]

        filled = used(0) + used(1) + used(2) + used(3)

        @pl.when(filled > 1)
        def _():
            def prepare(c, _):
                bh[:, at(c, 256)], bl[:, at(c, 256)] = split(cols[at(j, 256), at(c, 256)])
                return 0

            lax.fori_loop(0, 4, prepare, 0)

            def blocks(i, _):
                left = at(i, 256)
                apply(i, nt3(yh[left, :], yl[left, :], bh[...], bl[...]))
                return 0

            lax.fori_loop(0, chunks, blocks, 0)

        def chunk(c, _):
            @pl.when((filled == 1) & (used(c) == 1))
            def _():
                bh[:, :256], bl[:, :256] = split(cols[at(j, 256), at(c, 256)])

                def blocks(i, _):
                    left = (at(i, 256), at(c, 256))
                    apply(i, nt3(yh[left], yl[left], bh[:, :256], bl[:, :256]))
                    return 0

                lax.fori_loop(0, chunks, blocks, 0)

            return 0

        lax.fori_loop(0, 4, chunk, 0)
        done = two_tile + 1

        def one(c, _):
            send(c)
            return 0

        lax.fori_loop(sent, done, one, 0)
        return done

    sent = lax.fori_loop(0, (n_col + 1) // 2, columns, jnp.int32(0))

    def last(c, _):
        send(c)
        return 0

    lax.fori_loop(sent, 16, last, 0)
    pltpu.make_async_copy(rows, factor_hbm, factor_sem.at[0]).wait()
    pltpu.make_async_copy(out_ref, out_hbm, out_sem.at[0]).wait()


def schur(scal, lh, ll, wh, wl, col_cross, cross, recv, damp):
    return pl.pallas_call(
        schur_kernel,
        in_specs=[pl.BlockSpec(memory_space=SMEM), pl.BlockSpec(memory_space=VMEM)]
        + [pl.BlockSpec(memory_space=pltpu.HBM)] * 7,
        out_specs=[pl.BlockSpec(memory_space=pl.ANY)] * 2,
        out_shape=[
            jax.ShapeDtypeStruct((1024, 1024), F32),
            jax.ShapeDtypeStruct((1024, 2048), F32),
        ],
        scratch_shapes=[
            VMEM((1024, 1024), BF16),
            VMEM((1024, 1024), BF16),
            VMEM((1024, 256), BF16),
            VMEM((1024, 256), BF16),
            VMEM((64 * TILE, TILE), F32),
            VMEM((32 * TILE, TILE), F32),
            VMEM((NDEV, LEAD, TILE), F32),
            VMEM((1024, 2048), F32),
            VMEM((1024, 1024), F32),
            VMEM((2048, 1024), F32),
            VMEM((1024, 1024), BF16),
            VMEM((1024, 1024), BF16),
            VMEM((1024, 1024), BF16),
            VMEM((1024, 1024), BF16),
            VMEM((256, 1024), BF16),
            VMEM((256, 1024), BF16),
            VMEM((TILE, 1024), F32),
            SMEM((24,), jnp.int32),
            SMEM((9,), jnp.int32),
            SMEM((17,), jnp.int32),
            SMEM((64,), jnp.int32),
            pltpu.SemaphoreType.DMA((7,)),
            pltpu.SemaphoreType.DMA((1,)),
            pltpu.SemaphoreType.DMA((1,)),
        ],
        compiler_params=pltpu.CompilerParams(vmem_limit_bytes=60 * 1024 * 1024),
        cost_estimate=pl.CostEstimate(
            flops=20_000_000_000, bytes_accessed=30_000_000, transcendentals=0
        ),
        name="schur",
    )(scal, damp, lh, ll, wh, wl, col_cross, cross, recv)


def local(pair_list, jacobian, damping):
    row = lax.axis_index("row")
    column = lax.axis_index("col")
    payload, cross = grams(jacobian, pair_list.T, damping)
    recv = lax.all_to_all(payload.reshape(NDEV, SLOTS1, TILE), BOTH, 0, 0, tiled=True)
    cross = cross.reshape(4 * TILE, TILE)
    moves = [
        (r * NCOL + c, (NCOL * (r % 2) + c) * NCOL + r // 2) for r in range(NROW) for c in range(NCOL)
    ]
    moved = lax.ppermute(cross, BOTH, moves)
    row_cross = lax.all_gather(cross, "col", axis=0, tiled=True)
    me = (row * NCOL + column).astype(jnp.int32).reshape(1)
    payload, index = gather_rows(me, recv.reshape(NDEV * SLOTS1, TILE))
    recv = lax.all_to_all(payload.reshape(NDEV, SLOTS2, TILE), BOTH, 0, 0, tiled=True)
    recv, moved = lax.optimization_barrier((recv, moved))
    col_cross = lax.all_gather(moved, "row", axis=0, tiled=True)
    lh, ll, wh, wl = factorise(recv.reshape(NDEV * SLOTS2, TILE))

    index = index[:, :8].reshape(NDEV * 8)
    scal = jnp.concatenate(
        [
            lax.dynamic_slice(index, (row * 64,), (64,)),
            lax.dynamic_slice(index, (column * 128,), (128,)),
            jnp.stack([row, column]).astype(jnp.int32),
        ]
    )
    return tuple(schur(scal, lh, ll, wh, wl, col_cross, row_cross, recv, damping))


def solution(mesh):
    placed = (P(("row", "col"), None), P(("row", "col"), None, None), P("row"))
    return jax.shard_map(
        local,
        mesh=mesh,
        in_specs=placed,
        out_specs=(P("row", None), P("row", "col")),
        check_vma=False,
    )
```

```python
import jax
import jax.numpy as jnp
from jax import lax
from jax.experimental import pallas as pl
from jax.experimental.pallas import tpu as pltpu
from jax.sharding import PartitionSpec as P

F32 = jnp.float32
BF16 = jnp.bfloat16
HI = lax.Precision.HIGHEST
BOTH = ("row", "col")
NROW, NCOL = 16, 8
NDEV = NROW * NCOL
TILE = 128
LEAD = 8
SLOTS1 = 16
SLOTS2 = 40
PAIR_SLOT = 28
DAMP_SLOT = 32
DIAG_SLOT = 33
OWN_SLOT = 36
VMEM = pltpu.VMEM
SMEM = pltpu.SMEM


def nt(a, b, precision=None):
    return lax.dot_general(
        a, b, (((1,), (1,)), ((), ())), precision=precision, preferred_element_type=F32
    )


def tn(a, b, precision=None):
    return lax.dot_general(
        a, b, (((0,), (0,)), ((), ())), precision=precision, preferred_element_type=F32
    )


def split(x):
    high = x.astype(BF16)
    return high, (x - high.astype(F32)).astype(BF16)


def nt3(ah, al, bh, bl):
    return nt(ah, bh) + (nt(ah, bl) + nt(al, bh))


def nn3(ah, al, bh, bl):
    def nn(a, b):
        return jnp.dot(a, b, preferred_element_type=F32)

    return nn(ah, bh) + (nn(ah, bl) + nn(al, bh))


def below_tile(a, b):
    return b * (LEAD - 1) - (b * (b - 1)) // 2 + (a - b - 1)


def gram_kernel(jac_ref, idx_ref, damp_ref, pay_ref, cross_ref):
    q = pl.program_id(0)
    high, low = split(jac_ref[0])
    mixed = tn(high, low)
    gram = tn(high, high) + (mixed + mixed.T)
    pay_ref[pl.ds(q, TILE, stride=SLOTS1), :] = gram[:TILE, :TILE]
    pay_ref[pl.ds(q + 4, TILE, stride=SLOTS1), :] = gram[TILE:, TILE:]
    pay_ref[pl.ds(q + 8, TILE, stride=SLOTS1), :] = gram[:TILE, TILE:]
    cross_ref[0] = gram[:TILE, TILE:]

    @pl.when(q == 0)
    def _():
        lane = lax.broadcasted_iota(jnp.int32, (TILE, TILE), 1)
        index = jnp.zeros((TILE, TILE), F32)
        for e in range(8):
            index = jnp.where(lane == e, idx_ref[e % 2, e // 2].astype(F32), index)
        pay_ref[pl.ds(12, TILE, stride=SLOTS1), :] = index
        rows = [damp_ref[TILE * b : TILE * (b + 1)].reshape(1, TILE) for b in range(LEAD)]
        wide = jnp.concatenate(rows + [jnp.zeros((TILE - 8, TILE), F32)], axis=0)
        pay_ref[pl.ds(13, TILE, stride=SLOTS1), :] = wide.T
        zero = jnp.zeros((TILE, TILE), F32)
        pay_ref[pl.ds(14, TILE, stride=SLOTS1), :] = zero
        pay_ref[pl.ds(15, TILE, stride=SLOTS1), :] = zero


def grams(jacobian, idx, damp):
    return pl.pallas_call(
        gram_kernel,
        grid=(4,),
        in_specs=[
            pl.BlockSpec((1, 1024, 256), lambda q: (q, 0, 0)),
            pl.BlockSpec(memory_space=SMEM),
            pl.BlockSpec((1024,), lambda q: (0,)),
        ],
        out_specs=[
            pl.BlockSpec((TILE * SLOTS1, TILE), lambda q: (0, 0)),
            pl.BlockSpec((1, TILE, TILE), lambda q: (q, 0, 0)),
        ],
        out_shape=[
            jax.ShapeDtypeStruct((TILE * SLOTS1, TILE), F32),
            jax.ShapeDtypeStruct((4, TILE, TILE), F32),
        ],
        name="grams",
    )(jacobian, idx, damp)


def gather_kernel(me_ref, recv_ref, pay_ref, idx_ref, flip_ref):
    me = me_ref[0]
    lane = lax.broadcasted_iota(jnp.int32, (TILE, TILE), 1)
    sub = lax.broadcasted_iota(jnp.int32, (TILE, TILE), 0)
    index = recv_ref[pl.ds(12, NDEV, stride=SLOTS1), :]
    idx_ref[...] = index.astype(jnp.int32)
    across = index.T.astype(jnp.int32)
    diag = jnp.zeros((TILE, TILE), F32)
    lead = jnp.zeros((32, TILE), F32)
    sub32 = lax.broadcasted_iota(jnp.int32, (32, TILE), 0)
    lane32 = lax.broadcasted_iota(jnp.int32, (32, TILE), 1)
    for q in range(4):
        a = across[2 * q : 2 * q + 1, :]
        b = across[2 * q + 1 : 2 * q + 2, :]
        first = recv_ref[pl.ds(q, NDEV, stride=SLOTS1), :]
        second = recv_ref[pl.ds(q + 4, NDEV, stride=SLOTS1), :]
        cross = recv_ref[pl.ds(q + 8, NDEV, stride=SLOTS1), :]
        diag = diag + jnp.dot((sub == a).astype(F32), first, precision=HI)
        diag = diag + jnp.dot((sub == b).astype(F32), second, precision=HI)
        hit = (sub32 == below_tile(a, b)) & (lane32 < NCOL)
        lead = lead + jnp.dot(hit.astype(F32), cross, precision=HI)
    packed = jnp.where(lane <= me, pltpu.roll(diag, 4, 0), diag)
    flip_ref[...] = diag.T
    entries = jnp.broadcast_to(flip_ref[pl.ds(me, 1), :], (8, TILE))
    damp = jnp.broadcast_to(recv_ref[13:14, :], (8, TILE))
    sub8 = lax.broadcasted_iota(jnp.int32, (8, TILE), 0)
    head = jnp.where(sub8 == 0, damp, jnp.where(sub8 == 1, entries, 0.0))
    last = jnp.where(sub8 >= 4, packed[:8, :], lead[24:, :])
    for r in range(NROW):
        tail = jnp.where(sub8 >= 4, packed[8 * r : 8 * r + 8, :], head)
        for c in range(NCOL):
            base = (r * NCOL + c) * SLOTS2
            pay_ref[base : base + 24, :] = lead[:24, :]
            pay_ref[base + 24 : base + 32, :] = last
            pay_ref[base + 32 : base + 40, :] = tail


def gather_rows(me, recv):
    return pl.pallas_call(
        gather_kernel,
        in_specs=[pl.BlockSpec(memory_space=SMEM), pl.BlockSpec(memory_space=VMEM)],
        out_shape=[
            jax.ShapeDtypeStruct((NDEV * SLOTS2, TILE), F32),
            jax.ShapeDtypeStruct((NDEV, TILE), jnp.int32),
        ],
        scratch_shapes=[VMEM((TILE, TILE), F32)],
        compiler_params=pltpu.CompilerParams(vmem_limit_bytes=16 * 1024 * 1024),
        name="gather_rows",
    )(me, recv)


def pieces(x):
    high = x.astype(BF16).astype(F32)
    rest = x - high
    mid = rest.astype(BF16).astype(F32)
    return high, mid, rest - mid


def factor128(rows):
    lane = lax.broadcasted_iota(jnp.int32, (8, TILE), 1)
    sub = lax.broadcasted_iota(jnp.int32, (8, TILE), 0)
    block = list(rows)
    inv = [jnp.where(lane == sub + 8 * v, 1.0, 0.0) for v in range(16)]
    upper, inverse = [], []

    def row(x, i):
        return jnp.broadcast_to(x[i : i + 1, :], (8, TILE))

    def col(x, i):
        return jnp.broadcast_to(x[:, i : i + 1], (8, TILE))

    for t in range(16):
        cols = [col(block[t], 8 * t + k) for k in range(8)]
        left, right = block[t], inv[t]
        up = jnp.zeros((8, TILE), F32)
        low = up
        for j in range(0, 8, 2):
            one, two = sub == j, sub == j + 1
            both = one | two
            x, y = cols[j], cols[j + 1]
            p, b, q = row(x, j), row(x, j + 1), row(y, j + 1)
            det = p * q - b * b
            over = 1.0 / det
            n1 = jnp.where(one, -q, jnp.where(two, b, x * q - y * b))
            n2 = jnp.where(one, b, jnp.where(two, -p, y * p - x * b))
            for k in range(j + 2, 8):
                change = (n1 * row(cols[k], j) + n2 * row(cols[k], j + 1)) * over
                cols[k] = jnp.where(both, 0.0, cols[k]) - change
            m1, m2 = n1 * over, n2 * over
            inv_p = 1.0 / p
            root_1, root_2, ratio = lax.rsqrt(p), lax.rsqrt(det * inv_p), b * inv_p
            l1, l2, r1, r2 = row(left, j), row(left, j + 1), row(right, j), row(right, j + 1)
            up = jnp.where(one, l1 * root_1, jnp.where(two, (l2 - ratio * l1) * root_2, up))
            low = jnp.where(one, r1 * root_1, jnp.where(two, (r2 - ratio * r1) * root_2, low))
            left = jnp.where(both, 0.0, left) - (m1 * l1 + m2 * l2)
            right = jnp.where(both, 0.0, right) - (m1 * r1 + m2 * r2)
        upper.append(jnp.where(lane >= sub + 8 * t, up, 0.0))
        inverse.append(low)
        if t < 15:
            parts = [col(block[t + 1], 8 * t + k) for k in range(8)]
            one = [parts[k] * row(left, k) for k in range(8)]
            two = [parts[k] * row(right, k) for k in range(8)]
            while len(one) > 1:
                one = [one[i] + one[i + 1] for i in range(0, len(one), 2)]
                two = [two[i] + two[i + 1] for i in range(0, len(two), 2)]
            block[t + 1] = block[t + 1] - one[0]
            inv[t + 1] = inv[t + 1] - two[0]
        if t < 14:
            h, m, low_part = pieces(block[t])
            mult = jnp.concatenate([h, h, m, h, low_part, m], axis=0).T.astype(BF16)
            h, m, low_part = pieces(jnp.concatenate([left, right], axis=1))
            base = jnp.concatenate([h, m, h, low_part, h, m], axis=0).astype(BF16)
            late = jnp.dot(mult, base, preferred_element_type=F32)
            for v in range(t + 2, 16):
                block[v] = block[v] - late[8 * v : 8 * v + 8, :TILE]
                inv[v] = inv[v] - late[8 * v : 8 * v + 8, TILE:]
    return upper, inverse


def at(i, n=TILE):
    return pl.ds(pl.multiple_of(i * n, n), n)


def three(x):
    high = x.astype(BF16)
    rest = x - high.astype(F32)
    mid = rest.astype(BF16)
    return high, mid, (rest - mid.astype(F32)).astype(BF16)


def stacks(x):
    h, m, low = three(x)
    return (
        jnp.concatenate([h, h], axis=1),
        jnp.concatenate([m, h], axis=1),
        jnp.concatenate([low, m], axis=1),
    )


def right_stacks(x):
    h, m, low = three(x)
    return jnp.concatenate([h, m], axis=1), jnp.concatenate([h, low], axis=1)


def six(pa, pb, pc, ra, rb):
    return nt(pa, ra) + (nt(pb, rb) + nt(pc, ra))


def unpack(pair, entries):
    lane = lax.broadcasted_iota(jnp.int32, (TILE, TILE), 1)
    sub = lax.broadcasted_iota(jnp.int32, (TILE, TILE), 0)
    low = jnp.where(lane < sub, pair, 0.0)
    high = jnp.where(lane > sub, pair, 0.0)
    one = low + low.T + jnp.where(lane == sub, pair, 0.0)
    return one, high + high.T + jnp.where(lane == sub, entries, 0.0)


def nn(a, b):
    return jnp.dot(a, b, precision=HI, preferred_element_type=F32)


def mark_rows(scal_ref, where_ref, tiles_ref):
    row = scal_ref[192]
    for u in range(LEAD):
        where_ref[u] = 0

    def mark(p, _):
        a = scal_ref[2 * p] - LEAD * row
        where_ref[a] = jnp.where(scal_ref[2 * p + 1] < LEAD, 1, where_ref[a])
        return 0

    @pl.when(row >= 1)
    def _():
        lax.fori_loop(0, 32, mark, 0)

    def place(u, count):
        used = where_ref[u] == 1
        where_ref[u] = jnp.where(used, count, -1)
        tiles_ref[count] = u
        return count + used.astype(jnp.int32)

    return lax.fori_loop(0, LEAD, place, jnp.int32(0))


def factor_kernel(
    scal_ref, recv_ref, cross_hbm, factor_hbm, yh_hbm, yl_hbm,
    lh_ref, ll_ref, wh_ref, wl_ref, body, inv_ref, pa, pb, pc, ra, rb,
    cross_ref, rows, xh, xl, yh, yl, none_ref, where_ref, tiles_ref, load_sem, factor_sem, y_sem,
):
    load = pltpu.make_async_copy(cross_hbm, cross_ref, load_sem.at[0])
    load.start()
    row = scal_ref[192]
    n_row = mark_rows(scal_ref, where_ref, tiles_ref)
    chunks = (n_row + 1) // 2
    none_ref[...] = jnp.zeros_like(none_ref)

    def clear(i, _):
        rows[at(i), :] = jnp.zeros((TILE, 1024), F32)
        return 0

    lax.fori_loop(0, n_row, clear, 0)
    lane = lax.broadcasted_iota(jnp.int32, (TILE, TILE), 1)
    sub = lax.broadcasted_iota(jnp.int32, (TILE, TILE), 0)

    def slot(i):
        return recv_ref[pl.ds(i, TILE, stride=SLOTS2), :]

    place = 0
    for k in range(LEAD):
        for i in range(k + 1, LEAD):
            body[TILE * i : TILE * (i + 1), TILE * k : TILE * (k + 1)] = slot(place)
            place += 1
    damp, entries = slot(DAMP_SLOT), slot(DIAG_SLOT)
    for u in range(4):
        one, two = unpack(slot(PAIR_SLOT + u), entries[:, 4 + u : 5 + u])
        for k, tile in ((u, one), (u + 4, two)):
            here = slice(TILE * k, TILE * (k + 1))
            body[here, here] = tile + jnp.where(lane == sub, damp[:, k : k + 1], 0.0)

    load.wait()

    def fill(p, _):
        a = scal_ref[2 * p] - LEAD * row
        b = scal_ref[2 * p + 1]

        @pl.when((b < LEAD) & (where_ref[a] >= 0))
        def _():
            rows[at(where_ref[a]), at(b)] += cross_ref[at(p), :]

        return 0

    lax.fori_loop(0, 32, fill, 0)

    def step(k, _):
        groups = [
            body[pl.ds(pl.multiple_of(k * TILE + 8 * v, 8), 8), at(k)] for v in range(16)
        ]
        upper, inverse = factor128(groups)
        inv = jnp.concatenate(inverse, axis=0)
        inv_ref[at(k), :] = inv
        wa, wb = right_stacks(inv)

        def panel(i, _):
            x = six(*stacks(body[at(i, 512), at(k)]), wa, wb)
            index = i * 512 + lax.broadcasted_iota(jnp.int32, (512, TILE), 0)
            x = jnp.where(index >= (k + 1) * TILE, x, 0.0)
            h, m, low = three(x)
            pa[at(i, 512), :] = jnp.concatenate([h, h], axis=1)
            pb[at(i, 512), :] = jnp.concatenate([m, h], axis=1)
            pc[at(i, 512), :] = jnp.concatenate([low, m], axis=1)
            ra[at(i, 512), :] = jnp.concatenate([h, m], axis=1)
            rb[at(i, 512), :] = jnp.concatenate([h, low], axis=1)
            lh_ref[at(i, 512), at(k)] = h
            ll_ref[at(i, 512), at(k)] = m
            return 0

        begin = (k >= 3).astype(jnp.int32)

        @pl.when(k >= 3)
        def _():
            zero = jnp.zeros((512, TILE), BF16)
            lh_ref[:512, at(k)] = zero
            ll_ref[:512, at(k)] = zero

        lax.fori_loop(begin, 2, panel, 0)

        def update(j, _):
            wa, wb = ra[at(j, 256), :], rb[at(j, 256), :]

            def rows_of(i, _):
                part = at(i, 512)
                body[part, at(j, 256)] -= six(pa[part, :], pb[part, :], pc[part, :], wa, wb)
                return 0

            lax.fori_loop((j >= 2).astype(jnp.int32), 2, rows_of, 0)
            return 0

        lax.fori_loop((k + 1) // 2, 4, update, 0)
        tile = jnp.concatenate(upper, axis=0).T
        body[at(k), at(k)] = tile
        lh_ref[at(k), at(k)], ll_ref[at(k), at(k)] = split(tile)
        return 0

    lax.fori_loop(0, LEAD, step, 0)
    for g in range(4):
        one = slice(256 * g, 256 * g + TILE)
        two = slice(256 * g + TILE, 256 * g + 256)
        cross = lh_ref[two, one].astype(F32) + ll_ref[two, one].astype(F32)
        corner = -nn(inv_ref[two, :], nn(cross, inv_ref[one, :]))
        wh_ref[one, :TILE], wl_ref[one, :TILE] = split(inv_ref[one, :])
        zero = jnp.zeros((TILE, TILE), BF16)
        wh_ref[one, TILE:], wl_ref[one, TILE:] = zero, zero
        wh_ref[two, :TILE], wl_ref[two, :TILE] = split(corner)
        wh_ref[two, TILE:], wl_ref[two, TILE:] = split(inv_ref[two, :])
    for g in range(4):
        here = slice(256 * g, 256 * (g + 1))

        def forward(i, _, g=g, here=here):
            part = at(i, 256)
            rest = rows[part, here]
            if g:
                rest = rest - nt3(
                    xh[part, : 256 * g],
                    xl[part, : 256 * g],
                    lh_ref[here, : 256 * g],
                    ll_ref[here, : 256 * g],
                )
            x = nt3(*split(rest), wh_ref[here, :], wl_ref[here, :])
            rows[part, here] = x
            xh[part, here], xl[part, here] = split(x)
            return 0

        lax.fori_loop(0, chunks, forward, 0)

    for s in range(LEAD):
        part = slice(TILE * s, TILE * (s + 1))

        @pl.when(row == 0)
        def _(part=part):
            rows[part, :] = lh_ref[part, :].astype(F32) + ll_ref[part, :].astype(F32)
            pltpu.make_async_copy(rows.at[part], factor_hbm.at[part], factor_sem.at[0]).start()

        @pl.when((row >= 1) & (where_ref[s] >= 0))
        def _(s=s, part=part):
            pltpu.make_async_copy(
                rows.at[at(where_ref[s])], factor_hbm.at[part], factor_sem.at[0]
            ).start()

        @pl.when((row >= 1) & (where_ref[s] < 0))
        def _(part=part):
            pltpu.make_async_copy(none_ref, factor_hbm.at[part], factor_sem.at[0]).start()

    for g in reversed(range(4)):
        here = slice(256 * g, 256 * (g + 1))

        def backward(i, _, g=g, here=here):
            part = at(i, 256)
            rest = rows[part, here]
            if g < 3:
                past = slice(256 * (g + 1), 1024)
                rest = rest - nn3(
                    yh[part, past], yl[part, past], lh_ref[past, here], ll_ref[past, here]
                )
            yh[part, here], yl[part, here] = split(
                nn3(*split(rest), wh_ref[here, :], wl_ref[here, :])
            )
            if g == 0:
                pltpu.make_async_copy(yh.at[part], yh_hbm.at[part], y_sem.at[0]).start()
                pltpu.make_async_copy(yl.at[part], yl_hbm.at[part], y_sem.at[1]).start()
            return 0

        lax.fori_loop(0, chunks, backward, 0)

    def sent(i, _):
        part = at(i, 256)
        pltpu.make_async_copy(yh.at[part], yh_hbm.at[part], y_sem.at[0]).wait()
        pltpu.make_async_copy(yl.at[part], yl_hbm.at[part], y_sem.at[1]).wait()
        return 0

    lax.fori_loop(0, chunks, sent, 0)
    pltpu.make_async_copy(rows, factor_hbm, factor_sem.at[0]).wait()


def factorise(scal, recv, cross):
    return pl.pallas_call(
        factor_kernel,
        in_specs=[
            pl.BlockSpec(memory_space=SMEM),
            pl.BlockSpec(memory_space=VMEM),
            pl.BlockSpec(memory_space=pltpu.HBM),
        ],
        out_specs=[pl.BlockSpec(memory_space=pltpu.HBM)] * 3,
        out_shape=[
            jax.ShapeDtypeStruct((1024, 1024), F32),
            jax.ShapeDtypeStruct((1024, 1024), BF16),
            jax.ShapeDtypeStruct((1024, 1024), BF16),
        ],
        scratch_shapes=[VMEM((1024, 1024), BF16)] * 2
        + [VMEM((1024, 256), BF16)] * 2
        + [VMEM((1024, 1024), F32), VMEM((1024, TILE), F32)]
        + [VMEM((1024, 256), BF16)] * 5
        + [VMEM((32 * TILE, TILE), F32), VMEM((1024, 1024), F32)]
        + [VMEM((1024, 1024), BF16)] * 4
        + [
            VMEM((TILE, 1024), F32),
            SMEM((LEAD,), jnp.int32),
            SMEM((LEAD + 1,), jnp.int32),
            pltpu.SemaphoreType.DMA((1,)),
            pltpu.SemaphoreType.DMA((1,)),
            pltpu.SemaphoreType.DMA((2,)),
        ],
        compiler_params=pltpu.CompilerParams(vmem_limit_bytes=59 * 1024 * 1024),
        cost_estimate=pl.CostEstimate(
            flops=40_000_000_000, bytes_accessed=8_000_000, transcendentals=0
        ),
        name="factorise",
    )(scal, recv, cross)


def schur_kernel(
    scal_ref, damp_ref, yh_hbm, yl_hbm, col_hbm, cross_hbm, recv_hbm, out_hbm,
    yh, yl, col_ref, cross_ref, diag_ref, out_ref, cols, bh, bl,
    row_where, row_tiles, where_ref, col_tiles, used_ref, load_sem, out_sem,
):
    row = scal_ref[192]
    column = scal_ref[193]
    loads = [
        pltpu.make_async_copy(source, target, load_sem.at[i])
        for i, (source, target) in enumerate(
            [
                (cross_hbm, cross_ref),
                (col_hbm, col_ref),
                (recv_hbm.at[:, DAMP_SLOT:SLOTS2], diag_ref),
                (yh_hbm, yh),
                (yl_hbm, yl),
            ]
        )
    ]
    for copy in loads:
        copy.start()
    for u in range(16):
        where_ref[u] = 0
    for u in range(64):
        used_ref[u] = 0

    def mark_col(p, _):
        tile = scal_ref[64 + 2 * p]
        a = tile - 16 * column
        b = scal_ref[65 + 2 * p]

        @pl.when((b < LEAD) & (tile >= LEAD) & (tile <= LEAD * row + 7))
        def _():
            where_ref[a] = 1
            used_ref[4 * a + b // 2] = 1

        return 0

    @pl.when(row >= 1)
    def _():
        lax.fori_loop(0, 64, mark_col, 0)

    def place_col(u, count):
        used = where_ref[u] == 1
        where_ref[u] = jnp.where(used, count, -1)
        col_tiles[count] = u
        return count + used.astype(jnp.int32)

    n_row = mark_rows(scal_ref, row_where, row_tiles)
    chunks = (n_row + 1) // 2
    n_col = lax.fori_loop(0, 16, place_col, jnp.int32(0))

    def blank(i, _):
        out_ref[at(i, 32), :] = jnp.zeros((32, 2048), F32)
        return 0

    lax.fori_loop(0, 32, blank, 0)

    def clear_cols(i, _):
        cols[at(i), :] = jnp.zeros((TILE, 1024), F32)
        return 0

    lax.fori_loop(0, n_col, clear_cols, 0)
    loads[0].wait()

    def fill_row(p, _):
        a = scal_ref[2 * p] - LEAD * row
        b = scal_ref[2 * p + 1]
        here = b - 16 * column

        @pl.when((b >= LEAD) & (here >= 0) & (here < 16))
        def _():
            out_ref[at(a), at(here)] += cross_ref[at(p), :]

        return 0

    def fill_col(p, _):
        a = scal_ref[64 + 2 * p] - 16 * column
        b = scal_ref[65 + 2 * p]

        @pl.when((b < LEAD) & (where_ref[a] >= 0))
        def _():
            cols[at(where_ref[a]), at(b)] += col_ref[at(p), :]

        return 0

    lax.fori_loop(0, 32, fill_row, 0)
    loads[1].wait()
    lax.fori_loop(0, 64, fill_col, 0)
    loads[2].wait()

    @pl.when((row >= 1) & (row // 2 == column))
    def _():
        lane = lax.broadcasted_iota(jnp.int32, (TILE, TILE), 1)
        sub = lax.broadcasted_iota(jnp.int32, (TILE, TILE), 0)
        entries = diag_ref[:, DIAG_SLOT - DAMP_SLOT, :]
        for u in range(4):
            mine = jnp.where(lane == LEAD * row + 4 + u, entries, 0.0)
            pair = diag_ref[:, OWN_SLOT - DAMP_SLOT + u, :]
            one, two = unpack(pair, jnp.sum(mine, axis=1, keepdims=True))
            for s, tile in ((u, one), (u + 4, two)):
                damp = damp_ref[TILE * s : TILE * (s + 1)].reshape(1, TILE)
                damp = jnp.where(lane == sub, jnp.broadcast_to(damp, (TILE, TILE)), 0.0)
                out_ref[TILE * s : TILE * (s + 1), at(LEAD * (row % 2) + s)] += tile + damp

    for copy in loads[3:]:
        copy.wait()

    def send(c):
        part = at(c)
        pltpu.make_async_copy(out_ref.at[:, part], out_hbm.at[:, part], out_sem.at[0]).start()

    def columns(j, sent):
        one_tile = col_tiles[2 * j]
        two_tile = col_tiles[jnp.minimum(2 * j + 1, n_col - 1)]

        def apply(i, prod):
            for p in range(2):
                for q in range(2):
                    it = 2 * i + p
                    a = row_tiles[it]
                    b = two_tile if q else one_tile
                    keep = (it < n_row) & (LEAD * row + a >= 16 * column + b)
                    if q:
                        keep = keep & (2 * j + 1 < n_col)

                    @pl.when(keep)
                    def _(a=a, b=b, p=p, q=q):
                        out_ref[at(a), at(b)] -= prod[
                            TILE * p : TILE * (p + 1), TILE * q : TILE * (q + 1)
                        ]

        def used(c):
            return used_ref[4 * one_tile + c] | used_ref[4 * two_tile + c]

        filled = used(0) + used(1) + used(2) + used(3)

        @pl.when(filled > 1)
        def _():
            def prepare(c, _):
                bh[:, at(c, 256)], bl[:, at(c, 256)] = split(cols[at(j, 256), at(c, 256)])
                return 0

            lax.fori_loop(0, 4, prepare, 0)

            def blocks(i, _):
                left = at(i, 256)
                apply(i, nt3(yh[left, :], yl[left, :], bh[...], bl[...]))
                return 0

            lax.fori_loop(0, chunks, blocks, 0)

        def chunk(c, _):
            @pl.when((filled == 1) & (used(c) == 1))
            def _():
                bh[:, :256], bl[:, :256] = split(cols[at(j, 256), at(c, 256)])

                def blocks(i, _):
                    left = (at(i, 256), at(c, 256))
                    apply(i, nt3(yh[left], yl[left], bh[:, :256], bl[:, :256]))
                    return 0

                lax.fori_loop(0, chunks, blocks, 0)

            return 0

        lax.fori_loop(0, 4, chunk, 0)
        done = two_tile + 1

        def one(c, _):
            send(c)
            return 0

        lax.fori_loop(sent, done, one, 0)
        return done

    sent = lax.fori_loop(0, (n_col + 1) // 2, columns, jnp.int32(0))

    def last(c, _):
        send(c)
        return 0

    lax.fori_loop(sent, 16, last, 0)
    pltpu.make_async_copy(out_ref, out_hbm, out_sem.at[0]).wait()


def schur(scal, yh, yl, col_cross, cross, recv, damp):
    return pl.pallas_call(
        schur_kernel,
        in_specs=[pl.BlockSpec(memory_space=SMEM), pl.BlockSpec(memory_space=VMEM)]
        + [pl.BlockSpec(memory_space=pltpu.HBM)] * 5,
        out_specs=pl.BlockSpec(memory_space=pltpu.HBM),
        out_shape=jax.ShapeDtypeStruct((1024, 2048), F32),
        scratch_shapes=[
            VMEM((1024, 1024), BF16),
            VMEM((1024, 1024), BF16),
            VMEM((64 * TILE, TILE), F32),
            VMEM((32 * TILE, TILE), F32),
            VMEM((NDEV, LEAD, TILE), F32),
            VMEM((1024, 2048), F32),
            VMEM((2048, 1024), F32),
            VMEM((256, 1024), BF16),
            VMEM((256, 1024), BF16),
            SMEM((LEAD,), jnp.int32),
            SMEM((LEAD + 1,), jnp.int32),
            SMEM((16,), jnp.int32),
            SMEM((17,), jnp.int32),
            SMEM((64,), jnp.int32),
            pltpu.SemaphoreType.DMA((5,)),
            pltpu.SemaphoreType.DMA((1,)),
        ],
        compiler_params=pltpu.CompilerParams(vmem_limit_bytes=60 * 1024 * 1024),
        cost_estimate=pl.CostEstimate(
            flops=20_000_000_000, bytes_accessed=30_000_000, transcendentals=0
        ),
        name="schur",
    )(scal, damp, yh, yl, col_cross, cross, recv)


def local(pair_list, jacobian, damping):
    row = lax.axis_index("row")
    column = lax.axis_index("col")
    payload, cross = grams(jacobian, pair_list.T, damping)
    recv = lax.all_to_all(payload.reshape(NDEV, SLOTS1, TILE), BOTH, 0, 0, tiled=True)
    cross = cross.reshape(4 * TILE, TILE)
    moves = [
        (r * NCOL + c, (NCOL * (r % 2) + c) * NCOL + r // 2) for r in range(NROW) for c in range(NCOL)
    ]
    moved = lax.ppermute(cross, BOTH, moves)
    row_cross = lax.all_gather(cross, "col", axis=0, tiled=True)
    me = (row * NCOL + column).astype(jnp.int32).reshape(1)
    payload, index = gather_rows(me, recv.reshape(NDEV * SLOTS1, TILE))
    recv = lax.all_to_all(payload.reshape(NDEV, SLOTS2, TILE), BOTH, 0, 0, tiled=True)
    recv, moved = lax.optimization_barrier((recv, moved))
    col_cross = lax.all_gather(moved, "row", axis=0, tiled=True)

    index = index[:, :8].reshape(NDEV * 8)
    scal = jnp.concatenate(
        [
            lax.dynamic_slice(index, (row * 64,), (64,)),
            lax.dynamic_slice(index, (column * 128,), (128,)),
            jnp.stack([row, column]).astype(jnp.int32),
        ]
    )
    factor, yh, yl = factorise(scal, recv.reshape(NDEV * SLOTS2, TILE), row_cross)
    return factor, schur(scal, yh, yl, col_cross, row_cross, recv, damping)


def solution(mesh):
    placed = (P(("row", "col"), None), P(("row", "col"), None, None), P("row"))
    return jax.shard_map(
        local,
        mesh=mesh,
        in_specs=placed,
        out_specs=(P("row", None), P("row", "col")),
        check_vma=False,
    )
```

```python
import functools

import jax
import jax.numpy as jnp
from jax import lax
from jax.experimental import pallas as pl
from jax.experimental.pallas import tpu as pltpu
from jax.sharding import PartitionSpec as P

F32 = jnp.float32
BF16 = jnp.bfloat16
HI = lax.Precision.HIGHEST
BOTH = ("row", "col")
NROW, NCOL = 16, 8
NDEV = NROW * NCOL
TILE = 128
LEAD = 8
SLOTS1 = 16
SLOTS2 = 40
PAIR_SLOT = 28
DAMP_SLOT = 32
DIAG_SLOT = 33
OWN_SLOT = 36
VMEM = pltpu.VMEM
SMEM = pltpu.SMEM


def nt(a, b, precision=None):
    return lax.dot_general(
        a, b, (((1,), (1,)), ((), ())), precision=precision, preferred_element_type=F32
    )


def tn(a, b, precision=None):
    return lax.dot_general(
        a, b, (((0,), (0,)), ((), ())), precision=precision, preferred_element_type=F32
    )


def split(x):
    high = x.astype(BF16)
    return high, (x - high.astype(F32)).astype(BF16)


def nt3(ah, al, bh, bl):
    return nt(ah, bh) + (nt(ah, bl) + nt(al, bh))


def nn3(ah, al, bh, bl):
    def nn(a, b):
        return jnp.dot(a, b, preferred_element_type=F32)

    return nn(ah, bh) + (nn(ah, bl) + nn(al, bh))


def below_tile(a, b):
    return b * (LEAD - 1) - (b * (b - 1)) // 2 + (a - b - 1)


def gram_kernel(jac_ref, idx_ref, damp_ref, pay_ref, cross_ref):
    q = pl.program_id(0)
    high, low = split(jac_ref[0])
    mixed = tn(high, low)
    gram = tn(high, high) + (mixed + mixed.T)
    pay_ref[pl.ds(q, TILE, stride=SLOTS1), :] = gram[:TILE, :TILE]
    pay_ref[pl.ds(q + 4, TILE, stride=SLOTS1), :] = gram[TILE:, TILE:]
    pay_ref[pl.ds(q + 8, TILE, stride=SLOTS1), :] = gram[:TILE, TILE:]
    cross_ref[0] = gram[:TILE, TILE:]

    @pl.when(q == 0)
    def _():
        lane = lax.broadcasted_iota(jnp.int32, (TILE, TILE), 1)
        index = jnp.zeros((TILE, TILE), F32)
        for e in range(8):
            index = jnp.where(lane == e, idx_ref[e % 2, e // 2].astype(F32), index)
        pay_ref[pl.ds(12, TILE, stride=SLOTS1), :] = index
        rows = [damp_ref[TILE * b : TILE * (b + 1)].reshape(1, TILE) for b in range(LEAD)]
        wide = jnp.concatenate(rows + [jnp.zeros((TILE - 8, TILE), F32)], axis=0)
        pay_ref[pl.ds(13, TILE, stride=SLOTS1), :] = wide.T
        zero = jnp.zeros((TILE, TILE), F32)
        pay_ref[pl.ds(14, TILE, stride=SLOTS1), :] = zero
        pay_ref[pl.ds(15, TILE, stride=SLOTS1), :] = zero


def grams(jacobian, idx, damp):
    return pl.pallas_call(
        gram_kernel,
        grid=(4,),
        in_specs=[
            pl.BlockSpec((1, 1024, 256), lambda q: (q, 0, 0)),
            pl.BlockSpec(memory_space=SMEM),
            pl.BlockSpec((1024,), lambda q: (0,)),
        ],
        out_specs=[
            pl.BlockSpec((TILE * SLOTS1, TILE), lambda q: (0, 0)),
            pl.BlockSpec((1, TILE, TILE), lambda q: (q, 0, 0)),
        ],
        out_shape=[
            jax.ShapeDtypeStruct((TILE * SLOTS1, TILE), F32),
            jax.ShapeDtypeStruct((4, TILE, TILE), F32),
        ],
        name="grams",
    )(jacobian, idx, damp)


def gather_kernel(me_ref, recv_ref, pay_ref, idx_ref, flip_ref):
    me = me_ref[0]
    lane = lax.broadcasted_iota(jnp.int32, (TILE, TILE), 1)
    sub = lax.broadcasted_iota(jnp.int32, (TILE, TILE), 0)
    index = recv_ref[pl.ds(12, NDEV, stride=SLOTS1), :]
    idx_ref[...] = index.astype(jnp.int32)
    across = index.T.astype(jnp.int32)
    diag = jnp.zeros((TILE, TILE), F32)
    lead = jnp.zeros((32, TILE), F32)
    sub32 = lax.broadcasted_iota(jnp.int32, (32, TILE), 0)
    lane32 = lax.broadcasted_iota(jnp.int32, (32, TILE), 1)
    for q in range(4):
        a = across[2 * q : 2 * q + 1, :]
        b = across[2 * q + 1 : 2 * q + 2, :]
        first = recv_ref[pl.ds(q, NDEV, stride=SLOTS1), :]
        second = recv_ref[pl.ds(q + 4, NDEV, stride=SLOTS1), :]
        cross = recv_ref[pl.ds(q + 8, NDEV, stride=SLOTS1), :]
        diag = diag + jnp.dot((sub == a).astype(F32), first, precision=HI)
        diag = diag + jnp.dot((sub == b).astype(F32), second, precision=HI)
        hit = (sub32 == below_tile(a, b)) & (lane32 < NCOL)
        lead = lead + jnp.dot(hit.astype(F32), cross, precision=HI)
    packed = jnp.where(lane <= me, pltpu.roll(diag, 4, 0), diag)
    flip_ref[...] = diag.T
    entries = jnp.broadcast_to(flip_ref[pl.ds(me, 1), :], (8, TILE))
    damp = jnp.broadcast_to(recv_ref[13:14, :], (8, TILE))
    sub8 = lax.broadcasted_iota(jnp.int32, (8, TILE), 0)
    head = jnp.where(sub8 == 0, damp, jnp.where(sub8 == 1, entries, 0.0))
    last = jnp.where(sub8 >= 4, packed[:8, :], lead[24:, :])
    for r in range(NROW):
        tail = jnp.where(sub8 >= 4, packed[8 * r : 8 * r + 8, :], head)
        for c in range(NCOL):
            base = (r * NCOL + c) * SLOTS2
            pay_ref[base : base + 24, :] = lead[:24, :]
            pay_ref[base + 24 : base + 32, :] = last
            pay_ref[base + 32 : base + 40, :] = tail


def gather_rows(me, recv):
    return pl.pallas_call(
        gather_kernel,
        in_specs=[pl.BlockSpec(memory_space=SMEM), pl.BlockSpec(memory_space=VMEM)],
        out_shape=[
            jax.ShapeDtypeStruct((NDEV * SLOTS2, TILE), F32),
            jax.ShapeDtypeStruct((NDEV, TILE), jnp.int32),
        ],
        scratch_shapes=[VMEM((TILE, TILE), F32)],
        compiler_params=pltpu.CompilerParams(vmem_limit_bytes=16 * 1024 * 1024),
        name="gather_rows",
    )(me, recv)


def pieces(x):
    high = x.astype(BF16).astype(F32)
    rest = x - high
    mid = rest.astype(BF16).astype(F32)
    return high, mid, rest - mid


def factor128(rows):
    lane = lax.broadcasted_iota(jnp.int32, (8, TILE), 1)
    sub = lax.broadcasted_iota(jnp.int32, (8, TILE), 0)
    block = list(rows)
    inv = [jnp.where(lane == sub + 8 * v, 1.0, 0.0) for v in range(16)]
    upper, inverse = [], []

    def row(x, i):
        return jnp.broadcast_to(x[i : i + 1, :], (8, TILE))

    def col(x, i):
        return jnp.broadcast_to(x[:, i : i + 1], (8, TILE))

    for t in range(16):
        cols = [col(block[t], 8 * t + k) for k in range(8)]
        left, right = block[t], inv[t]
        up = jnp.zeros((8, TILE), F32)
        low = up
        for j in range(0, 8, 2):
            one, two = sub == j, sub == j + 1
            both = one | two
            x, y = cols[j], cols[j + 1]
            p, b, q = row(x, j), row(x, j + 1), row(y, j + 1)
            det = p * q - b * b
            over = 1.0 / det
            n1 = jnp.where(one, -q, jnp.where(two, b, x * q - y * b))
            n2 = jnp.where(one, b, jnp.where(two, -p, y * p - x * b))
            for k in range(j + 2, 8):
                change = (n1 * row(cols[k], j) + n2 * row(cols[k], j + 1)) * over
                cols[k] = jnp.where(both, 0.0, cols[k]) - change
            m1, m2 = n1 * over, n2 * over
            inv_p = 1.0 / p
            root_1, root_2, ratio = lax.rsqrt(p), lax.rsqrt(det * inv_p), b * inv_p
            l1, l2, r1, r2 = row(left, j), row(left, j + 1), row(right, j), row(right, j + 1)
            up = jnp.where(one, l1 * root_1, jnp.where(two, (l2 - ratio * l1) * root_2, up))
            low = jnp.where(one, r1 * root_1, jnp.where(two, (r2 - ratio * r1) * root_2, low))
            left = jnp.where(both, 0.0, left) - (m1 * l1 + m2 * l2)
            right = jnp.where(both, 0.0, right) - (m1 * r1 + m2 * r2)
        upper.append(jnp.where(lane >= sub + 8 * t, up, 0.0))
        inverse.append(low)
        if t < 15:
            parts = [col(block[t + 1], 8 * t + k) for k in range(8)]
            one = [parts[k] * row(left, k) for k in range(8)]
            two = [parts[k] * row(right, k) for k in range(8)]
            while len(one) > 1:
                one = [one[i] + one[i + 1] for i in range(0, len(one), 2)]
                two = [two[i] + two[i + 1] for i in range(0, len(two), 2)]
            block[t + 1] = block[t + 1] - one[0]
            inv[t + 1] = inv[t + 1] - two[0]
        if t < 14:
            h, m, low_part = pieces(block[t])
            mult = jnp.concatenate([h, h, m, h, low_part, m], axis=0).T.astype(BF16)
            h, m, low_part = pieces(jnp.concatenate([left, right], axis=1))
            base = jnp.concatenate([h, m, h, low_part, h, m], axis=0).astype(BF16)
            late = jnp.dot(mult, base, preferred_element_type=F32)
            for v in range(t + 2, 16):
                block[v] = block[v] - late[8 * v : 8 * v + 8, :TILE]
                inv[v] = inv[v] - late[8 * v : 8 * v + 8, TILE:]
    return upper, inverse


def at(i, n=TILE):
    return pl.ds(pl.multiple_of(i * n, n), n)


def three(x):
    high = x.astype(BF16)
    rest = x - high.astype(F32)
    mid = rest.astype(BF16)
    return high, mid, (rest - mid.astype(F32)).astype(BF16)


def stacks(x):
    h, m, low = three(x)
    return (
        jnp.concatenate([h, h], axis=1),
        jnp.concatenate([m, h], axis=1),
        jnp.concatenate([low, m], axis=1),
    )


def right_stacks(x):
    h, m, low = three(x)
    return jnp.concatenate([h, m], axis=1), jnp.concatenate([h, low], axis=1)


def six(pa, pb, pc, ra, rb):
    return nt(pa, ra) + (nt(pb, rb) + nt(pc, ra))


def unpack(pair, entries):
    lane = lax.broadcasted_iota(jnp.int32, (TILE, TILE), 1)
    sub = lax.broadcasted_iota(jnp.int32, (TILE, TILE), 0)
    low = jnp.where(lane < sub, pair, 0.0)
    high = jnp.where(lane > sub, pair, 0.0)
    one = low + low.T + jnp.where(lane == sub, pair, 0.0)
    return one, high + high.T + jnp.where(lane == sub, entries, 0.0)


def nn(a, b):
    return jnp.dot(a, b, precision=HI, preferred_element_type=F32)


def mark_rows(scal_ref, where_ref, tiles_ref):
    row = scal_ref[192]
    for u in range(LEAD):
        where_ref[u] = 0

    def mark(p, _):
        a = scal_ref[2 * p] - LEAD * row
        where_ref[a] = jnp.where(scal_ref[2 * p + 1] < LEAD, 1, where_ref[a])
        return 0

    @pl.when(row >= 1)
    def _():
        lax.fori_loop(0, 32, mark, 0)

    def place(u, count):
        used = where_ref[u] == 1
        where_ref[u] = jnp.where(used, count, -1)
        tiles_ref[count] = u
        return count + used.astype(jnp.int32)

    return lax.fori_loop(0, LEAD, place, jnp.int32(0))


def factor_kernel(
    scal_ref, recv_ref, cross_hbm, factor_hbm, yh_hbm, yl_hbm,
    lh_ref, ll_ref, wh_ref, wl_ref, body, inv_ref, pa, pb, pc, ra, rb,
    cross_ref, rows, xh, xl, yh, yl, none_ref, where_ref, tiles_ref, load_sem, factor_sem, y_sem,
):
    load = pltpu.make_async_copy(cross_hbm, cross_ref, load_sem.at[0])
    load.start()
    row = scal_ref[192]
    n_row = mark_rows(scal_ref, where_ref, tiles_ref)
    chunks = (n_row + 1) // 2
    fours = (n_row + 1) // 4
    none_ref[...] = jnp.zeros_like(none_ref)

    def clear(i, _):
        rows[at(i), :] = jnp.zeros((TILE, 1024), F32)
        return 0

    lax.fori_loop(0, n_row, clear, 0)
    lane = lax.broadcasted_iota(jnp.int32, (TILE, TILE), 1)
    sub = lax.broadcasted_iota(jnp.int32, (TILE, TILE), 0)

    def slot(i):
        return recv_ref[pl.ds(i, TILE, stride=SLOTS2), :]

    place = 0
    for k in range(LEAD):
        for i in range(k + 1, LEAD):
            body[TILE * i : TILE * (i + 1), TILE * k : TILE * (k + 1)] = slot(place)
            place += 1
    damp, entries = slot(DAMP_SLOT), slot(DIAG_SLOT)
    for u in range(4):
        one, two = unpack(slot(PAIR_SLOT + u), entries[:, 4 + u : 5 + u])
        for k, tile in ((u, one), (u + 4, two)):
            here = slice(TILE * k, TILE * (k + 1))
            body[here, here] = tile + jnp.where(lane == sub, damp[:, k : k + 1], 0.0)

    load.wait()

    def fill(p, _):
        a = scal_ref[2 * p] - LEAD * row
        b = scal_ref[2 * p + 1]

        @pl.when((b < LEAD) & (where_ref[a] >= 0))
        def _():
            rows[at(where_ref[a]), at(b)] += cross_ref[at(p), :]

        return 0

    lax.fori_loop(0, 32, fill, 0)

    def step(k, _):
        groups = [
            body[pl.ds(pl.multiple_of(k * TILE + 8 * v, 8), 8), at(k)] for v in range(16)
        ]
        upper, inverse = factor128(groups)
        inv = jnp.concatenate(inverse, axis=0)
        inv_ref[at(k), :] = inv
        wa, wb = right_stacks(inv)

        def panel(i, _):
            x = six(*stacks(body[at(i, 512), at(k)]), wa, wb)
            index = i * 512 + lax.broadcasted_iota(jnp.int32, (512, TILE), 0)
            x = jnp.where(index >= (k + 1) * TILE, x, 0.0)
            h, m, low = three(x)
            pa[at(i, 512), :] = jnp.concatenate([h, h], axis=1)
            pb[at(i, 512), :] = jnp.concatenate([m, h], axis=1)
            pc[at(i, 512), :] = jnp.concatenate([low, m], axis=1)
            ra[at(i, 512), :] = jnp.concatenate([h, m], axis=1)
            rb[at(i, 512), :] = jnp.concatenate([h, low], axis=1)
            lh_ref[at(i, 512), at(k)] = h
            ll_ref[at(i, 512), at(k)] = m
            return 0

        begin = (k >= 3).astype(jnp.int32)

        @pl.when(k >= 3)
        def _():
            zero = jnp.zeros((512, TILE), BF16)
            lh_ref[:512, at(k)] = zero
            ll_ref[:512, at(k)] = zero

        lax.fori_loop(begin, 2, panel, 0)

        def update(j, _):
            wa, wb = ra[at(j, 256), :], rb[at(j, 256), :]

            def rows_of(i, _):
                part = at(i, 512)
                body[part, at(j, 256)] -= six(pa[part, :], pb[part, :], pc[part, :], wa, wb)
                return 0

            lax.fori_loop((j >= 2).astype(jnp.int32), 2, rows_of, 0)
            return 0

        lax.fori_loop((k + 1) // 2, 4, update, 0)
        tile = jnp.concatenate(upper, axis=0).T
        body[at(k), at(k)] = tile
        lh_ref[at(k), at(k)], ll_ref[at(k), at(k)] = split(tile)
        return 0

    lax.fori_loop(0, LEAD, step, 0)
    for g in range(4):
        one = slice(256 * g, 256 * g + TILE)
        two = slice(256 * g + TILE, 256 * g + 256)
        cross = lh_ref[two, one].astype(F32) + ll_ref[two, one].astype(F32)
        corner = -nn(inv_ref[two, :], nn(cross, inv_ref[one, :]))
        wh_ref[one, :TILE], wl_ref[one, :TILE] = split(inv_ref[one, :])
        zero = jnp.zeros((TILE, TILE), BF16)
        wh_ref[one, TILE:], wl_ref[one, TILE:] = zero, zero
        wh_ref[two, :TILE], wl_ref[two, :TILE] = split(corner)
        wh_ref[two, TILE:], wl_ref[two, TILE:] = split(inv_ref[two, :])
    for g in range(4):
        here = slice(256 * g, 256 * (g + 1))

        def forward(i, _, g=g, here=here, size=512):
            part = at(i, size)
            rest = rows[part, here]
            if g:
                rest = rest - nt3(
                    xh[part, : 256 * g],
                    xl[part, : 256 * g],
                    lh_ref[here, : 256 * g],
                    ll_ref[here, : 256 * g],
                )
            x = nt3(*split(rest), wh_ref[here, :], wl_ref[here, :])
            rows[part, here] = x
            xh[part, here], xl[part, here] = split(x)
            return 0

        lax.fori_loop(0, fours, forward, 0)
        lax.fori_loop(2 * fours, chunks, functools.partial(forward, size=256), 0)

    for s in range(LEAD):
        part = slice(TILE * s, TILE * (s + 1))

        @pl.when(row == 0)
        def _(part=part):
            rows[part, :] = lh_ref[part, :].astype(F32) + ll_ref[part, :].astype(F32)
            pltpu.make_async_copy(rows.at[part], factor_hbm.at[part], factor_sem.at[0]).start()

        @pl.when((row >= 1) & (where_ref[s] >= 0))
        def _(s=s, part=part):
            pltpu.make_async_copy(
                rows.at[at(where_ref[s])], factor_hbm.at[part], factor_sem.at[0]
            ).start()

        @pl.when((row >= 1) & (where_ref[s] < 0))
        def _(part=part):
            pltpu.make_async_copy(none_ref, factor_hbm.at[part], factor_sem.at[0]).start()

    for g in reversed(range(4)):
        here = slice(256 * g, 256 * (g + 1))

        def backward(i, _, g=g, here=here, size=512):
            part = at(i, size)
            rest = rows[part, here]
            if g < 3:
                past = slice(256 * (g + 1), 1024)
                rest = rest - nn3(
                    yh[part, past], yl[part, past], lh_ref[past, here], ll_ref[past, here]
                )
            yh[part, here], yl[part, here] = split(
                nn3(*split(rest), wh_ref[here, :], wl_ref[here, :])
            )
            if g == 0:
                pltpu.make_async_copy(yh.at[part], yh_hbm.at[part], y_sem.at[0]).start()
                pltpu.make_async_copy(yl.at[part], yl_hbm.at[part], y_sem.at[1]).start()
            return 0

        lax.fori_loop(0, fours, backward, 0)
        lax.fori_loop(2 * fours, chunks, functools.partial(backward, size=256), 0)

    def sent(i, _):
        part = at(i, 256)
        pltpu.make_async_copy(yh.at[part], yh_hbm.at[part], y_sem.at[0]).wait()
        pltpu.make_async_copy(yl.at[part], yl_hbm.at[part], y_sem.at[1]).wait()
        return 0

    lax.fori_loop(0, chunks, sent, 0)
    pltpu.make_async_copy(rows, factor_hbm, factor_sem.at[0]).wait()


def factorise(scal, recv, cross):
    return pl.pallas_call(
        factor_kernel,
        in_specs=[
            pl.BlockSpec(memory_space=SMEM),
            pl.BlockSpec(memory_space=VMEM),
            pl.BlockSpec(memory_space=pltpu.HBM),
        ],
        out_specs=[pl.BlockSpec(memory_space=pltpu.HBM)] * 3,
        out_shape=[
            jax.ShapeDtypeStruct((1024, 1024), F32),
            jax.ShapeDtypeStruct((1024, 1024), BF16),
            jax.ShapeDtypeStruct((1024, 1024), BF16),
        ],
        scratch_shapes=[VMEM((1024, 1024), BF16)] * 2
        + [VMEM((1024, 256), BF16)] * 2
        + [VMEM((1024, 1024), F32), VMEM((1024, TILE), F32)]
        + [VMEM((1024, 256), BF16)] * 5
        + [VMEM((32 * TILE, TILE), F32), VMEM((1024, 1024), F32)]
        + [VMEM((1024, 1024), BF16)] * 4
        + [
            VMEM((TILE, 1024), F32),
            SMEM((LEAD,), jnp.int32),
            SMEM((LEAD + 1,), jnp.int32),
            pltpu.SemaphoreType.DMA((1,)),
            pltpu.SemaphoreType.DMA((1,)),
            pltpu.SemaphoreType.DMA((2,)),
        ],
        compiler_params=pltpu.CompilerParams(vmem_limit_bytes=59 * 1024 * 1024),
        cost_estimate=pl.CostEstimate(
            flops=40_000_000_000, bytes_accessed=8_000_000, transcendentals=0
        ),
        name="factorise",
    )(scal, recv, cross)


def schur_kernel(
    scal_ref, damp_ref, yh_hbm, yl_hbm, col_hbm, cross_hbm, recv_hbm, out_hbm,
    yh, yl, col_ref, cross_ref, diag_ref, out_ref, cols, bh, bl,
    row_where, row_tiles, where_ref, col_tiles, used_ref, load_sem, out_sem,
):
    row = scal_ref[192]
    column = scal_ref[193]
    loads = [
        pltpu.make_async_copy(source, target, load_sem.at[i])
        for i, (source, target) in enumerate(
            [
                (cross_hbm, cross_ref),
                (col_hbm, col_ref),
                (recv_hbm.at[:, DAMP_SLOT:SLOTS2], diag_ref),
                (yh_hbm, yh),
                (yl_hbm, yl),
            ]
        )
    ]
    for copy in loads:
        copy.start()
    for u in range(16):
        where_ref[u] = 0
    for u in range(64):
        used_ref[u] = 0

    def mark_col(p, _):
        tile = scal_ref[64 + 2 * p]
        a = tile - 16 * column
        b = scal_ref[65 + 2 * p]

        @pl.when((b < LEAD) & (tile >= LEAD) & (tile <= LEAD * row + 7))
        def _():
            where_ref[a] = 1
            used_ref[4 * a + b // 2] = 1

        return 0

    @pl.when(row >= 1)
    def _():
        lax.fori_loop(0, 64, mark_col, 0)

    def place_col(u, count):
        used = where_ref[u] == 1
        where_ref[u] = jnp.where(used, count, -1)
        col_tiles[count] = u
        return count + used.astype(jnp.int32)

    n_row = mark_rows(scal_ref, row_where, row_tiles)
    chunks = (n_row + 1) // 2
    n_col = lax.fori_loop(0, 16, place_col, jnp.int32(0))

    def blank(i, _):
        out_ref[at(i, 32), :] = jnp.zeros((32, 2048), F32)
        return 0

    lax.fori_loop(0, 32, blank, 0)

    def clear_cols(i, _):
        cols[at(i), :] = jnp.zeros((TILE, 1024), F32)
        return 0

    lax.fori_loop(0, n_col, clear_cols, 0)
    loads[0].wait()

    def fill_row(p, _):
        a = scal_ref[2 * p] - LEAD * row
        b = scal_ref[2 * p + 1]
        here = b - 16 * column

        @pl.when((b >= LEAD) & (here >= 0) & (here < 16))
        def _():
            out_ref[at(a), at(here)] += cross_ref[at(p), :]

        return 0

    def fill_col(p, _):
        a = scal_ref[64 + 2 * p] - 16 * column
        b = scal_ref[65 + 2 * p]

        @pl.when((b < LEAD) & (where_ref[a] >= 0))
        def _():
            cols[at(where_ref[a]), at(b)] += col_ref[at(p), :]

        return 0

    lax.fori_loop(0, 32, fill_row, 0)
    loads[1].wait()
    lax.fori_loop(0, 64, fill_col, 0)
    loads[2].wait()

    @pl.when((row >= 1) & (row // 2 == column))
    def _():
        lane = lax.broadcasted_iota(jnp.int32, (TILE, TILE), 1)
        sub = lax.broadcasted_iota(jnp.int32, (TILE, TILE), 0)
        entries = diag_ref[:, DIAG_SLOT - DAMP_SLOT, :]
        for u in range(4):
            mine = jnp.where(lane == LEAD * row + 4 + u, entries, 0.0)
            pair = diag_ref[:, OWN_SLOT - DAMP_SLOT + u, :]
            one, two = unpack(pair, jnp.sum(mine, axis=1, keepdims=True))
            for s, tile in ((u, one), (u + 4, two)):
                damp = damp_ref[TILE * s : TILE * (s + 1)].reshape(1, TILE)
                damp = jnp.where(lane == sub, jnp.broadcast_to(damp, (TILE, TILE)), 0.0)
                out_ref[TILE * s : TILE * (s + 1), at(LEAD * (row % 2) + s)] += tile + damp

    for copy in loads[3:]:
        copy.wait()

    def send(c):
        part = at(c)
        pltpu.make_async_copy(out_ref.at[:, part], out_hbm.at[:, part], out_sem.at[0]).start()

    def columns(j, sent):
        one_tile = col_tiles[2 * j]
        two_tile = col_tiles[jnp.minimum(2 * j + 1, n_col - 1)]

        def apply(i, prod):
            for p in range(2):
                for q in range(2):
                    it = 2 * i + p
                    a = row_tiles[it]
                    b = two_tile if q else one_tile
                    keep = (it < n_row) & (LEAD * row + a >= 16 * column + b)
                    if q:
                        keep = keep & (2 * j + 1 < n_col)

                    @pl.when(keep)
                    def _(a=a, b=b, p=p, q=q):
                        out_ref[at(a), at(b)] -= prod[
                            TILE * p : TILE * (p + 1), TILE * q : TILE * (q + 1)
                        ]

        def below(i):
            a = row_tiles[jnp.minimum(2 * i + 1, n_row - 1)]
            return LEAD * row + a >= 16 * column + one_tile

        def used(c):
            return used_ref[4 * one_tile + c] | used_ref[4 * two_tile + c]

        filled = used(0) + used(1) + used(2) + used(3)

        @pl.when(filled > 1)
        def _():
            def prepare(c, _):
                bh[:, at(c, 256)], bl[:, at(c, 256)] = split(cols[at(j, 256), at(c, 256)])
                return 0

            lax.fori_loop(0, 4, prepare, 0)

            def blocks(i, _):
                @pl.when(below(i))
                def _():
                    left = at(i, 256)
                    apply(i, nt3(yh[left, :], yl[left, :], bh[...], bl[...]))

                return 0

            lax.fori_loop(0, chunks, blocks, 0)

        def chunk(c, _):
            @pl.when((filled == 1) & (used(c) == 1))
            def _():
                bh[:, :256], bl[:, :256] = split(cols[at(j, 256), at(c, 256)])

                def blocks(i, _):
                    @pl.when(below(i))
                    def _():
                        left = (at(i, 256), at(c, 256))
                        apply(i, nt3(yh[left], yl[left], bh[:, :256], bl[:, :256]))

                    return 0

                lax.fori_loop(0, chunks, blocks, 0)

            return 0

        lax.fori_loop(0, 4, chunk, 0)
        done = two_tile + 1

        def one(c, _):
            send(c)
            return 0

        lax.fori_loop(sent, done, one, 0)
        return done

    sent = lax.fori_loop(0, (n_col + 1) // 2, columns, jnp.int32(0))

    def last(c, _):
        send(c)
        return 0

    lax.fori_loop(sent, 16, last, 0)
    pltpu.make_async_copy(out_ref, out_hbm, out_sem.at[0]).wait()


def schur(scal, yh, yl, col_cross, cross, recv, damp):
    return pl.pallas_call(
        schur_kernel,
        in_specs=[pl.BlockSpec(memory_space=SMEM), pl.BlockSpec(memory_space=VMEM)]
        + [pl.BlockSpec(memory_space=pltpu.HBM)] * 5,
        out_specs=pl.BlockSpec(memory_space=pltpu.HBM),
        out_shape=jax.ShapeDtypeStruct((1024, 2048), F32),
        scratch_shapes=[
            VMEM((1024, 1024), BF16),
            VMEM((1024, 1024), BF16),
            VMEM((64 * TILE, TILE), F32),
            VMEM((32 * TILE, TILE), F32),
            VMEM((NDEV, LEAD, TILE), F32),
            VMEM((1024, 2048), F32),
            VMEM((2048, 1024), F32),
            VMEM((256, 1024), BF16),
            VMEM((256, 1024), BF16),
            SMEM((LEAD,), jnp.int32),
            SMEM((LEAD + 1,), jnp.int32),
            SMEM((16,), jnp.int32),
            SMEM((17,), jnp.int32),
            SMEM((64,), jnp.int32),
            pltpu.SemaphoreType.DMA((5,)),
            pltpu.SemaphoreType.DMA((1,)),
        ],
        compiler_params=pltpu.CompilerParams(vmem_limit_bytes=60 * 1024 * 1024),
        cost_estimate=pl.CostEstimate(
            flops=20_000_000_000, bytes_accessed=30_000_000, transcendentals=0
        ),
        name="schur",
    )(scal, damp, yh, yl, col_cross, cross, recv)


def local(pair_list, jacobian, damping):
    row = lax.axis_index("row")
    column = lax.axis_index("col")
    payload, cross = grams(jacobian, pair_list.T, damping)
    recv = lax.all_to_all(payload.reshape(NDEV, SLOTS1, TILE), BOTH, 0, 0, tiled=True)
    cross = cross.reshape(4 * TILE, TILE)
    moves = [
        (r * NCOL + c, (NCOL * (r % 2) + c) * NCOL + r // 2) for r in range(NROW) for c in range(NCOL)
    ]
    moved = lax.ppermute(cross, BOTH, moves)
    row_cross = lax.all_gather(cross, "col", axis=0, tiled=True)
    me = (row * NCOL + column).astype(jnp.int32).reshape(1)
    payload, index = gather_rows(me, recv.reshape(NDEV * SLOTS1, TILE))
    recv = lax.all_to_all(payload.reshape(NDEV, SLOTS2, TILE), BOTH, 0, 0, tiled=True)
    recv, moved = lax.optimization_barrier((recv, moved))
    col_cross = lax.all_gather(moved, "row", axis=0, tiled=True)

    index = index[:, :8].reshape(NDEV * 8)
    scal = jnp.concatenate(
        [
            lax.dynamic_slice(index, (row * 64,), (64,)),
            lax.dynamic_slice(index, (column * 128,), (128,)),
            jnp.stack([row, column]).astype(jnp.int32),
        ]
    )
    factor, yh, yl = factorise(scal, recv.reshape(NDEV * SLOTS2, TILE), row_cross)
    return factor, schur(scal, yh, yl, col_cross, row_cross, recv, damping)


def solution(mesh):
    placed = (P(("row", "col"), None), P(("row", "col"), None, None), P("row"))
    return jax.shard_map(
        local,
        mesh=mesh,
        in_specs=placed,
        out_specs=(P("row", None), P("row", "col")),
        check_vma=False,
    )
```

```python
import functools

import jax
import jax.numpy as jnp
from jax import lax
from jax.experimental import pallas as pl
from jax.experimental.pallas import tpu as pltpu
from jax.sharding import PartitionSpec as P

F32 = jnp.float32
BF16 = jnp.bfloat16
HI = lax.Precision.HIGHEST
BOTH = ("row", "col")
NROW, NCOL = 16, 8
NDEV = NROW * NCOL
TILE = 128
LEAD = 8
SLOTS1 = 16
SLOTS2 = 40
PAIR_SLOT = 28
DAMP_SLOT = 32
DIAG_SLOT = 33
OWN_SLOT = 36
VMEM = pltpu.VMEM
SMEM = pltpu.SMEM


def nt(a, b, precision=None):
    return lax.dot_general(
        a, b, (((1,), (1,)), ((), ())), precision=precision, preferred_element_type=F32
    )


def tn(a, b, precision=None):
    return lax.dot_general(
        a, b, (((0,), (0,)), ((), ())), precision=precision, preferred_element_type=F32
    )


def split(x):
    high = x.astype(BF16)
    return high, (x - high.astype(F32)).astype(BF16)


def nt3(ah, al, bh, bl):
    return nt(ah, bh) + (nt(ah, bl) + nt(al, bh))


def nn3(ah, al, bh, bl):
    def nn(a, b):
        return jnp.dot(a, b, preferred_element_type=F32)

    return nn(ah, bh) + (nn(ah, bl) + nn(al, bh))


def below_tile(a, b):
    return b * (LEAD - 1) - (b * (b - 1)) // 2 + (a - b - 1)


def gram_kernel(jac_ref, idx_ref, damp_ref, pay_ref, cross_ref):
    q = pl.program_id(0)
    high, low = split(jac_ref[0])
    mixed = tn(high, low)
    gram = tn(high, high) + (mixed + mixed.T)
    pay_ref[pl.ds(q, TILE, stride=SLOTS1), :] = gram[:TILE, :TILE]
    pay_ref[pl.ds(q + 4, TILE, stride=SLOTS1), :] = gram[TILE:, TILE:]
    pay_ref[pl.ds(q + 8, TILE, stride=SLOTS1), :] = gram[:TILE, TILE:]
    cross_ref[0] = gram[:TILE, TILE:]

    @pl.when(q == 0)
    def _():
        lane = lax.broadcasted_iota(jnp.int32, (TILE, TILE), 1)
        index = jnp.zeros((TILE, TILE), F32)
        for e in range(8):
            index = jnp.where(lane == e, idx_ref[e % 2, e // 2].astype(F32), index)
        pay_ref[pl.ds(12, TILE, stride=SLOTS1), :] = index
        rows = [damp_ref[TILE * b : TILE * (b + 1)].reshape(1, TILE) for b in range(LEAD)]
        wide = jnp.concatenate(rows + [jnp.zeros((TILE - 8, TILE), F32)], axis=0)
        pay_ref[pl.ds(13, TILE, stride=SLOTS1), :] = wide.T
        zero = jnp.zeros((TILE, TILE), F32)
        pay_ref[pl.ds(14, TILE, stride=SLOTS1), :] = zero
        pay_ref[pl.ds(15, TILE, stride=SLOTS1), :] = zero


def grams(jacobian, idx, damp):
    return pl.pallas_call(
        gram_kernel,
        grid=(4,),
        in_specs=[
            pl.BlockSpec((1, 1024, 256), lambda q: (q, 0, 0)),
            pl.BlockSpec(memory_space=SMEM),
            pl.BlockSpec((1024,), lambda q: (0,)),
        ],
        out_specs=[
            pl.BlockSpec((TILE * SLOTS1, TILE), lambda q: (0, 0)),
            pl.BlockSpec((1, TILE, TILE), lambda q: (q, 0, 0)),
        ],
        out_shape=[
            jax.ShapeDtypeStruct((TILE * SLOTS1, TILE), F32),
            jax.ShapeDtypeStruct((4, TILE, TILE), F32),
        ],
        name="grams",
    )(jacobian, idx, damp)


def gather_kernel(me_ref, recv_ref, pay_ref, idx_ref, flip_ref):
    me = me_ref[0]
    lane = lax.broadcasted_iota(jnp.int32, (TILE, TILE), 1)
    sub = lax.broadcasted_iota(jnp.int32, (TILE, TILE), 0)
    index = recv_ref[pl.ds(12, NDEV, stride=SLOTS1), :]
    idx_ref[...] = index.astype(jnp.int32)
    across = index.T.astype(jnp.int32)
    diag = jnp.zeros((TILE, TILE), F32)
    lead = jnp.zeros((32, TILE), F32)
    sub32 = lax.broadcasted_iota(jnp.int32, (32, TILE), 0)
    lane32 = lax.broadcasted_iota(jnp.int32, (32, TILE), 1)
    for q in range(4):
        a = across[2 * q : 2 * q + 1, :]
        b = across[2 * q + 1 : 2 * q + 2, :]
        first = recv_ref[pl.ds(q, NDEV, stride=SLOTS1), :]
        second = recv_ref[pl.ds(q + 4, NDEV, stride=SLOTS1), :]
        cross = recv_ref[pl.ds(q + 8, NDEV, stride=SLOTS1), :]
        diag = diag + jnp.dot((sub == a).astype(F32), first, precision=HI)
        diag = diag + jnp.dot((sub == b).astype(F32), second, precision=HI)
        hit = (sub32 == below_tile(a, b)) & (lane32 < NCOL)
        lead = lead + jnp.dot(hit.astype(F32), cross, precision=HI)
    packed = jnp.where(lane <= me, pltpu.roll(diag, 4, 0), diag)
    flip_ref[...] = diag.T
    entries = jnp.broadcast_to(flip_ref[pl.ds(me, 1), :], (8, TILE))
    damp = jnp.broadcast_to(recv_ref[13:14, :], (8, TILE))
    sub8 = lax.broadcasted_iota(jnp.int32, (8, TILE), 0)
    head = jnp.where(sub8 == 0, damp, jnp.where(sub8 == 1, entries, 0.0))
    last = jnp.where(sub8 >= 4, packed[:8, :], lead[24:, :])
    for r in range(NROW):
        tail = jnp.where(sub8 >= 4, packed[8 * r : 8 * r + 8, :], head)
        for c in range(NCOL):
            base = (r * NCOL + c) * SLOTS2
            pay_ref[base : base + 24, :] = lead[:24, :]
            pay_ref[base + 24 : base + 32, :] = last
            pay_ref[base + 32 : base + 40, :] = tail


def gather_rows(me, recv):
    return pl.pallas_call(
        gather_kernel,
        in_specs=[pl.BlockSpec(memory_space=SMEM), pl.BlockSpec(memory_space=VMEM)],
        out_shape=[
            jax.ShapeDtypeStruct((NDEV * SLOTS2, TILE), F32),
            jax.ShapeDtypeStruct((NDEV, TILE), jnp.int32),
        ],
        scratch_shapes=[VMEM((TILE, TILE), F32)],
        compiler_params=pltpu.CompilerParams(vmem_limit_bytes=16 * 1024 * 1024),
        name="gather_rows",
    )(me, recv)


def pieces(x):
    high = x.astype(BF16).astype(F32)
    rest = x - high
    mid = rest.astype(BF16).astype(F32)
    return high, mid, rest - mid


def factor128(rows):
    lane = lax.broadcasted_iota(jnp.int32, (8, TILE), 1)
    sub = lax.broadcasted_iota(jnp.int32, (8, TILE), 0)
    block = list(rows)
    inv = [jnp.where(lane == sub + 8 * v, 1.0, 0.0) for v in range(16)]
    upper, inverse = [], []

    def row(x, i):
        return jnp.broadcast_to(x[i : i + 1, :], (8, TILE))

    def col(x, i):
        return jnp.broadcast_to(x[:, i : i + 1], (8, TILE))

    for t in range(16):
        cols = [col(block[t], 8 * t + k) for k in range(8)]
        left, right = block[t], inv[t]
        up = jnp.zeros((8, TILE), F32)
        low = up
        for j in range(0, 8, 2):
            one, two = sub == j, sub == j + 1
            both = one | two
            x, y = cols[j], cols[j + 1]
            p, b, q = row(x, j), row(x, j + 1), row(y, j + 1)
            det = p * q - b * b
            over = 1.0 / det
            n1 = jnp.where(one, -q, jnp.where(two, b, x * q - y * b))
            n2 = jnp.where(one, b, jnp.where(two, -p, y * p - x * b))
            for k in range(j + 2, 8):
                change = (n1 * row(cols[k], j) + n2 * row(cols[k], j + 1)) * over
                cols[k] = jnp.where(both, 0.0, cols[k]) - change
            m1, m2 = n1 * over, n2 * over
            inv_p = 1.0 / p
            root_1, root_2, ratio = lax.rsqrt(p), lax.rsqrt(det * inv_p), b * inv_p
            l1, l2, r1, r2 = row(left, j), row(left, j + 1), row(right, j), row(right, j + 1)
            up = jnp.where(one, l1 * root_1, jnp.where(two, (l2 - ratio * l1) * root_2, up))
            low = jnp.where(one, r1 * root_1, jnp.where(two, (r2 - ratio * r1) * root_2, low))
            left = jnp.where(both, 0.0, left) - (m1 * l1 + m2 * l2)
            right = jnp.where(both, 0.0, right) - (m1 * r1 + m2 * r2)
        upper.append(jnp.where(lane >= sub + 8 * t, up, 0.0))
        inverse.append(low)
        if t < 15:
            parts = [col(block[t + 1], 8 * t + k) for k in range(8)]
            one = [parts[k] * row(left, k) for k in range(8)]
            two = [parts[k] * row(right, k) for k in range(8)]
            while len(one) > 1:
                one = [one[i] + one[i + 1] for i in range(0, len(one), 2)]
                two = [two[i] + two[i + 1] for i in range(0, len(two), 2)]
            block[t + 1] = block[t + 1] - one[0]
            inv[t + 1] = inv[t + 1] - two[0]
        if t < 14:
            h, m, low_part = pieces(block[t])
            mult = jnp.concatenate([h, h, m, h, low_part, m], axis=0).T.astype(BF16)
            h, m, low_part = pieces(jnp.concatenate([left, right], axis=1))
            base = jnp.concatenate([h, m, h, low_part, h, m], axis=0).astype(BF16)
            late = jnp.dot(mult, base, preferred_element_type=F32)
            for v in range(t + 2, 16):
                block[v] = block[v] - late[8 * v : 8 * v + 8, :TILE]
                inv[v] = inv[v] - late[8 * v : 8 * v + 8, TILE:]
    return upper, inverse


def at(i, n=TILE):
    return pl.ds(pl.multiple_of(i * n, n), n)


def three(x):
    high = x.astype(BF16)
    rest = x - high.astype(F32)
    mid = rest.astype(BF16)
    return high, mid, (rest - mid.astype(F32)).astype(BF16)


def stacks(x):
    h, m, low = three(x)
    return (
        jnp.concatenate([h, h], axis=1),
        jnp.concatenate([m, h], axis=1),
        jnp.concatenate([low, m], axis=1),
    )


def right_stacks(x):
    h, m, low = three(x)
    return jnp.concatenate([h, m], axis=1), jnp.concatenate([h, low], axis=1)


def six(pa, pb, pc, ra, rb):
    return nt(pa, ra) + (nt(pb, rb) + nt(pc, ra))


def unpack(pair, entries):
    lane = lax.broadcasted_iota(jnp.int32, (TILE, TILE), 1)
    sub = lax.broadcasted_iota(jnp.int32, (TILE, TILE), 0)
    low = jnp.where(lane < sub, pair, 0.0)
    high = jnp.where(lane > sub, pair, 0.0)
    one = low + low.T + jnp.where(lane == sub, pair, 0.0)
    return one, high + high.T + jnp.where(lane == sub, entries, 0.0)


def mark_rows(scal_ref, where_ref, tiles_ref):
    row = scal_ref[192]
    for u in range(LEAD):
        where_ref[u] = 0

    def mark(p, _):
        a = scal_ref[2 * p] - LEAD * row
        where_ref[a] = jnp.where(scal_ref[2 * p + 1] < LEAD, 1, where_ref[a])
        return 0

    @pl.when(row >= 1)
    def _():
        lax.fori_loop(0, 32, mark, 0)

    def place(u, count):
        used = where_ref[u] == 1
        where_ref[u] = jnp.where(used, count, -1)
        tiles_ref[count] = u
        return count + used.astype(jnp.int32)

    return lax.fori_loop(0, LEAD, place, jnp.int32(0))


def factor_kernel(
    scal_ref, recv_ref, cross_hbm, factor_hbm, yh_hbm, yl_hbm,
    lh_ref, ll_ref, wh_ref, wl_ref, body, inv_ref, pa, pb, pc, ra, rb,
    cross_ref, rows, xh, xl, yh, yl, none_ref, where_ref, tiles_ref, load_sem, factor_sem, y_sem,
):
    load = pltpu.make_async_copy(cross_hbm, cross_ref, load_sem.at[0])
    load.start()
    row = scal_ref[192]
    n_row = mark_rows(scal_ref, where_ref, tiles_ref)
    chunks = (n_row + 1) // 2
    fours = (n_row + 1) // 4
    none_ref[...] = jnp.zeros_like(none_ref)

    def clear(i, _):
        rows[at(i), :] = jnp.zeros((TILE, 1024), F32)
        return 0

    lax.fori_loop(0, n_row, clear, 0)
    lane = lax.broadcasted_iota(jnp.int32, (TILE, TILE), 1)
    sub = lax.broadcasted_iota(jnp.int32, (TILE, TILE), 0)

    def slot(i):
        return recv_ref[pl.ds(i, TILE, stride=SLOTS2), :]

    place = 0
    for k in range(LEAD):
        for i in range(k + 1, LEAD):
            body[TILE * i : TILE * (i + 1), TILE * k : TILE * (k + 1)] = slot(place)
            place += 1
    damp, entries = slot(DAMP_SLOT), slot(DIAG_SLOT)
    for u in range(4):
        one, two = unpack(slot(PAIR_SLOT + u), entries[:, 4 + u : 5 + u])
        for k, tile in ((u, one), (u + 4, two)):
            here = slice(TILE * k, TILE * (k + 1))
            body[here, here] = tile + jnp.where(lane == sub, damp[:, k : k + 1], 0.0)

    load.wait()

    def fill(p, _):
        a = scal_ref[2 * p] - LEAD * row
        b = scal_ref[2 * p + 1]

        @pl.when((b < LEAD) & (where_ref[a] >= 0))
        def _():
            rows[at(where_ref[a]), at(b)] += cross_ref[at(p), :]

        return 0

    lax.fori_loop(0, 32, fill, 0)
    for ref in (pa, pb, pc, ra, rb):
        ref[...] = jnp.zeros_like(ref)

    def step(k, _):
        groups = [
            body[pl.ds(pl.multiple_of(k * TILE + 8 * v, 8), 8), at(k)] for v in range(16)
        ]
        for j in range(2, 4):
            part = slice(256 * j, 1024)
            wide = slice(256 * j, 256 * (j + 1))
            later = j > k // 2
            wa = jnp.where(later, ra[wide, :], jnp.zeros_like(ra[wide, :]))
            wb = jnp.where(later, rb[wide, :], jnp.zeros_like(rb[wide, :]))
            body[part, wide] -= six(pa[part, :], pb[part, :], pc[part, :], wa, wb)
        upper, inverse = factor128(groups)
        inv = jnp.concatenate(inverse, axis=0)
        inv_ref[at(k), :] = inv
        wa, wb = right_stacks(inv)

        def panel(i, _):
            x = six(*stacks(body[at(i, 512), at(k)]), wa, wb)
            index = i * 512 + lax.broadcasted_iota(jnp.int32, (512, TILE), 0)
            x = jnp.where(index >= (k + 1) * TILE, x, 0.0)
            h, m, low = three(x)
            pa[at(i, 512), :] = jnp.concatenate([h, h], axis=1)
            pb[at(i, 512), :] = jnp.concatenate([m, h], axis=1)
            pc[at(i, 512), :] = jnp.concatenate([low, m], axis=1)
            ra[at(i, 512), :] = jnp.concatenate([h, m], axis=1)
            rb[at(i, 512), :] = jnp.concatenate([h, low], axis=1)
            lh_ref[at(i, 512), at(k)] = h
            ll_ref[at(i, 512), at(k)] = m
            return 0

        begin = (k >= 3).astype(jnp.int32)

        @pl.when(k >= 3)
        def _():
            zero = jnp.zeros((512, TILE), BF16)
            lh_ref[:512, at(k)] = zero
            ll_ref[:512, at(k)] = zero

        lax.fori_loop(begin, 2, panel, 0)

        def update(j, _):
            wa, wb = ra[at(j, 256), :], rb[at(j, 256), :]

            def rows_of(i, _):
                part = at(i, 512)
                body[part, at(j, 256)] -= six(pa[part, :], pb[part, :], pc[part, :], wa, wb)
                return 0

            lax.fori_loop((j >= 2).astype(jnp.int32), 2, rows_of, 0)
            return 0

        lax.fori_loop((k + 1) // 2, jnp.minimum(jnp.maximum((k + 3) // 2, 2), 4), update, 0)
        tile = jnp.concatenate(upper, axis=0).T
        body[at(k), at(k)] = tile
        lh_ref[at(k), at(k)], ll_ref[at(k), at(k)] = split(tile)
        return 0

    lax.fori_loop(0, LEAD, step, 0)
    for g in range(4):
        one = slice(256 * g, 256 * g + TILE)
        two = slice(256 * g + TILE, 256 * g + 256)
        w1, w2 = split(inv_ref[one, :]), split(inv_ref[two, :])
        inner = split(nn3(lh_ref[two, one], ll_ref[two, one], *w1))
        corner = -nn3(*w2, *inner)
        wh_ref[one, :TILE], wl_ref[one, :TILE] = w1
        zero = jnp.zeros((TILE, TILE), BF16)
        wh_ref[one, TILE:], wl_ref[one, TILE:] = zero, zero
        wh_ref[two, :TILE], wl_ref[two, :TILE] = split(corner)
        wh_ref[two, TILE:], wl_ref[two, TILE:] = w2
    for g in range(4):
        here = slice(256 * g, 256 * (g + 1))

        def forward(i, _, g=g, here=here, size=512):
            part = at(i, size)
            rest = rows[part, here]
            if g:
                rest = rest - nt3(
                    xh[part, : 256 * g],
                    xl[part, : 256 * g],
                    lh_ref[here, : 256 * g],
                    ll_ref[here, : 256 * g],
                )
            x = nt3(*split(rest), wh_ref[here, :], wl_ref[here, :])
            rows[part, here] = x
            xh[part, here], xl[part, here] = split(x)
            return 0

        lax.fori_loop(0, fours, forward, 0)
        lax.fori_loop(2 * fours, chunks, functools.partial(forward, size=256), 0)

    for s in range(LEAD):
        part = slice(TILE * s, TILE * (s + 1))

        @pl.when(row == 0)
        def _(part=part):
            rows[part, :] = lh_ref[part, :].astype(F32) + ll_ref[part, :].astype(F32)
            pltpu.make_async_copy(rows.at[part], factor_hbm.at[part], factor_sem.at[0]).start()

        @pl.when((row >= 1) & (where_ref[s] >= 0))
        def _(s=s, part=part):
            pltpu.make_async_copy(
                rows.at[at(where_ref[s])], factor_hbm.at[part], factor_sem.at[0]
            ).start()

        @pl.when((row >= 1) & (where_ref[s] < 0))
        def _(part=part):
            pltpu.make_async_copy(none_ref, factor_hbm.at[part], factor_sem.at[0]).start()

    for g in reversed(range(4)):
        here = slice(256 * g, 256 * (g + 1))

        def backward(i, _, g=g, here=here, size=512):
            part = at(i, size)
            rest = rows[part, here]
            if g < 3:
                past = slice(256 * (g + 1), 1024)
                rest = rest - nn3(
                    yh[part, past], yl[part, past], lh_ref[past, here], ll_ref[past, here]
                )
            yh[part, here], yl[part, here] = split(
                nn3(*split(rest), wh_ref[here, :], wl_ref[here, :])
            )
            if g == 0:
                pltpu.make_async_copy(yh.at[part], yh_hbm.at[part], y_sem.at[0]).start()
                pltpu.make_async_copy(yl.at[part], yl_hbm.at[part], y_sem.at[1]).start()
            return 0

        lax.fori_loop(0, fours, backward, 0)
        lax.fori_loop(2 * fours, chunks, functools.partial(backward, size=256), 0)

    def sent(i, _):
        part = at(i, 256)
        pltpu.make_async_copy(yh.at[part], yh_hbm.at[part], y_sem.at[0]).wait()
        pltpu.make_async_copy(yl.at[part], yl_hbm.at[part], y_sem.at[1]).wait()
        return 0

    lax.fori_loop(0, chunks, sent, 0)
    pltpu.make_async_copy(rows, factor_hbm, factor_sem.at[0]).wait()


def factorise(scal, recv, cross):
    return pl.pallas_call(
        factor_kernel,
        in_specs=[
            pl.BlockSpec(memory_space=SMEM),
            pl.BlockSpec(memory_space=VMEM),
            pl.BlockSpec(memory_space=pltpu.HBM),
        ],
        out_specs=[pl.BlockSpec(memory_space=pltpu.HBM)] * 3,
        out_shape=[
            jax.ShapeDtypeStruct((1024, 1024), F32),
            jax.ShapeDtypeStruct((1024, 1024), BF16),
            jax.ShapeDtypeStruct((1024, 1024), BF16),
        ],
        scratch_shapes=[VMEM((1024, 1024), BF16)] * 2
        + [VMEM((1024, 256), BF16)] * 2
        + [VMEM((1024, 1024), F32), VMEM((1024, TILE), F32)]
        + [VMEM((1024, 256), BF16)] * 5
        + [VMEM((32 * TILE, TILE), F32), VMEM((1024, 1024), F32)]
        + [VMEM((1024, 1024), BF16)] * 4
        + [
            VMEM((TILE, 1024), F32),
            SMEM((LEAD,), jnp.int32),
            SMEM((LEAD + 1,), jnp.int32),
            pltpu.SemaphoreType.DMA((1,)),
            pltpu.SemaphoreType.DMA((1,)),
            pltpu.SemaphoreType.DMA((2,)),
        ],
        compiler_params=pltpu.CompilerParams(vmem_limit_bytes=59 * 1024 * 1024),
        cost_estimate=pl.CostEstimate(
            flops=40_000_000_000, bytes_accessed=8_000_000, transcendentals=0
        ),
        name="factorise",
    )(scal, recv, cross)


def schur_kernel(
    scal_ref, damp_ref, yh_hbm, yl_hbm, col_hbm, cross_hbm, recv_hbm, out_hbm,
    yh, yl, col_ref, cross_ref, diag_ref, out_ref, cols, bh, bl,
    row_where, row_tiles, where_ref, col_tiles, used_ref, load_sem, out_sem,
):
    row = scal_ref[192]
    column = scal_ref[193]
    loads = [
        pltpu.make_async_copy(source, target, load_sem.at[i])
        for i, (source, target) in enumerate(
            [
                (cross_hbm, cross_ref),
                (col_hbm, col_ref),
                (recv_hbm.at[:, DAMP_SLOT:SLOTS2], diag_ref),
                (yh_hbm, yh),
                (yl_hbm, yl),
            ]
        )
    ]
    for copy in loads:
        copy.start()
    for u in range(16):
        where_ref[u] = 0
    for u in range(64):
        used_ref[u] = 0

    def mark_col(p, _):
        tile = scal_ref[64 + 2 * p]
        a = tile - 16 * column
        b = scal_ref[65 + 2 * p]

        @pl.when((b < LEAD) & (tile >= LEAD) & (tile <= LEAD * row + 7))
        def _():
            where_ref[a] = 1
            used_ref[4 * a + b // 2] = 1

        return 0

    @pl.when(row >= 1)
    def _():
        lax.fori_loop(0, 64, mark_col, 0)

    def place_col(u, count):
        used = where_ref[u] == 1
        where_ref[u] = jnp.where(used, count, -1)
        col_tiles[count] = u
        return count + used.astype(jnp.int32)

    n_row = mark_rows(scal_ref, row_where, row_tiles)
    chunks = (n_row + 1) // 2
    n_col = lax.fori_loop(0, 16, place_col, jnp.int32(0))

    def blank(i, _):
        out_ref[at(i, 32), :] = jnp.zeros((32, 2048), F32)
        return 0

    lax.fori_loop(0, 32, blank, 0)

    def clear_cols(i, _):
        cols[at(i), :] = jnp.zeros((TILE, 1024), F32)
        return 0

    lax.fori_loop(0, n_col, clear_cols, 0)
    loads[0].wait()

    def fill_row(p, _):
        a = scal_ref[2 * p] - LEAD * row
        b = scal_ref[2 * p + 1]
        here = b - 16 * column

        @pl.when((b >= LEAD) & (here >= 0) & (here < 16))
        def _():
            out_ref[at(a), at(here)] += cross_ref[at(p), :]

        return 0

    def fill_col(p, _):
        a = scal_ref[64 + 2 * p] - 16 * column
        b = scal_ref[65 + 2 * p]

        @pl.when((b < LEAD) & (where_ref[a] >= 0))
        def _():
            cols[at(where_ref[a]), at(b)] += col_ref[at(p), :]

        return 0

    lax.fori_loop(0, 32, fill_row, 0)
    loads[1].wait()
    lax.fori_loop(0, 64, fill_col, 0)
    loads[2].wait()

    @pl.when((row >= 1) & (row // 2 == column))
    def _():
        lane = lax.broadcasted_iota(jnp.int32, (TILE, TILE), 1)
        sub = lax.broadcasted_iota(jnp.int32, (TILE, TILE), 0)
        entries = diag_ref[:, DIAG_SLOT - DAMP_SLOT, :]
        for u in range(4):
            mine = jnp.where(lane == LEAD * row + 4 + u, entries, 0.0)
            pair = diag_ref[:, OWN_SLOT - DAMP_SLOT + u, :]
            one, two = unpack(pair, jnp.sum(mine, axis=1, keepdims=True))
            for s, tile in ((u, one), (u + 4, two)):
                damp = damp_ref[TILE * s : TILE * (s + 1)].reshape(1, TILE)
                damp = jnp.where(lane == sub, jnp.broadcast_to(damp, (TILE, TILE)), 0.0)
                out_ref[TILE * s : TILE * (s + 1), at(LEAD * (row % 2) + s)] += tile + damp

    for copy in loads[3:]:
        copy.wait()

    def send(c):
        part = at(c)
        pltpu.make_async_copy(out_ref.at[:, part], out_hbm.at[:, part], out_sem.at[0]).start()

    def columns(j, sent):
        one_tile = col_tiles[2 * j]
        two_tile = col_tiles[jnp.minimum(2 * j + 1, n_col - 1)]

        def apply(i, prod):
            for p in range(2):
                for q in range(2):
                    it = 2 * i + p
                    a = row_tiles[it]
                    b = two_tile if q else one_tile
                    keep = (it < n_row) & (LEAD * row + a >= 16 * column + b)
                    if q:
                        keep = keep & (2 * j + 1 < n_col)

                    @pl.when(keep)
                    def _(a=a, b=b, p=p, q=q):
                        out_ref[at(a), at(b)] -= prod[
                            TILE * p : TILE * (p + 1), TILE * q : TILE * (q + 1)
                        ]

        def below(i):
            a = row_tiles[jnp.minimum(2 * i + 1, n_row - 1)]
            return LEAD * row + a >= 16 * column + one_tile

        def used(c):
            return used_ref[4 * one_tile + c] | used_ref[4 * two_tile + c]

        filled = used(0) + used(1) + used(2) + used(3)

        @pl.when(filled > 1)
        def _():
            def prepare(c, _):
                bh[:, at(c, 256)], bl[:, at(c, 256)] = split(cols[at(j, 256), at(c, 256)])
                return 0

            lax.fori_loop(0, 4, prepare, 0)

            def blocks(i, _):
                @pl.when(below(i))
                def _():
                    left = at(i, 256)
                    apply(i, nt3(yh[left, :], yl[left, :], bh[...], bl[...]))

                return 0

            lax.fori_loop(0, chunks, blocks, 0)

        def chunk(c, _):
            @pl.when((filled == 1) & (used(c) == 1))
            def _():
                bh[:, :256], bl[:, :256] = split(cols[at(j, 256), at(c, 256)])

                def blocks(i, _):
                    @pl.when(below(i))
                    def _():
                        left = (at(i, 256), at(c, 256))
                        apply(i, nt3(yh[left], yl[left], bh[:, :256], bl[:, :256]))

                    return 0

                lax.fori_loop(0, chunks, blocks, 0)

            return 0

        lax.fori_loop(0, 4, chunk, 0)
        done = two_tile + 1

        def one(c, _):
            send(c)
            return 0

        lax.fori_loop(sent, done, one, 0)
        return done

    sent = lax.fori_loop(0, (n_col + 1) // 2, columns, jnp.int32(0))

    def last(c, _):
        send(c)
        return 0

    lax.fori_loop(sent, 16, last, 0)
    pltpu.make_async_copy(out_ref, out_hbm, out_sem.at[0]).wait()


def schur(scal, yh, yl, col_cross, cross, recv, damp):
    return pl.pallas_call(
        schur_kernel,
        in_specs=[pl.BlockSpec(memory_space=SMEM), pl.BlockSpec(memory_space=VMEM)]
        + [pl.BlockSpec(memory_space=pltpu.HBM)] * 5,
        out_specs=pl.BlockSpec(memory_space=pltpu.HBM),
        out_shape=jax.ShapeDtypeStruct((1024, 2048), F32),
        scratch_shapes=[
            VMEM((1024, 1024), BF16),
            VMEM((1024, 1024), BF16),
            VMEM((64 * TILE, TILE), F32),
            VMEM((32 * TILE, TILE), F32),
            VMEM((NDEV, LEAD, TILE), F32),
            VMEM((1024, 2048), F32),
            VMEM((2048, 1024), F32),
            VMEM((256, 1024), BF16),
            VMEM((256, 1024), BF16),
            SMEM((LEAD,), jnp.int32),
            SMEM((LEAD + 1,), jnp.int32),
            SMEM((16,), jnp.int32),
            SMEM((17,), jnp.int32),
            SMEM((64,), jnp.int32),
            pltpu.SemaphoreType.DMA((5,)),
            pltpu.SemaphoreType.DMA((1,)),
        ],
        compiler_params=pltpu.CompilerParams(vmem_limit_bytes=60 * 1024 * 1024),
        cost_estimate=pl.CostEstimate(
            flops=20_000_000_000, bytes_accessed=30_000_000, transcendentals=0
        ),
        name="schur",
    )(scal, damp, yh, yl, col_cross, cross, recv)


def local(pair_list, jacobian, damping):
    row = lax.axis_index("row")
    column = lax.axis_index("col")
    payload, cross = grams(jacobian, pair_list.T, damping)
    recv = lax.all_to_all(payload.reshape(NDEV, SLOTS1, TILE), BOTH, 0, 0, tiled=True)
    cross = cross.reshape(4 * TILE, TILE)
    moves = [
        (r * NCOL + c, (NCOL * (r % 2) + c) * NCOL + r // 2) for r in range(NROW) for c in range(NCOL)
    ]
    moved = lax.ppermute(cross, BOTH, moves)
    row_cross = lax.all_gather(cross, "col", axis=0, tiled=True)
    me = (row * NCOL + column).astype(jnp.int32).reshape(1)
    payload, index = gather_rows(me, recv.reshape(NDEV * SLOTS1, TILE))
    recv = lax.all_to_all(payload.reshape(NDEV, SLOTS2, TILE), BOTH, 0, 0, tiled=True)
    recv, moved = lax.optimization_barrier((recv, moved))
    col_cross = lax.all_gather(moved, "row", axis=0, tiled=True)

    index = index[:, :8].reshape(NDEV * 8)
    scal = jnp.concatenate(
        [
            lax.dynamic_slice(index, (row * 64,), (64,)),
            lax.dynamic_slice(index, (column * 128,), (128,)),
            jnp.stack([row, column]).astype(jnp.int32),
        ]
    )
    factor, yh, yl = factorise(scal, recv.reshape(NDEV * SLOTS2, TILE), row_cross)
    return factor, schur(scal, yh, yl, col_cross, row_cross, recv, damping)


def solution(mesh):
    placed = (P(("row", "col"), None), P(("row", "col"), None, None), P("row"))
    return jax.shard_map(
        local,
        mesh=mesh,
        in_specs=placed,
        out_specs=(P("row", None), P("row", "col")),
        check_vma=False,
    )
```

```python
import functools

import jax
import jax.numpy as jnp
from jax import lax
from jax.experimental import pallas as pl
from jax.experimental.pallas import tpu as pltpu
from jax.sharding import PartitionSpec as P

F32 = jnp.float32
BF16 = jnp.bfloat16
HI = lax.Precision.HIGHEST
BOTH = ("row", "col")
NROW, NCOL = 16, 8
NDEV = NROW * NCOL
TILE = 128
LEAD = 8
SLOTS1 = 16
SLOTS2 = 40
PAIR_SLOT = 28
DAMP_SLOT = 32
DIAG_SLOT = 33
OWN_SLOT = 36
VMEM = pltpu.VMEM
SMEM = pltpu.SMEM


def nt(a, b, precision=None):
    return lax.dot_general(
        a, b, (((1,), (1,)), ((), ())), precision=precision, preferred_element_type=F32
    )


def tn(a, b, precision=None):
    return lax.dot_general(
        a, b, (((0,), (0,)), ((), ())), precision=precision, preferred_element_type=F32
    )


def split(x):
    high = x.astype(BF16)
    return high, (x - high.astype(F32)).astype(BF16)


def nt3(ah, al, bh, bl):
    return nt(ah, bh) + (nt(ah, bl) + nt(al, bh))


def nn3(ah, al, bh, bl):
    def nn(a, b):
        return jnp.dot(a, b, preferred_element_type=F32)

    return nn(ah, bh) + (nn(ah, bl) + nn(al, bh))


def below_tile(a, b):
    return b * (LEAD - 1) - (b * (b - 1)) // 2 + (a - b - 1)


def gram_kernel(jac_ref, idx_ref, damp_ref, pay_ref, cross_ref):
    q = pl.program_id(0)
    high, low = split(jac_ref[0])
    mixed = tn(high, low)
    gram = tn(high, high) + (mixed + mixed.T)
    pay_ref[pl.ds(q, TILE, stride=SLOTS1), :] = gram[:TILE, :TILE]
    pay_ref[pl.ds(q + 4, TILE, stride=SLOTS1), :] = gram[TILE:, TILE:]
    pay_ref[pl.ds(q + 8, TILE, stride=SLOTS1), :] = gram[:TILE, TILE:]
    cross_ref[0] = gram[:TILE, TILE:]

    @pl.when(q == 0)
    def _():
        lane = lax.broadcasted_iota(jnp.int32, (TILE, TILE), 1)
        index = jnp.zeros((TILE, TILE), F32)
        for e in range(8):
            index = jnp.where(lane == e, idx_ref[e % 2, e // 2].astype(F32), index)
        pay_ref[pl.ds(12, TILE, stride=SLOTS1), :] = index
        rows = [damp_ref[TILE * b : TILE * (b + 1)].reshape(1, TILE) for b in range(LEAD)]
        wide = jnp.concatenate(rows + [jnp.zeros((TILE - 8, TILE), F32)], axis=0)
        pay_ref[pl.ds(13, TILE, stride=SLOTS1), :] = wide.T
        zero = jnp.zeros((TILE, TILE), F32)
        pay_ref[pl.ds(14, TILE, stride=SLOTS1), :] = zero
        pay_ref[pl.ds(15, TILE, stride=SLOTS1), :] = zero


def grams(jacobian, idx, damp):
    return pl.pallas_call(
        gram_kernel,
        grid=(4,),
        in_specs=[
            pl.BlockSpec((1, 1024, 256), lambda q: (q, 0, 0)),
            pl.BlockSpec(memory_space=SMEM),
            pl.BlockSpec((1024,), lambda q: (0,)),
        ],
        out_specs=[
            pl.BlockSpec((TILE * SLOTS1, TILE), lambda q: (0, 0)),
            pl.BlockSpec((1, TILE, TILE), lambda q: (q, 0, 0)),
        ],
        out_shape=[
            jax.ShapeDtypeStruct((TILE * SLOTS1, TILE), F32),
            jax.ShapeDtypeStruct((4, TILE, TILE), F32),
        ],
        name="grams",
    )(jacobian, idx, damp)


def gather_kernel(me_ref, recv_ref, pay_ref, idx_ref, flip_ref):
    me = me_ref[0]
    lane = lax.broadcasted_iota(jnp.int32, (TILE, TILE), 1)
    sub = lax.broadcasted_iota(jnp.int32, (TILE, TILE), 0)
    index = recv_ref[pl.ds(12, NDEV, stride=SLOTS1), :]
    idx_ref[...] = index.astype(jnp.int32)
    across = index.T.astype(jnp.int32)
    diag = jnp.zeros((TILE, TILE), F32)
    lead = jnp.zeros((32, TILE), F32)
    sub32 = lax.broadcasted_iota(jnp.int32, (32, TILE), 0)
    lane32 = lax.broadcasted_iota(jnp.int32, (32, TILE), 1)
    for q in range(4):
        a = across[2 * q : 2 * q + 1, :]
        b = across[2 * q + 1 : 2 * q + 2, :]
        first = recv_ref[pl.ds(q, NDEV, stride=SLOTS1), :]
        second = recv_ref[pl.ds(q + 4, NDEV, stride=SLOTS1), :]
        cross = recv_ref[pl.ds(q + 8, NDEV, stride=SLOTS1), :]
        diag = diag + jnp.dot((sub == a).astype(F32), first, precision=HI)
        diag = diag + jnp.dot((sub == b).astype(F32), second, precision=HI)
        hit = (sub32 == below_tile(a, b)) & (lane32 < NCOL)
        lead = lead + jnp.dot(hit.astype(F32), cross, precision=HI)
    packed = jnp.where(lane <= me, pltpu.roll(diag, 4, 0), diag)
    flip_ref[...] = diag.T
    entries = jnp.broadcast_to(flip_ref[pl.ds(me, 1), :], (8, TILE))
    damp = jnp.broadcast_to(recv_ref[13:14, :], (8, TILE))
    sub8 = lax.broadcasted_iota(jnp.int32, (8, TILE), 0)
    head = jnp.where(sub8 == 0, damp, jnp.where(sub8 == 1, entries, 0.0))
    last = jnp.where(sub8 >= 4, packed[:8, :], lead[24:, :])
    for r in range(NROW):
        tail = jnp.where(sub8 >= 4, packed[8 * r : 8 * r + 8, :], head)
        for c in range(NCOL):
            base = (r * NCOL + c) * SLOTS2
            pay_ref[base : base + 24, :] = lead[:24, :]
            pay_ref[base + 24 : base + 32, :] = last
            pay_ref[base + 32 : base + 40, :] = tail


def gather_rows(me, recv):
    return pl.pallas_call(
        gather_kernel,
        in_specs=[pl.BlockSpec(memory_space=SMEM), pl.BlockSpec(memory_space=VMEM)],
        out_shape=[
            jax.ShapeDtypeStruct((NDEV * SLOTS2, TILE), F32),
            jax.ShapeDtypeStruct((NDEV, TILE), jnp.int32),
        ],
        scratch_shapes=[VMEM((TILE, TILE), F32)],
        compiler_params=pltpu.CompilerParams(vmem_limit_bytes=16 * 1024 * 1024),
        name="gather_rows",
    )(me, recv)


def pieces(x):
    high = x.astype(BF16).astype(F32)
    rest = x - high
    mid = rest.astype(BF16).astype(F32)
    return high, mid, rest - mid


def factor128(rows):
    lane = lax.broadcasted_iota(jnp.int32, (8, TILE), 1)
    sub = lax.broadcasted_iota(jnp.int32, (8, TILE), 0)
    block = list(rows)
    inv = [jnp.where(lane == sub + 8 * v, 1.0, 0.0) for v in range(16)]
    upper, inverse = [], []

    def row(x, i):
        return jnp.broadcast_to(x[i : i + 1, :], (8, TILE))

    def col(x, i):
        return jnp.broadcast_to(x[:, i : i + 1], (8, TILE))

    for t in range(16):
        cols = [col(block[t], 8 * t + k) for k in range(8)]
        left, right = block[t], inv[t]
        up = jnp.zeros((8, TILE), F32)
        low = up
        for j in range(0, 8, 2):
            one, two = sub == j, sub == j + 1
            both = one | two
            x, y = cols[j], cols[j + 1]
            p, b, q = row(x, j), row(x, j + 1), row(y, j + 1)
            det = p * q - b * b
            over = 1.0 / det
            n1 = jnp.where(one, -q, jnp.where(two, b, x * q - y * b))
            n2 = jnp.where(one, b, jnp.where(two, -p, y * p - x * b))
            for k in range(j + 2, 8):
                change = (n1 * row(cols[k], j) + n2 * row(cols[k], j + 1)) * over
                cols[k] = jnp.where(both, 0.0, cols[k]) - change
            m1, m2 = n1 * over, n2 * over
            inv_p = 1.0 / p
            root_1, root_2, ratio = lax.rsqrt(p), lax.rsqrt(det * inv_p), b * inv_p
            l1, l2, r1, r2 = row(left, j), row(left, j + 1), row(right, j), row(right, j + 1)
            up = jnp.where(one, l1 * root_1, jnp.where(two, (l2 - ratio * l1) * root_2, up))
            low = jnp.where(one, r1 * root_1, jnp.where(two, (r2 - ratio * r1) * root_2, low))
            left = jnp.where(both, 0.0, left) - (m1 * l1 + m2 * l2)
            right = jnp.where(both, 0.0, right) - (m1 * r1 + m2 * r2)
        upper.append(jnp.where(lane >= sub + 8 * t, up, 0.0))
        inverse.append(low)
        if t < 15:
            parts = [col(block[t + 1], 8 * t + k) for k in range(8)]
            one = [parts[k] * row(left, k) for k in range(8)]
            two = [parts[k] * row(right, k) for k in range(8)]
            while len(one) > 1:
                one = [one[i] + one[i + 1] for i in range(0, len(one), 2)]
                two = [two[i] + two[i + 1] for i in range(0, len(two), 2)]
            block[t + 1] = block[t + 1] - one[0]
            inv[t + 1] = inv[t + 1] - two[0]
        if t < 14:
            h, m, low_part = pieces(block[t])
            mult = jnp.concatenate([h, h, m, h, low_part, m], axis=0).T.astype(BF16)
            h, m, low_part = pieces(jnp.concatenate([left, right], axis=1))
            base = jnp.concatenate([h, m, h, low_part, h, m], axis=0).astype(BF16)
            late = jnp.dot(mult, base, preferred_element_type=F32)
            for v in range(t + 2, 16):
                block[v] = block[v] - late[8 * v : 8 * v + 8, :TILE]
                inv[v] = inv[v] - late[8 * v : 8 * v + 8, TILE:]
    return upper, inverse


def at(i, n=TILE):
    return pl.ds(pl.multiple_of(i * n, n), n)


def three(x):
    high = x.astype(BF16)
    rest = x - high.astype(F32)
    mid = rest.astype(BF16)
    return high, mid, (rest - mid.astype(F32)).astype(BF16)


def stacks(x):
    h, m, low = three(x)
    return (
        jnp.concatenate([h, h], axis=1),
        jnp.concatenate([m, h], axis=1),
        jnp.concatenate([low, m], axis=1),
    )


def right_stacks(x):
    h, m, low = three(x)
    return jnp.concatenate([h, m], axis=1), jnp.concatenate([h, low], axis=1)


def six(pa, pb, pc, ra, rb):
    return nt(pa, ra) + (nt(pb, rb) + nt(pc, ra))


def unpack(pair, entries):
    lane = lax.broadcasted_iota(jnp.int32, (TILE, TILE), 1)
    sub = lax.broadcasted_iota(jnp.int32, (TILE, TILE), 0)
    low = jnp.where(lane < sub, pair, 0.0)
    high = jnp.where(lane > sub, pair, 0.0)
    one = low + low.T + jnp.where(lane == sub, pair, 0.0)
    return one, high + high.T + jnp.where(lane == sub, entries, 0.0)


def mark_rows(scal_ref, where_ref, tiles_ref):
    row = scal_ref[192]
    for u in range(LEAD):
        where_ref[u] = 0

    def mark(p, _):
        a = scal_ref[2 * p] - LEAD * row
        where_ref[a] = jnp.where(scal_ref[2 * p + 1] < LEAD, 1, where_ref[a])
        return 0

    @pl.when(row >= 1)
    def _():
        lax.fori_loop(0, 32, mark, 0)

    def place(u, count):
        used = where_ref[u] == 1
        where_ref[u] = jnp.where(used, count, -1)
        tiles_ref[count] = u
        return count + used.astype(jnp.int32)

    return lax.fori_loop(0, LEAD, place, jnp.int32(0))


def factor_kernel(
    scal_ref, recv_ref, cross_hbm, factor_hbm, yh_hbm, yl_hbm,
    lh_ref, ll_ref, wh_ref, wl_ref, body, inv_ref, pa, pb, pc, ra, rb,
    cross_ref, rows, xh, xl, yh, yl, none_ref, where_ref, tiles_ref, load_sem, factor_sem, y_sem,
):
    load = pltpu.make_async_copy(cross_hbm, cross_ref, load_sem.at[0])
    load.start()
    row = scal_ref[192]
    n_row = mark_rows(scal_ref, where_ref, tiles_ref)
    chunks = (n_row + 1) // 2
    fours = (n_row + 1) // 4
    none_ref[...] = jnp.zeros_like(none_ref)

    def clear(i, _):
        rows[at(i), :] = jnp.zeros((TILE, 1024), F32)
        return 0

    lax.fori_loop(0, n_row, clear, 0)
    lane = lax.broadcasted_iota(jnp.int32, (TILE, TILE), 1)
    sub = lax.broadcasted_iota(jnp.int32, (TILE, TILE), 0)

    def slot(i):
        return recv_ref[pl.ds(i, TILE, stride=SLOTS2), :]

    place = 0
    for k in range(LEAD):
        for i in range(k + 1, LEAD):
            body[TILE * i : TILE * (i + 1), TILE * k : TILE * (k + 1)] = slot(place)
            place += 1
    damp, entries = slot(DAMP_SLOT), slot(DIAG_SLOT)
    for u in range(4):
        one, two = unpack(slot(PAIR_SLOT + u), entries[:, 4 + u : 5 + u])
        for k, tile in ((u, one), (u + 4, two)):
            here = slice(TILE * k, TILE * (k + 1))
            body[here, here] = tile + jnp.where(lane == sub, damp[:, k : k + 1], 0.0)

    load.wait()

    def fill(p, _):
        a = scal_ref[2 * p] - LEAD * row
        b = scal_ref[2 * p + 1]

        @pl.when((b < LEAD) & (where_ref[a] >= 0))
        def _():
            rows[at(where_ref[a]), at(b)] += cross_ref[at(p), :]

        return 0

    lax.fori_loop(0, 32, fill, 0)
    for ref in (pa, pb, pc, ra, rb):
        ref[...] = jnp.zeros_like(ref)

    def step(k, _):
        groups = [
            body[pl.ds(pl.multiple_of(k * TILE + 8 * v, 8), 8), at(k)] for v in range(16)
        ]
        for j in range(2, 4):
            part = slice(256 * j, 1024)
            wide = slice(256 * j, 256 * (j + 1))
            later = j > k // 2
            wa = jnp.where(later, ra[wide, :], jnp.zeros_like(ra[wide, :]))
            wb = jnp.where(later, rb[wide, :], jnp.zeros_like(rb[wide, :]))
            body[part, wide] -= six(pa[part, :], pb[part, :], pc[part, :], wa, wb)
        upper, inverse = factor128(groups)
        inv = jnp.concatenate(inverse, axis=0)
        inv_ref[at(k), :] = inv
        wa, wb = right_stacks(inv)

        def panel(i, _):
            x = six(*stacks(body[at(i, 512), at(k)]), wa, wb)
            index = i * 512 + lax.broadcasted_iota(jnp.int32, (512, TILE), 0)
            x = jnp.where(index >= (k + 1) * TILE, x, 0.0)
            h, m, low = three(x)
            pa[at(i, 512), :] = jnp.concatenate([h, h], axis=1)
            pb[at(i, 512), :] = jnp.concatenate([m, h], axis=1)
            pc[at(i, 512), :] = jnp.concatenate([low, m], axis=1)
            ra[at(i, 512), :] = jnp.concatenate([h, m], axis=1)
            rb[at(i, 512), :] = jnp.concatenate([h, low], axis=1)
            lh_ref[at(i, 512), at(k)] = h
            ll_ref[at(i, 512), at(k)] = m
            return 0

        begin = (k >= 3).astype(jnp.int32)

        @pl.when(k >= 3)
        def _():
            zero = jnp.zeros((512, TILE), BF16)
            lh_ref[:512, at(k)] = zero
            ll_ref[:512, at(k)] = zero

        lax.fori_loop(begin, 2, panel, 0)

        def update(j, _):
            wa, wb = ra[at(j, 256), :], rb[at(j, 256), :]

            def rows_of(i, _):
                part = at(i, 512)
                body[part, at(j, 256)] -= six(pa[part, :], pb[part, :], pc[part, :], wa, wb)
                return 0

            lax.fori_loop((j >= 2).astype(jnp.int32), 2, rows_of, 0)
            return 0

        lax.fori_loop((k + 1) // 2, jnp.minimum(jnp.maximum((k + 3) // 2, 2), 4), update, 0)
        tile = jnp.concatenate(upper, axis=0).T
        body[at(k), at(k)] = tile
        lh_ref[at(k), at(k)], ll_ref[at(k), at(k)] = split(tile)
        return 0

    lax.fori_loop(0, LEAD, step, 0)
    for g in range(4):
        one = slice(256 * g, 256 * g + TILE)
        two = slice(256 * g + TILE, 256 * g + 256)
        w1, w2 = split(inv_ref[one, :]), split(inv_ref[two, :])
        inner = split(nn3(lh_ref[two, one], ll_ref[two, one], *w1))
        corner = -nn3(*w2, *inner)
        wh_ref[one, :TILE], wl_ref[one, :TILE] = w1
        zero = jnp.zeros((TILE, TILE), BF16)
        wh_ref[one, TILE:], wl_ref[one, TILE:] = zero, zero
        wh_ref[two, :TILE], wl_ref[two, :TILE] = split(corner)
        wh_ref[two, TILE:], wl_ref[two, TILE:] = w2
    for g in range(4):
        here = slice(256 * g, 256 * (g + 1))

        def forward(i, _, g=g, here=here, size=512):
            part = at(i, size)
            rest = rows[part, here]
            if g:
                rest = rest - nt3(
                    xh[part, : 256 * g],
                    xl[part, : 256 * g],
                    lh_ref[here, : 256 * g],
                    ll_ref[here, : 256 * g],
                )
            x = nt3(*split(rest), wh_ref[here, :], wl_ref[here, :])
            rows[part, here] = x
            xh[part, here], xl[part, here] = split(x)
            return 0

        lax.fori_loop(0, fours, forward, 0)
        lax.fori_loop(2 * fours, chunks, functools.partial(forward, size=256), 0)

    for s in range(LEAD):
        part = slice(TILE * s, TILE * (s + 1))

        @pl.when(row == 0)
        def _(part=part):
            rows[part, :] = lh_ref[part, :].astype(F32) + ll_ref[part, :].astype(F32)
            pltpu.make_async_copy(rows.at[part], factor_hbm.at[part], factor_sem.at[0]).start()

        @pl.when((row >= 1) & (where_ref[s] >= 0))
        def _(s=s, part=part):
            pltpu.make_async_copy(
                rows.at[at(where_ref[s])], factor_hbm.at[part], factor_sem.at[0]
            ).start()

        @pl.when((row >= 1) & (where_ref[s] < 0))
        def _(part=part):
            pltpu.make_async_copy(none_ref, factor_hbm.at[part], factor_sem.at[0]).start()

    for g in reversed(range(4)):
        here = slice(256 * g, 256 * (g + 1))

        def backward(i, _, g=g, here=here, size=512):
            part = at(i, size)
            rest = rows[part, here]
            if g < 3:
                past = slice(256 * (g + 1), 1024)
                rest = rest - nn3(
                    yh[part, past], yl[part, past], lh_ref[past, here], ll_ref[past, here]
                )
            yh[part, here], yl[part, here] = split(
                nn3(*split(rest), wh_ref[here, :], wl_ref[here, :])
            )
            if g == 0:
                pltpu.make_async_copy(yh.at[part], yh_hbm.at[part], y_sem.at[0]).start()
                pltpu.make_async_copy(yl.at[part], yl_hbm.at[part], y_sem.at[1]).start()
            return 0

        lax.fori_loop(0, fours, backward, 0)
        lax.fori_loop(2 * fours, chunks, functools.partial(backward, size=256), 0)

    def sent(i, _):
        part = at(i, 256)
        pltpu.make_async_copy(yh.at[part], yh_hbm.at[part], y_sem.at[0]).wait()
        pltpu.make_async_copy(yl.at[part], yl_hbm.at[part], y_sem.at[1]).wait()
        return 0

    lax.fori_loop(0, chunks, sent, 0)
    pltpu.make_async_copy(rows, factor_hbm, factor_sem.at[0]).wait()


def factorise(scal, recv, cross):
    return pl.pallas_call(
        factor_kernel,
        in_specs=[
            pl.BlockSpec(memory_space=SMEM),
            pl.BlockSpec(memory_space=VMEM),
            pl.BlockSpec(memory_space=pltpu.HBM),
        ],
        out_specs=[pl.BlockSpec(memory_space=pltpu.HBM)] * 3,
        out_shape=[
            jax.ShapeDtypeStruct((1024, 1024), F32),
            jax.ShapeDtypeStruct((1024, 1024), BF16),
            jax.ShapeDtypeStruct((1024, 1024), BF16),
        ],
        scratch_shapes=[VMEM((1024, 1024), BF16)] * 2
        + [VMEM((1024, 256), BF16)] * 2
        + [VMEM((1024, 1024), F32), VMEM((1024, TILE), F32)]
        + [VMEM((1024, 256), BF16)] * 5
        + [VMEM((32 * TILE, TILE), F32), VMEM((1024, 1024), F32)]
        + [VMEM((1024, 1024), BF16)] * 4
        + [
            VMEM((TILE, 1024), F32),
            SMEM((LEAD,), jnp.int32),
            SMEM((LEAD + 1,), jnp.int32),
            pltpu.SemaphoreType.DMA((1,)),
            pltpu.SemaphoreType.DMA((1,)),
            pltpu.SemaphoreType.DMA((2,)),
        ],
        compiler_params=pltpu.CompilerParams(vmem_limit_bytes=59 * 1024 * 1024),
        cost_estimate=pl.CostEstimate(
            flops=40_000_000_000, bytes_accessed=8_000_000, transcendentals=0
        ),
        name="factorise",
    )(scal, recv, cross)


def schur_kernel(
    scal_ref, damp_ref, yh_hbm, yl_hbm, col_hbm, cross_hbm, recv_hbm, out_hbm,
    yh, yl, col_ref, cross_ref, diag_ref, out_ref, cols, bh, bl,
    row_where, row_tiles, where_ref, col_tiles, used_ref, chunk_ref, load_sem, out_sem,
):
    row = scal_ref[192]
    column = scal_ref[193]
    loads = [
        pltpu.make_async_copy(source, target, load_sem.at[i])
        for i, (source, target) in enumerate(
            [
                (cross_hbm, cross_ref),
                (col_hbm, col_ref),
                (recv_hbm.at[:, DAMP_SLOT:SLOTS2], diag_ref),
                (yh_hbm, yh),
                (yl_hbm, yl),
            ]
        )
    ]
    for copy in loads:
        copy.start()
    for u in range(16):
        where_ref[u] = 0
    for u in range(64):
        used_ref[u] = 0

    def mark_col(p, _):
        tile = scal_ref[64 + 2 * p]
        a = tile - 16 * column
        b = scal_ref[65 + 2 * p]

        @pl.when((b < LEAD) & (tile >= LEAD) & (tile <= LEAD * row + 7))
        def _():
            where_ref[a] = 1
            used_ref[4 * a + b // 2] = 1

        return 0

    @pl.when(row >= 1)
    def _():
        lax.fori_loop(0, 64, mark_col, 0)

    def place_col(u, count):
        used = where_ref[u] == 1
        where_ref[u] = jnp.where(used, count, -1)
        col_tiles[count] = u
        return count + used.astype(jnp.int32)

    n_row = mark_rows(scal_ref, row_where, row_tiles)
    chunks = (n_row + 1) // 2
    n_col = lax.fori_loop(0, 16, place_col, jnp.int32(0))

    def blank(i, _):
        out_ref[at(i, 32), :] = jnp.zeros((32, 2048), F32)
        return 0

    lax.fori_loop(0, 32, blank, 0)

    def clear_cols(i, _):
        cols[at(i), :] = jnp.zeros((TILE, 1024), F32)
        return 0

    lax.fori_loop(0, n_col, clear_cols, 0)
    loads[0].wait()

    def fill_row(p, _):
        a = scal_ref[2 * p] - LEAD * row
        b = scal_ref[2 * p + 1]
        here = b - 16 * column

        @pl.when((b >= LEAD) & (here >= 0) & (here < 16))
        def _():
            out_ref[at(a), at(here)] += cross_ref[at(p), :]

        return 0

    def fill_col(p, _):
        a = scal_ref[64 + 2 * p] - 16 * column
        b = scal_ref[65 + 2 * p]

        @pl.when((b < LEAD) & (where_ref[a] >= 0))
        def _():
            cols[at(where_ref[a]), at(b)] += col_ref[at(p), :]

        return 0

    lax.fori_loop(0, 32, fill_row, 0)
    loads[1].wait()
    lax.fori_loop(0, 64, fill_col, 0)
    loads[2].wait()

    @pl.when((row >= 1) & (row // 2 == column))
    def _():
        lane = lax.broadcasted_iota(jnp.int32, (TILE, TILE), 1)
        sub = lax.broadcasted_iota(jnp.int32, (TILE, TILE), 0)
        entries = diag_ref[:, DIAG_SLOT - DAMP_SLOT, :]
        for u in range(4):
            mine = jnp.where(lane == LEAD * row + 4 + u, entries, 0.0)
            pair = diag_ref[:, OWN_SLOT - DAMP_SLOT + u, :]
            one, two = unpack(pair, jnp.sum(mine, axis=1, keepdims=True))
            for s, tile in ((u, one), (u + 4, two)):
                damp = damp_ref[TILE * s : TILE * (s + 1)].reshape(1, TILE)
                damp = jnp.where(lane == sub, jnp.broadcast_to(damp, (TILE, TILE)), 0.0)
                out_ref[TILE * s : TILE * (s + 1), at(LEAD * (row % 2) + s)] += tile + damp

    for copy in loads[3:]:
        copy.wait()

    def send(c):
        part = at(c)
        pltpu.make_async_copy(out_ref.at[:, part], out_hbm.at[:, part], out_sem.at[0]).start()

    def columns(j, sent):
        one_tile = col_tiles[2 * j]
        two_tile = col_tiles[jnp.minimum(2 * j + 1, n_col - 1)]

        def apply(i, prod):
            for p in range(2):
                for q in range(2):
                    it = 2 * i + p
                    a = row_tiles[it]
                    b = two_tile if q else one_tile
                    keep = (it < n_row) & (LEAD * row + a >= 16 * column + b)
                    if q:
                        keep = keep & (2 * j + 1 < n_col)

                    @pl.when(keep)
                    def _(a=a, b=b, p=p, q=q):
                        out_ref[at(a), at(b)] -= prod[
                            TILE * p : TILE * (p + 1), TILE * q : TILE * (q + 1)
                        ]

        def below(i):
            a = row_tiles[jnp.minimum(2 * i + 1, n_row - 1)]
            return LEAD * row + a >= 16 * column + one_tile

        def used(c):
            return used_ref[4 * one_tile + c] | used_ref[4 * two_tile + c]

        filled = jnp.int32(0)
        for c in range(4):

            @pl.when(used(c) == 1)
            def _(c=c, filled=filled):
                chunk_ref[filled] = c
                part = at(filled, 256)
                bh[:, part], bl[:, part] = split(cols[at(j, 256), 256 * c : 256 * (c + 1)])

            filled = filled + used(c)
        for depth in range(1, 5):

            @pl.when(filled == depth)
            def _(depth=depth):
                wide = slice(0, 256 * depth)

                def blocks(i, _):
                    @pl.when(below(i))
                    def _():
                        picks = [at(chunk_ref[f], 256) for f in range(depth)]
                        high = jnp.concatenate([yh[at(i, 256), p] for p in picks], axis=1)
                        low = jnp.concatenate([yl[at(i, 256), p] for p in picks], axis=1)
                        apply(i, nt3(high, low, bh[:, wide], bl[:, wide]))

                    return 0

                lax.fori_loop(0, chunks, blocks, 0)

        done = two_tile + 1

        def one(c, _):
            send(c)
            return 0

        lax.fori_loop(sent, done, one, 0)
        return done

    sent = lax.fori_loop(0, (n_col + 1) // 2, columns, jnp.int32(0))

    def last(c, _):
        send(c)
        return 0

    lax.fori_loop(sent, 16, last, 0)
    pltpu.make_async_copy(out_ref, out_hbm, out_sem.at[0]).wait()


def schur(scal, yh, yl, col_cross, cross, recv, damp):
    return pl.pallas_call(
        schur_kernel,
        in_specs=[pl.BlockSpec(memory_space=SMEM), pl.BlockSpec(memory_space=VMEM)]
        + [pl.BlockSpec(memory_space=pltpu.HBM)] * 5,
        out_specs=pl.BlockSpec(memory_space=pltpu.HBM),
        out_shape=jax.ShapeDtypeStruct((1024, 2048), F32),
        scratch_shapes=[
            VMEM((1024, 1024), BF16),
            VMEM((1024, 1024), BF16),
            VMEM((64 * TILE, TILE), F32),
            VMEM((32 * TILE, TILE), F32),
            VMEM((NDEV, LEAD, TILE), F32),
            VMEM((1024, 2048), F32),
            VMEM((2048, 1024), F32),
            VMEM((256, 1024), BF16),
            VMEM((256, 1024), BF16),
            SMEM((LEAD,), jnp.int32),
            SMEM((LEAD + 1,), jnp.int32),
            SMEM((16,), jnp.int32),
            SMEM((17,), jnp.int32),
            SMEM((64,), jnp.int32),
            SMEM((4,), jnp.int32),
            pltpu.SemaphoreType.DMA((5,)),
            pltpu.SemaphoreType.DMA((1,)),
        ],
        compiler_params=pltpu.CompilerParams(vmem_limit_bytes=60 * 1024 * 1024),
        cost_estimate=pl.CostEstimate(
            flops=20_000_000_000, bytes_accessed=30_000_000, transcendentals=0
        ),
        name="schur",
    )(scal, damp, yh, yl, col_cross, cross, recv)


def local(pair_list, jacobian, damping):
    row = lax.axis_index("row")
    column = lax.axis_index("col")
    payload, cross = grams(jacobian, pair_list.T, damping)
    recv = lax.all_to_all(payload.reshape(NDEV, SLOTS1, TILE), BOTH, 0, 0, tiled=True)
    cross = cross.reshape(4 * TILE, TILE)
    moves = [
        (r * NCOL + c, (NCOL * (r % 2) + c) * NCOL + r // 2) for r in range(NROW) for c in range(NCOL)
    ]
    moved = lax.ppermute(cross, BOTH, moves)
    row_cross = lax.all_gather(cross, "col", axis=0, tiled=True)
    me = (row * NCOL + column).astype(jnp.int32).reshape(1)
    payload, index = gather_rows(me, recv.reshape(NDEV * SLOTS1, TILE))
    recv = lax.all_to_all(payload.reshape(NDEV, SLOTS2, TILE), BOTH, 0, 0, tiled=True)
    recv, moved = lax.optimization_barrier((recv, moved))
    col_cross = lax.all_gather(moved, "row", axis=0, tiled=True)

    index = index[:, :8].reshape(NDEV * 8)
    scal = jnp.concatenate(
        [
            lax.dynamic_slice(index, (row * 64,), (64,)),
            lax.dynamic_slice(index, (column * 128,), (128,)),
            jnp.stack([row, column]).astype(jnp.int32),
        ]
    )
    factor, yh, yl = factorise(scal, recv.reshape(NDEV * SLOTS2, TILE), row_cross)
    return factor, schur(scal, yh, yl, col_cross, row_cross, recv, damping)


def solution(mesh):
    placed = (P(("row", "col"), None), P(("row", "col"), None, None), P("row"))
    return jax.shard_map(
        local,
        mesh=mesh,
        in_specs=placed,
        out_specs=(P("row", None), P("row", "col")),
        check_vma=False,
    )
```
